32 devices in a mesh: dp: 4 (over y, x), row: 4 (over z), col: 2 (over core).
Axes of the slice: x: 2, y: 2, z: 4, core: 2. Of those that a mesh axis runs over, the one named last changes fastest.
Arguments:
- inputs: bfloat16 [16384, 768], P(('dp', 'row'), 'col'), may hold values from -6 to 6
- out_grad: bfloat16 [16384, 768], P(('dp', 'row'), 'col'), may hold values from -6 to 6
- deal: int32 [16, 1024], P(('dp', 'row')), may hold values from 0 to 1023, each once within a row
- seq_lengths: int32 [8, 4], P(('dp', 'col')), may hold values from 1 to 1024, 2048 in all within a row
- key_trim: int32 [8, 4], P(('dp', 'col')), may hold values from 0 to 255
- query_weight: bfloat16 [768, 768], P('col', 'row'), may hold values from -0.21875 to 0.21875
- query_bias: bfloat16 [768], P('row'), may hold values from -3 to 3
- key_weight: bfloat16 [768, 768], P('col', 'row'), may hold values from -0.21875 to 0.21875
- value_weight: bfloat16 [768, 768], P('col', 'row'), may hold values from -0.21875 to 0.21875
- value_bias: bfloat16 [768], P('row'), may hold values from -3 to 3
- out_weight: bfloat16 [768, 768], P('row', 'col'), may hold values from -3.5 to 3.5
- out_bias: bfloat16 [768], P('col'), may hold values from -3 to 3
- first_gain: bfloat16 [768], P('col'), may hold values from 0.5 to 1.5
- first_shift: bfloat16 [768], P('col'), may hold values from -3 to 3
- up_weight: bfloat16 [768, 3072], P('col', 'row'), may hold values from -0.21875 to 0.21875
- up_bias: bfloat16 [3072], P('row'), may hold values from -3 to 3
- down_weight: bfloat16 [3072, 768], P('row', 'col'), may hold values from -0.109375 to 0.109375
- down_bias: bfloat16 [768], P('col'), may hold values from -3 to 3
- second_gain: bfloat16 [768], P('col'), may hold values from 0.5 to 1.5
- second_shift: bfloat16 [768], P('col'), may hold values from -3 to 3
Outputs:
- output: bfloat16 [16384, 768], P(('dp', 'row'), 'col')
- input_grad: bfloat16 [16384, 768], P(('dp', 'row'), 'col')
- query_weight_grad: float32 [768, 768], P('col', 'row')
- query_bias_grad: float32 [768], P('row')
- key_weight_grad: float32 [768, 768], P('col', 'row')
- value_weight_grad: float32 [768, 768], P('col', 'row')
- value_bias_grad: float32 [768], P('row')
- out_weight_grad: float32 [768, 768], P('row', 'col')
- out_bias_grad: float32 [768], P('col')
- first_gain_grad: float32 [768], P('col')
- first_shift_grad: float32 [768], P('col')
- up_weight_grad: float32 [768, 3072], P('col', 'row')
- up_bias_grad: float32 [3072], P('row')
- down_weight_grad: float32 [3072, 768], P('row', 'col')
- down_bias_grad: float32 [768], P('col')
- second_gain_grad: float32 [768], P('col')
- second_shift_grad: float32 [768], P('col')
The draws below stay inside these ranges and needn't reach their ends.
Inputs may be any that keep to these rules, and one draw needn't show every extreme that they name: Each row of deal lists every number below 1024 once. `seq_lengths`: each row sums to 2048, and its largest entry is exactly 1024.
All inputs are finite; a program needn't handle non-finite values.
Results may differ from the reference program's by a relative error of at most 0.022.
Values may be sent and summed in bfloat16 or wider, within the bound.
A program may use at most 192 MiB of HBM per device.

```python
import math
import jax
import jax.numpy as jnp
import numpy as np
from jax import lax

HEADS = 12
HEAD_DIM = 64
FF = 3072
D = 768
SLOT = 2048
SEQS = 4
PACKS = 1
ROW_TOK = 1024
GROUP = 4096
PIECE = 256
TOKENS = 16384
N_DP = 4
N_ROW = 4
N_COL = 2


def plant(values, own_key, smallest, high):
    spot = [jax.random.randint(jax.random.fold_in(own_key, axis), (), 0, length) for axis, length in enumerate(values.shape)]
    longest = values.shape.index(max(values.shape))
    neighbour = spot[:longest] + [(spot[longest] + 1) % values.shape[longest]] + spot[longest + 1:]
    return values.at[tuple(spot)].set(smallest).at[tuple(neighbour)].set(high)


def steps_of(stream_key, shape, shards, smallest, largest):
    factor_of = 1.0
    for dim, shards_of in shards:
        steps = jax.random.uniform(jax.random.fold_in(jax.random.fold_in(stream_key, 6), dim), (shards_of,), jnp.float32, smallest / len(shards), largest / len(shards))
        factor_of = factor_of * jnp.repeat(jnp.exp(steps), shape[dim] // shards_of).reshape((-1,) + (1,) * (len(shape) - 1 - dim))
    return factor_of


def split_up(amount, total, reach, skew):
    loads = [(1 << 20) // math.isqrt(rank ** skew) + 1 for rank in range(2, amount + 1)]
    rest, counts = total - reach - (amount - 1), [1] * (amount - 1)
    while rest > 0:
        candidates = [i for i in range(amount - 1) if counts[i] < reach]
        mass, remaining = sum([loads[i] for i in candidates]), rest
        for i in candidates:
            extra = min(reach - counts[i], max(1, remaining * loads[i] // mass), rest)
            counts[i] = counts[i] + extra
            rest = rest - extra
    return np.array([reach] + counts)


def ragged(rng, number_of, total, most, skew):
    if number_of == 2:
        one = jax.random.randint(rng, (), max(1, total - most), min(most, total - 1) + 1)
        return jnp.stack([one, total - one])
    tallies = jnp.asarray(split_up(number_of, total, most, skew), jnp.int32)
    couples = (number_of - 1) // 2
    source_of, receiver = tallies[1:1 + 2 * couples:2], tallies[2:2 + 2 * couples:2]
    margin = jnp.minimum(source_of - 1, most - receiver)
    passed = jax.random.randint(jax.random.fold_in(rng, 1), (couples,), 0, 1 << 20) % (margin + 1)
    tallies = tallies.at[1:1 + 2 * couples:2].set(source_of - passed).at[2:2 + 2 * couples:2].set(receiver + passed)
    return tallies[jax.random.permutation(jax.random.fold_in(rng, 2), number_of)]


def scatter_about(rng, extent, spread, most, cuts=(), held_as=jnp.bfloat16):
    values = spread * jax.random.normal(rng, extent, jnp.float32)
    if cuts:
        values = values * steps_of(rng, extent, cuts, -0.22, 0.18)
    return jnp.clip(values, -most, most).astype(held_as)


def setup_inputs(seed: int = 0) -> dict:
    key_of = jax.random.split(jax.random.key(seed), 21)
    return {
        "inputs": scatter_about(key_of[0], (TOKENS, D), 1.0, 6.0, ((0, 16), (1, 2))),
        "out_grad": scatter_about(key_of[1], (TOKENS, D), 1.0, 6.0, ((0, 16), (1, 2))),
        "deal": jax.vmap(lambda own: jax.random.permutation(own, ROW_TOK))(jax.random.split(key_of[2], (N_DP * N_ROW))).reshape((N_DP * N_ROW, ROW_TOK)).astype(jnp.int32),
        "seq_lengths": jax.vmap(lambda own: ragged(own, SEQS, SLOT, SLOT // 2, 2))(jax.random.split(key_of[3], (N_DP * N_COL * PACKS))).reshape((N_DP * N_COL * PACKS, SEQS)).astype(jnp.int32),
        "key_trim": plant(jax.random.randint(key_of[4], (N_DP * N_COL * PACKS, SEQS), 0, SLOT // 8), jax.random.fold_in(key_of[4], 1), 0, (SLOT // 8) - 1).astype(jnp.int32),
        "query_weight": scatter_about(key_of[5], (D, D), D ** -0.5, 0.21875, ((0, 2), (1, 4))),
        "query_bias": scatter_about(key_of[6], (D,), 0.5, 3.0, ((0, 4),)),
        "key_weight": scatter_about(key_of[7], (D, D), D ** -0.5, 0.21875, ((0, 2), (1, 4))),
        "value_weight": scatter_about(key_of[8], (D, D), D ** -0.5, 0.21875, ((0, 2), (1, 4))),
        "value_bias": scatter_about(key_of[9], (D,), 0.5, 3.0, ((0, 4),)),
        "out_weight": scatter_about(key_of[10], (D, D), (max(2, D // 256)) ** -0.5, 3.5, ((0, 4), (1, 2))),
        "out_bias": scatter_about(key_of[11], (D,), 0.5, 3.0, ((0, 2),)),
        "first_gain": jnp.clip(1.0 + 0.1 * jax.random.normal(key_of[12], (D,), jnp.float32), 0.5, 1.5).astype(jnp.bfloat16),
        "first_shift": scatter_about(key_of[13], (D,), 0.5, 3.0, ((0, 2),)),
        "up_weight": scatter_about(key_of[14], (D, FF), D ** -0.5, 0.21875, ((0, 2), (1, 4))),
        "up_bias": scatter_about(key_of[15], (FF,), 0.5, 3.0, ((0, 4),)),
        "down_weight": scatter_about(key_of[16], (FF, D), FF ** -0.5, 0.109375, ((0, 4), (1, 2))),
        "down_bias": scatter_about(key_of[17], (D,), 0.5, 3.0, ((0, 2),)),
        "second_gain": jnp.clip(1.0 + 0.1 * jax.random.normal(key_of[18], (D,), jnp.float32), 0.5, 1.5).astype(jnp.bfloat16),
        "second_shift": scatter_about(key_of[19], (D,), 0.5, 3.0, ((0, 2),)),
    }


norm_eps = 1e-05
far_below = -1e+30

@jax.custom_vjp
def low(v):
    return lax.optimization_barrier(v.astype(jnp.bfloat16)).astype(jnp.float32)

@jax.custom_vjp
def low_back(v):
    return v

def low_keep(v):
    return (low(v), None)

def low_pass(kept, grad):
    return (grad,)

def back_keep(v):
    return (v, None)

def back_low(kept, grad):
    return (low(grad),)
low.defvjp(low_keep, low_pass)
low_back.defvjp(back_keep, back_low)

def product(left, right):
    return jnp.dot(left, right, precision=lax.Precision.HIGHEST, preferred_element_type=jnp.float32)

def layer_norm(hidden, gain_vec, shift_vec):
    row_mean = lax.optimization_barrier(jnp.mean(hidden, axis=-1, keepdims=True))
    row_var = lax.optimization_barrier(jnp.mean(hidden * hidden, axis=-1, keepdims=True)) - row_mean * row_mean
    return (hidden - row_mean) * lax.rsqrt(row_var + norm_eps) * gain_vec + shift_vec

def pack_info(seq_len, trim_len):
    seq_ends = jnp.cumsum(seq_len).astype(jnp.int32)
    seq_starts = (seq_ends - seq_len).astype(jnp.int32)
    position = jnp.arange(SLOT, dtype=jnp.int32)
    segment = lax.optimization_barrier(jnp.sum((position[:, None] >= seq_ends[None, :]).astype(jnp.int32), axis=1)).astype(jnp.int32)
    onehot = segment[:, None] == jnp.arange(seq_len.shape[0], dtype=jnp.int32)[None, :]
    begin = lax.optimization_barrier(jnp.sum(jnp.where(onehot, seq_starts[None, :], 0), axis=1)).astype(jnp.int32)
    valid_len = jnp.maximum(seq_len - trim_len, 1).astype(jnp.int32)
    limit = lax.optimization_barrier(jnp.sum(jnp.where(onehot, valid_len[None, :], 0), axis=1)).astype(jnp.int32)
    return (segment, position - begin < limit)

def pack_attend(query, key, value, segment, live_keys):
    scores = jnp.einsum('qhd,khd->hqk', query, key, precision=lax.Precision.HIGHEST) * HEAD_DIM ** (-0.5)
    scores = low_back(scores)
    allowed = (segment[:, None] == segment[None, :]) & live_keys[None, :]
    scores = jnp.where(allowed[None, :, :], scores, far_below)
    probs = jax.nn.softmax(scores, axis=-1)
    return jnp.einsum('hqk,khd->qhd', low(probs), value, precision=lax.Precision.HIGHEST)

def group_layer(tokens, params, segment, live_keys):
    query_weight, query_bias, key_weight, value_weight, value_bias, out_weight, out_bias, first_gain, first_shift, up_weight, up_bias, down_weight, down_bias, second_gain, second_shift = params
    tokens = low_back(tokens)
    query = low_back(low(product(tokens, query_weight) + query_bias))
    key = low_back(low(product(tokens, key_weight)))
    value = low_back(low(product(tokens, value_weight) + value_bias))
    shaped = (N_COL * PACKS, SLOT, HEADS, HEAD_DIM)
    checked = jax.checkpoint(pack_attend)

    def one_pack(operands):
        return checked(*operands)
    attended = lax.map(one_pack, (query.reshape(shaped), key.reshape(shaped), value.reshape(shaped), segment, live_keys))
    attended = low_back(low(attended.reshape(GROUP, D)))
    branch = low_back(product(attended, out_weight) + out_bias)
    normed = low(layer_norm(tokens + branch, first_gain, first_shift))
    pre_act = low_back(product(normed, up_weight) + up_bias)
    hidden = low(jax.nn.gelu(pre_act, approximate=False))
    ffn_out = low_back(product(hidden, down_weight) + down_bias)
    return layer_norm(normed + ffn_out, second_gain, second_shift)

def arrange(rows, deal):
    blocks = rows.reshape(N_DP * N_ROW, ROW_TOK, D)
    picked = jnp.take_along_axis(blocks, deal[:, :, None], axis=1)
    picked = picked.reshape(N_DP, N_ROW, N_DP, PIECE, D)
    return picked.transpose(2, 1, 0, 3, 4).reshape(N_DP, GROUP, D)

def restore(groups, deal):
    picked = groups.reshape(N_DP, N_ROW, N_DP, PIECE, D).transpose(2, 1, 0, 3, 4).reshape(N_DP * N_ROW, ROW_TOK, D)

    def place(blank, where_to, values):
        return blank.at[where_to].set(values)
    return jax.vmap(place)(jnp.zeros_like(picked), deal, picked).reshape(TOKENS, D)

def reference(inputs, out_grad, deal, seq_lengths, key_trim, query_weight, query_bias, key_weight, value_weight, value_bias, out_weight, out_bias, first_gain, first_shift, up_weight, up_bias, down_weight, down_bias, second_gain, second_shift):
    params = tuple((p.astype(jnp.float32) for p in (query_weight, query_bias, key_weight, value_weight, value_bias, out_weight, out_bias, first_gain, first_shift, up_weight, up_bias, down_weight, down_bias, second_gain, second_shift)))
    arranged = arrange(inputs.astype(jnp.float32), deal)
    cotangent = arrange(out_grad.astype(jnp.float32), deal)
    segments, live_all = jax.vmap(pack_info)(seq_lengths, key_trim)
    segments = segments.reshape(N_DP, N_COL * PACKS, SLOT)
    live_all = live_all.reshape(N_DP, N_COL * PACKS, SLOT)

    def one_group(accum, operands):
        tokens, grad_out, segment, live_keys = operands

        def forward(tok_in, par_in):
            return group_layer(tok_in, par_in, segment, live_keys)
        result, pullback = jax.vjp(forward, tokens, params)
        tok_grad, par_grad = pullback(grad_out)
        accum = jax.tree.map(jnp.add, accum, par_grad)
        return (accum, (result, tok_grad))
    zero_grads = jax.tree.map(jnp.zeros_like, params)
    grads, (results, tok_grads) = lax.scan(one_group, zero_grads, (arranged, cotangent, segments, live_all))
    output = restore(results, deal).astype(jnp.bfloat16)
    input_grad = restore(tok_grads, deal).astype(jnp.bfloat16)
    return (output, input_grad, grads[0], grads[1], grads[2], grads[3], grads[4], grads[5], grads[6], grads[7], grads[8], grads[9], grads[10], grads[11], grads[12], grads[13], grads[14])
```

```python
import functools
import math

import jax
import jax.numpy as jnp
from jax import lax
from jax.experimental import pallas as pl
from jax.experimental.pallas import tpu as pltpu
from jax.sharding import PartitionSpec as P

MESH = pl.DeviceIdType.MESH
f32 = jnp.float32
bf16 = jnp.bfloat16

HEAD = 64
EPS = 1e-05
FAR = -1e30
INV_ROOT_TWO = 0.7071067811865476
INV_ROOT_TAU = 0.3989422804014327
VMEM_LIMIT = 62 * 1024 * 1024

VM = pl.BlockSpec(memory_space=pltpu.VMEM)
SM = pl.BlockSpec(memory_space=pltpu.SMEM)
ANY = pl.BlockSpec(memory_space=pl.ANY)
DMA = pltpu.SemaphoreType.DMA


def nn(a, b):
    return lax.dot_general(a, b, (((1,), (0,)), ((), ())), preferred_element_type=f32)


def nt(a, b):
    return lax.dot_general(a, b, (((1,), (1,)), ((), ())), preferred_element_type=f32)


def tn(a, b):
    return lax.dot_general(a, b, (((0,), (0,)), ((), ())), preferred_element_type=f32)


def sds(shape, dtype):
    return jax.ShapeDtypeStruct(shape, dtype)


def me():
    return lax.axis_index("dp"), lax.axis_index("row"), lax.axis_index("col")


def flip(v):
    return v + 1 - 2 * lax.rem(v, 2)


def remote(src, dst, ssem, rsem, dev):
    return pltpu.make_async_remote_copy(
        src_ref=src, dst_ref=dst, send_sem=ssem, recv_sem=rsem, device_id=dev, device_id_type=MESH
    )


def greet(devs):
    barrier = pltpu.get_barrier_semaphore()
    for dev in devs:
        pl.semaphore_signal(barrier, inc=1, device_id=dev, device_id_type=MESH)
    pl.semaphore_wait(barrier, len(devs))


def deal_kernel(
    n_dp, x_ref, dy_ref, deal_ref, w_ref, seq_ref,
    xf_ref, dya_ref, dyb_ref, qkv_ref, qkvt_ref, wq_ref, seqo_ref,
    xs, dys, dyin, seqrx, sx, rx, sc, rc, sz, rz, sc2, rc2, sd, rd, sw, rw, sm, rm,
):
    d, r, c = me()
    half = lax.rem(r, 2)
    tokens = x_ref.shape[0]
    piece = tokens // n_dp
    core = (d, r, 1 - c)
    zdev = (d, flip(r), c)
    far_row = lax.rem(r + 2, 4)
    ring = [(lax.rem(d + k, n_dp), r, c) for k in range(1, n_dp)]
    greet(ring + [core, zdev, (d, far_row, 0), (d, far_row, 1)])

    w_far = remote(w_ref, wq_ref.at[c], sw.at[0], rw.at[c], (d, far_row, 1))
    w_far.start()
    w_near = remote(w_ref, wq_ref.at[1], sw.at[1], rw.at[1], (d, r, 0))

    @pl.when(c == 0)
    def _():
        wq_ref[0] = w_ref[...]

    @pl.when(c == 1)
    def _():
        w_near.start()

    seq_cp = remote(seq_ref, seqrx, sm.at[0], rm.at[0], core)
    seq_cp.start()

    def rows(s):
        return pl.ds(pl.multiple_of(s * piece, piece), piece)

    lane = lax.broadcasted_iota(jnp.int32, (piece, tokens), 1)
    sends = []
    dsends = []
    for k in list(range(1, n_dp)) + [0]:
        dest = lax.rem(d + k, n_dp)
        pick = (deal_ref[rows(dest), :] == lane).astype(bf16)
        px = nn(pick, x_ref[...]).astype(bf16)
        pd = nn(pick, dy_ref[...]).astype(bf16)
        if k:
            xs[k] = px
            cp = remote(xs.at[k], xf_ref.at[half, c, rows(d), :], sx.at[k], rx.at[k], (dest, r, c))
            cp.start()
            sends.append(cp)
            dys[k] = pd
            dsends.append(remote(dys.at[k], dyin.at[rows(d), :], sd.at[k], rd.at[k], (dest, r, c)))
        else:
            xf_ref[half, c, rows(d), :] = px
            dyin[rows(d), :] = pd

    core_cp, z_cp, core2_cp = [], [], []
    for k in range(n_dp):
        s = lax.rem(d - k + n_dp, n_dp)
        ref = xf_ref.at[half, c, rows(s), :]
        if k:
            sends[k - 1].wait_recv()
        a = remote(ref, ref, sz.at[k], rz.at[k], zdev)
        a.start()
        b = remote(ref, ref, sc.at[k], rc.at[k], core)
        b.start()
        z_cp.append(a)
        core_cp.append(b)
        if k == 0:
            for cp in dsends:
                cp.start()
    for k in range(n_dp):
        s = lax.rem(d - k + n_dp, n_dp)
        z_cp[k].wait_recv()
        ref = xf_ref.at[1 - half, c, rows(s), :]
        b = remote(ref, ref, sc2.at[k], rc2.at[k], core)
        b.start()
        core2_cp.append(b)
    for cp in dsends:
        cp.wait_recv()
    own = tokens // 2
    theirs = pl.ds(pl.multiple_of((1 - c) * own, own), own)
    mine = pl.ds(pl.multiple_of(c * own, own), own)
    dy_cp = remote(dyin.at[theirs, :], dyb_ref, sm.at[1], rm.at[1], core)
    dy_cp.start()
    dya_ref[...] = dyin[mine, :]
    seq_cp.wait()
    is_mine = lax.div(r, 2) == c
    seqo_ref[...] = jnp.where(is_mine, seq_ref[...], seqrx[...])

    @pl.when(c == 0)
    def _():
        w_near.wait_recv()

    @pl.when(c == 1)
    def _():
        w_near.wait_send()
        remote(w_ref, wq_ref.at[0], sw.at[0], rw.at[0], (d, far_row, 1)).wait_recv()
        remote(w_ref, wq_ref.at[1], sw.at[0], rw.at[1], (d, far_row, 1)).wait_recv()

    w_far.wait_send()
    for k in range(n_dp):
        core_cp[k].wait_recv()
        core2_cp[k].wait_recv()
    width = w_ref.shape[0] - 16
    bias = wq_ref[0, width : width + 1, :].astype(f32)

    def project(i, carry):
        h = lax.div(i, 2)
        base = pl.ds(pl.multiple_of(lax.rem(i, 2) * 512, 512), 512)
        y = nn(xf_ref[h, 0, base, :], wq_ref[0, :width, :])
        y = y + nn(xf_ref[h, 1, base, :], wq_ref[1, :width, :]) + bias
        y = y.astype(bf16)
        out = pl.ds(pl.multiple_of(i * 512, 512), 512)
        qkv_ref[out, :] = y
        qkvt_ref[:, out] = y.T
        return carry

    lax.fori_loop(0, 4, project, 0)
    for cp in sends + dsends + core_cp + z_cp + core2_cp:
        cp.wait_send()
    dy_cp.wait()


def deal_call(n_dp, x, dy, deal_col, w, seq):
    tokens, wide = x.shape
    piece = tokens // n_dp
    cols = w.shape[1]
    return pl.pallas_call(
        functools.partial(deal_kernel, n_dp),
        out_shape=(
            sds((2, 2, tokens, wide), bf16),
            sds((tokens // 2, wide), bf16),
            sds((tokens // 2, wide), bf16),
            sds((2 * tokens, cols), bf16),
            sds((cols, 2 * tokens), bf16),
            sds((2,) + w.shape, bf16),
            sds(seq.shape, jnp.int32),
        ),
        in_specs=[VM] * 5,
        out_specs=(VM,) * 7,
        scratch_shapes=[
            pltpu.VMEM((n_dp, piece, wide), bf16),
            pltpu.VMEM((n_dp, piece, wide), bf16),
            pltpu.VMEM((tokens, wide), bf16),
            pltpu.VMEM(seq.shape, jnp.int32),
        ]
        + [DMA((n_dp,))] * 10
        + [DMA((2,))] * 4,
        compiler_params=pltpu.CompilerParams(
            collective_id=1, has_side_effects=True, vmem_limit_bytes=VMEM_LIMIT
        ),
        name="deal",
    )(x, dy, deal_col, w, seq)


def seq_bounds(seq_ref, n_seq):
    ends, total = [], 0
    for j in range(n_seq):
        total = total + seq_ref[0, j]
        ends.append(total)
    starts = [ends[j] - seq_ref[0, j] for j in range(n_seq)]
    lives = [starts[j] + jnp.maximum(seq_ref[0, j] - seq_ref[1, j], 1) for j in range(n_seq)]
    return starts, ends, lives


def block_range(first, last, starts, ends, block):
    lo, hi = 0, ends[-1]
    for j in range(len(ends)):
        lo = jnp.where((first >= starts[j]) & (first < ends[j]), starts[j], lo)
        hi = jnp.where((last >= starts[j]) & (last < ends[j]), ends[j], hi)
    return lax.div(lo, block), lax.div(hi + block - 1, block)


def key_columns(starts, ends, lives, length, extra):
    pos = lax.broadcasted_iota(jnp.int32, (length, HEAD), 0)
    lane = lax.broadcasted_iota(jnp.int32, (length, HEAD), 1)
    n_seq = len(ends)
    cols = jnp.where(lane < n_seq, FAR, 0.0)
    cols = jnp.where((lane >= n_seq) & (lane < n_seq + extra), -1.0, cols)
    for j in range(n_seq):
        live = (pos >= starts[j]) & (pos < lives[j]) & (lane == j)
        cols = jnp.where(live, 0.0, cols)
    return cols.astype(bf16)


def query_rows(starts, ends, length):
    pos = lax.broadcasted_iota(jnp.int32, (16, length), 1)
    row = lax.broadcasted_iota(jnp.int32, (16, length), 0)
    out = jnp.zeros((16, length), f32)
    for j in range(len(ends)):
        out = jnp.where((row == j) & (pos >= starts[j]) & (pos < ends[j]), 1.0, out)
    return out


def split_three(v):
    hi = v.astype(bf16).astype(f32)
    mid = (v - hi).astype(bf16).astype(f32)
    low = (v - hi - mid).astype(bf16).astype(f32)
    return hi, mid, low


def put_rows(base, values, first):
    row = lax.broadcasted_iota(jnp.int32, base.shape, 0)
    for i, v in enumerate(values):
        base = jnp.where(row == first + i, v, base)
    return base


def attend_kernel(n_seq, block, seq_ref, qkv_ref, qkvt_ref, ot_ref, lse_ref, kaug, qaug, vaug, acc, mx):
    length = qkv_ref.shape[0]
    heads = qkv_ref.shape[1] // (3 * HEAD)
    width = heads * HEAD
    starts, ends, lives = seq_bounds(seq_ref, n_seq)
    kcols = key_columns(starts, ends, lives, length, 0)
    qrows = query_rows(starts, ends, length).astype(bf16)
    ones = (lax.broadcasted_iota(jnp.int32, (16, length), 0) == 0).astype(f32).astype(bf16)
    for h in range(heads):
        kaug[h, :, :HEAD] = qkv_ref[:, width + h * HEAD : width + (h + 1) * HEAD]
        kaug[h, :, HEAD:] = kcols
        qaug[h, :HEAD, :] = qkvt_ref[h * HEAD : (h + 1) * HEAD, :] * 0.125
        qaug[h, HEAD : HEAD + 16, :] = qrows
        qaug[h, HEAD + 16 :, :] = jnp.zeros((HEAD - 16, length), bf16)
        vaug[h, :HEAD, :] = qkvt_ref[2 * width + h * HEAD : 2 * width + (h + 1) * HEAD, :]
        vaug[h, HEAD:, :] = ones
    lse_ref[...] = jnp.zeros_like(lse_ref)

    def q_step(qb, carry):
        qs = pl.ds(pl.multiple_of(qb * block, block), block)
        lo, hi = block_range(qb * block, qb * block + block - 1, starts, ends, block)
        for h in range(heads):
            acc[h] = jnp.zeros((HEAD + 16, block), f32)
            mx[h] = jnp.full((8, block), 2 * FAR, f32)

        def k_step(kb, inner):
            ks = pl.ds(pl.multiple_of(kb * block, block), block)
            for h in range(heads):
                s = nn(kaug[h, ks, :], qaug[h, :, qs])
                old = mx[h, 0:1, :]
                new = jnp.maximum(old, jnp.max(s, axis=0, keepdims=True))
                p = jnp.exp(s - new).astype(bf16)
                acc[h] = acc[h] * jnp.exp(old - new) + nn(vaug[h, :, ks], p)
                mx[h] = jnp.broadcast_to(new, (8, block))
            return inner

        lax.fori_loop(lo, hi, k_step, 0)
        for h in range(heads):
            total = acc[h, HEAD : HEAD + 1, :]
            ot_ref[h * HEAD : (h + 1) * HEAD, qs] = (acc[h, :HEAD, :] / total).astype(bf16)
            lse_ref[h : h + 1, qs] = mx[h, 0:1, :] + jnp.log(total)
        return carry

    lax.fori_loop(0, length // block, q_step, 0)


def attend_call(n_seq, seq, qkv, qkvt):
    length, cols = qkv.shape
    heads = cols // (3 * HEAD)
    block = 256
    return pl.pallas_call(
        functools.partial(attend_kernel, n_seq, block),
        out_shape=(sds((heads * HEAD, length), bf16), sds((8, length), f32)),
        in_specs=[SM, VM, VM],
        out_specs=(VM, VM),
        scratch_shapes=[
            pltpu.VMEM((heads, length, 2 * HEAD), bf16),
            pltpu.VMEM((heads, 2 * HEAD, length), bf16),
            pltpu.VMEM((heads, HEAD + 16, length), bf16),
            pltpu.VMEM((heads, HEAD + 16, block), f32),
            pltpu.VMEM((heads, 8, block), f32),
        ],
        compiler_params=pltpu.CompilerParams(vmem_limit_bytes=VMEM_LIMIT),
        cost_estimate=pl.CostEstimate(flops=4 * 10**9, bytes_accessed=6 * 10**6, transcendentals=10**7),
        name="attend",
    )(seq, qkv, qkvt)


def attend_back_kernel(
    n_seq, block, seq_ref, qkv_ref, qkvt_ref, dot_ref, ot_ref, lse_ref, dqkv_ref, dqkvt_ref,
    kaug, qaug, vaug, doaug, qn, don, dqt, dk, dv,
):
    length = qkv_ref.shape[0]
    heads = qkv_ref.shape[1] // (3 * HEAD)
    width = heads * HEAD
    starts, ends, lives = seq_bounds(seq_ref, n_seq)
    kcols = key_columns(starts, ends, lives, length, 3)
    lane = lax.broadcasted_iota(jnp.int32, (length, HEAD), 1)
    vcols = jnp.where(lane < 3, -1.0, 0.0).astype(bf16)
    qrows = query_rows(starts, ends, length)
    zero = jnp.zeros((HEAD - 16, length), bf16)
    for h in range(heads):
        hs = slice(h * HEAD, (h + 1) * HEAD)
        kaug[h, :, :HEAD] = qkv_ref[:, width + h * HEAD : width + (h + 1) * HEAD]
        kaug[h, :, HEAD:] = kcols
        vaug[h, :, :HEAD] = qkv_ref[:, 2 * width + h * HEAD : 2 * width + (h + 1) * HEAD]
        vaug[h, :, HEAD:] = vcols
        qaug[h, :HEAD, :] = qkvt_ref[hs, :] * 0.125
        qaug[h, HEAD : HEAD + 16, :] = put_rows(qrows, split_three(lse_ref[h : h + 1, :]), n_seq).astype(bf16)
        qaug[h, HEAD + 16 :, :] = zero
        do = dot_ref[hs, :]
        delta = jnp.sum(do.astype(f32) * ot_ref[hs, :].astype(f32), axis=0, keepdims=True)
        doaug[h, :HEAD, :] = do
        doaug[h, HEAD : HEAD + 16, :] = put_rows(
            jnp.zeros((16, length), f32), split_three(delta), 0
        ).astype(bf16)
        doaug[h, HEAD + 16 :, :] = zero
        qn[h] = qkv_ref[:, hs] * 0.125
        don[h] = do.T
        dqt[h] = jnp.zeros((HEAD, length), f32)

    def k_step(kb, carry):
        ks = pl.ds(pl.multiple_of(kb * block, block), block)
        lo, hi = block_range(kb * block, kb * block + block - 1, starts, ends, block)
        dk[...] = jnp.zeros_like(dk)
        dv[...] = jnp.zeros_like(dv)

        def q_step(qb, inner):
            qs = pl.ds(pl.multiple_of(qb * block, block), block)
            for h in range(heads):
                p = jnp.exp(nn(kaug[h, ks, :], qaug[h, :, qs]))
                ds = (p * nn(vaug[h, ks, :], doaug[h, :, qs])).astype(bf16)
                dv[h] = dv[h] + nn(p.astype(bf16), don[h, qs, :])
                dk[h] = dk[h] + nn(ds, qn[h, qs, :])
                kt = qkvt_ref[width + h * HEAD : width + (h + 1) * HEAD, ks]
                dqt[h, :, qs] = dqt[h, :, qs] + nn(kt, ds)
            return inner

        lax.fori_loop(lo, hi, q_step, 0)
        for h in range(heads):
            vk = dk[h].astype(bf16)
            vv = dv[h].astype(bf16)
            a, b = width + h * HEAD, 2 * width + h * HEAD
            dqkv_ref[ks, a : a + HEAD] = vk
            dqkv_ref[ks, b : b + HEAD] = vv
            dqkvt_ref[a : a + HEAD, ks] = vk.T
            dqkvt_ref[b : b + HEAD, ks] = vv.T
        return carry

    lax.fori_loop(0, length // block, k_step, 0)
    for h in range(heads):
        v = (dqt[h] * 0.125).astype(bf16)
        dqkvt_ref[h * HEAD : (h + 1) * HEAD, :] = v
        dqkv_ref[:, h * HEAD : (h + 1) * HEAD] = v.T


def attend_back_call(n_seq, seq, qkv, qkvt, dot, ot, lse):
    length, cols = qkv.shape
    heads = cols // (3 * HEAD)
    block = 256
    nat = pltpu.VMEM((heads, length, 2 * HEAD), bf16)
    tra = pltpu.VMEM((heads, 2 * HEAD, length), bf16)
    return pl.pallas_call(
        functools.partial(attend_back_kernel, n_seq, block),
        out_shape=(sds((length, cols), bf16), sds((cols, length), bf16)),
        in_specs=[SM] + [VM] * 5,
        out_specs=(VM, VM),
        scratch_shapes=[
            nat, tra, nat, tra,
            pltpu.VMEM((heads, length, HEAD), bf16),
            pltpu.VMEM((heads, length, HEAD), bf16),
            pltpu.VMEM((heads, HEAD, length), f32),
            pltpu.VMEM((heads, block, HEAD), f32),
            pltpu.VMEM((heads, block, HEAD), f32),
        ],
        compiler_params=pltpu.CompilerParams(vmem_limit_bytes=VMEM_LIMIT),
        cost_estimate=pl.CostEstimate(flops=10**10, bytes_accessed=12 * 10**6, transcendentals=10**7),
        name="attend_back",
    )(seq, qkv, qkvt, dot, ot, lse)


def shard_of(r, c):
    return lax.rem(r + 2 * c, 4)


def spread_kernel(src_ref, dst_ref, ss, rs):
    d, r, c = me()
    half = lax.rem(r, 2)
    base = r - half
    n = dst_ref.shape[2]
    peers = [(d, flip(r), c), (d, flip(r), 1 - c), (d, r, 1 - c)]
    greet(peers)
    shard = shard_of(r, c)
    cps = []
    for i, dev in enumerate(peers):
        q = (dev[1] - base) * 2 + dev[2]
        src = src_ref.at[:, pl.ds(pl.multiple_of(q * n, n), n)]
        cp = remote(src, dst_ref.at[shard], ss.at[i], rs.at[i], dev)
        cp.start()
        cps.append(cp)
    q = half * 2 + c
    dst_ref[shard] = src_ref[:, pl.ds(pl.multiple_of(q * n, n), n)]
    for cp in cps:
        cp.wait()


def spread_call(src):
    rows, length = src.shape
    n = length // 4
    return pl.pallas_call(
        spread_kernel,
        out_shape=sds((4, rows, n), bf16),
        in_specs=[VM],
        out_specs=VM,
        scratch_shapes=[DMA((3,)), DMA((3,))],
        compiler_params=pltpu.CompilerParams(
            collective_id=2, has_side_effects=True, vmem_limit_bytes=VMEM_LIMIT
        ),
        name="spread",
    )(src)


def gather_kernel(src_ref, dst_ref, ss, rs):
    d, r, c = me()
    half = lax.rem(r, 2)
    n = src_ref.shape[2]
    peers = [(d, flip(r), c), (d, flip(r), 1 - c), (d, r, 1 - c)]
    greet(peers)
    q = half * 2 + c
    mine = pl.ds(pl.multiple_of(q * n, n), n)
    cps = []
    for i, dev in enumerate(peers):
        cp = remote(src_ref.at[shard_of(dev[1], dev[2])], dst_ref.at[:, mine], ss.at[i], rs.at[i], dev)
        cp.start()
        cps.append(cp)
    dst_ref[:, mine] = src_ref[shard_of(r, c)]
    for cp in cps:
        cp.wait()


def gather_call(src):
    _, rows, n = src.shape
    return pl.pallas_call(
        gather_kernel,
        out_shape=sds((rows, 4 * n), bf16),
        in_specs=[VM],
        out_specs=VM,
        scratch_shapes=[DMA((3,)), DMA((3,))],
        compiler_params=pltpu.CompilerParams(
            collective_id=3, has_side_effects=True, vmem_limit_bytes=VMEM_LIMIT
        ),
        name="gather",
    )(src)


UP, DOWN, OUT, VEC = 0, 768, 1536, 1728
BLOCK_ROWS = 1744


def middle_kernel(
    ot_ref, xf_ref, dya_ref, dyb_ref, w_ref, res_ref, dh1_ref, dot_ref, g_ref,
    wup, wdn, wo, vec, ub, hid, slope, gbuf, facc, yacc, wsem, gsem,
):
    r, c = lax.axis_index("row"), lax.axis_index("col")
    half = lax.rem(r, 2)
    wide = xf_ref.shape[3]
    width = 2 * wide
    tok = dya_ref.shape[0]
    loads_a, loads_b, loads_c = [], [], []
    for j in range(4):
        for cc in range(2):
            cs = slice(cc * wide, (cc + 1) * wide)
            loads_a.append((w_ref.at[j, cc, OUT:VEC], wo.at[j * 192 : (j + 1) * 192, cs], wsem.at[0]))
            for h in range(2):
                hs = slice(h * wide, (h + 1) * wide)
                loads_b.append((w_ref.at[j, cc, hs], wup.at[j, cs, hs], wsem.at[1]))
            loads_c.append((w_ref.at[j, cc, DOWN:OUT], wdn.at[j, :, cs], wsem.at[2]))
        loads_a.append((w_ref.at[j, 0, VEC:BLOCK_ROWS], ub.at[j], wsem.at[0]))
    for cc in range(2):
        loads_a.append((w_ref.at[0, cc, VEC:BLOCK_ROWS], vec.at[:, cc * wide : (cc + 1) * wide], wsem.at[0]))
    for group in (loads_a, loads_b, loads_c):
        for src, dst, sem in group:
            pltpu.make_async_copy(src, dst, sem).start()

    def settle(group):
        for src, dst, sem in group:
            pltpu.make_async_copy(src, dst, sem).wait()

    mine = pl.ds(pl.multiple_of(c * tok, tok), tok)
    x = jnp.concatenate([xf_ref[half, 0, mine, :], xf_ref[half, 1, mine, :]], axis=1).astype(f32)
    settle(loads_a)
    ob, g1, s1, db, g2, s2 = [vec[i : i + 1, :].astype(f32) for i in range(6)]
    o = ot_ref[...].reshape(width, tok).T
    h1 = x + (nn(o, wo[...]) + ob)
    mu = jnp.mean(h1, axis=1, keepdims=True)
    r1 = lax.rsqrt(jnp.mean(h1 * h1, axis=1, keepdims=True) - mu * mu + EPS)
    n1 = (h1 - mu) * r1
    y1 = (n1 * g1 + s1).astype(bf16)
    settle(loads_b)
    settle(loads_c)
    facc[...] = jnp.zeros_like(facc)

    def ahead(j, carry):
        bias = jnp.concatenate([ub[j, 6:7, :], ub[j, 7:8, :]], axis=1).astype(f32)
        u = nn(y1, wup[j]) + bias
        cdf = 0.5 * (1.0 + lax.erf(u * INV_ROOT_TWO))
        hj = (u * cdf).astype(bf16)
        hid[j] = hj
        slope[j] = cdf + u * jnp.exp(-0.5 * u * u) * INV_ROOT_TAU
        facc[...] += nn(hj, wdn[j])
        return carry

    lax.fori_loop(0, 4, ahead, 0)
    h2 = y1.astype(f32) + (facc[...] + db)
    mu2 = jnp.mean(h2, axis=1, keepdims=True)
    r2 = lax.rsqrt(jnp.mean(h2 * h2, axis=1, keepdims=True) - mu2 * mu2 + EPS)
    n2 = (h2 - mu2) * r2
    res_ref[...] = (n2 * g2 + s2).astype(bf16)
    own, other = dya_ref[...], dyb_ref[...]
    left = jnp.where(c == 0, own, other)
    right = jnp.where(c == 0, other, own)
    dy = jnp.concatenate([left, right], axis=1).astype(f32)
    e2 = dy * g2
    dh2 = r2 * (e2 - jnp.mean(e2, axis=1, keepdims=True) - n2 * jnp.mean(e2 * n2, axis=1, keepdims=True))
    g2g = jnp.sum(dy * n2, axis=0, keepdims=True)
    s2g = jnp.sum(dy, axis=0, keepdims=True)
    df = dh2.astype(bf16)
    dbg = jnp.sum(df.astype(f32), axis=0, keepdims=True)
    yacc[...] = dh2
    y1t = y1.T

    def back(j, carry):
        du = (nt(df, wdn[j]) * slope[j]).astype(bf16)
        ubg = jnp.sum(du.astype(f32), axis=0, keepdims=True)
        gd = tn(hid[j], df).astype(bf16)
        gu = nn(y1t, du).astype(bf16)
        for cc in range(2):
            cs = slice(cc * wide, (cc + 1) * wide)
            for h in range(2):
                gbuf[j, cc, h * wide : (h + 1) * wide, :] = gu[cs, h * wide : (h + 1) * wide]
            gbuf[j, cc, DOWN:OUT, :] = gd[:, cs]
        ub[j, 6:7, :] = ubg[:, :wide].astype(bf16)
        ub[j, 7:8, :] = ubg[:, wide:].astype(bf16)
        yacc[...] += nt(du, wup[j])
        return carry

    lax.fori_loop(0, 4, back, 0)
    dy1 = yacc[...]
    e1 = dy1 * g1
    dh1 = r1 * (e1 - jnp.mean(e1, axis=1, keepdims=True) - n1 * jnp.mean(e1 * n1, axis=1, keepdims=True))
    dh1_ref[...] = dh1
    g1g = jnp.sum(dy1 * n1, axis=0, keepdims=True)
    s1g = jnp.sum(dy1, axis=0, keepdims=True)
    da = dh1.astype(bf16)
    obg = jnp.sum(da.astype(f32), axis=0, keepdims=True)
    dot_ref[...] = nt(da, wo[...]).T.astype(bf16).reshape(dot_ref.shape)
    go = nn(ot_ref[...].reshape(width, tok), da).astype(bf16)
    pad = g_ref.shape[2] - VEC
    row = lax.broadcasted_iota(jnp.int32, (pad, wide), 0)
    for j in range(4):
        for cc in range(2):
            cs = slice(cc * wide, (cc + 1) * wide)
            gbuf[j, cc, OUT:VEC, :] = go[j * 192 : (j + 1) * 192, cs]
            tail = jnp.zeros((pad, wide), f32)
            for i, v in enumerate((obg, g1g, s1g, dbg, g2g, s2g)):
                tail = jnp.where(row == i, v[:, cs], tail)
            tail = jnp.where(row == 6, ub[j, 6:7, :].astype(f32), tail)
            tail = jnp.where(row == 7, ub[j, 7:8, :].astype(f32), tail)
            gbuf[j, cc, VEC:, :] = tail.astype(bf16)
    out = pltpu.make_async_copy(gbuf, g_ref, gsem)
    out.start()
    out.wait()


def middle_call(ot, xf, dya, dyb, w, g_rows):
    tok, wide = dya.shape
    width = 2 * wide
    return pl.pallas_call(
        middle_kernel,
        out_shape=(
            sds((tok, width), bf16),
            sds((tok, width), f32),
            sds((4, width // 4, tok), bf16),
            sds((4, 2, g_rows, wide), bf16),
        ),
        in_specs=[VM] * 4 + [ANY],
        out_specs=(VM, VM, VM, ANY),
        scratch_shapes=[
            pltpu.VMEM((4, width, width), bf16),
            pltpu.VMEM((4, width, width), bf16),
            pltpu.VMEM((width, width), bf16),
            pltpu.VMEM((16, width), bf16),
            pltpu.VMEM((4, 16, wide), bf16),
            pltpu.VMEM((4, tok, width), bf16),
            pltpu.VMEM((4, tok, width), f32),
            pltpu.VMEM((4, 2, g_rows, wide), bf16),
            pltpu.VMEM((tok, width), f32),
            pltpu.VMEM((tok, width), f32),
            DMA((3,)),
            DMA,
        ],
        compiler_params=pltpu.CompilerParams(vmem_limit_bytes=VMEM_LIMIT),
        cost_estimate=pl.CostEstimate(flops=16 * 10**9, bytes_accessed=30 * 10**6, transcendentals=4 * 10**6),
        name="middle",
    )(ot, xf, dya, dyb, w)


def return_kernel(
    n_dp, dqkv_ref, dqkvt_ref, wq_ref, xf_ref, dh1_ref, res_ref, deal_ref,
    out_ref, ig_ref, gq_ref,
    back_a, back_b, fin, tocore, fromcore, toz, fromz, s_a, r_a, s_b, r_b, s_c, r_c, s_z, r_z,
):
    d, r, c = me()
    half = lax.rem(r, 2)
    tok = dh1_ref.shape[0]
    wide = wq_ref.shape[2] if False else xf_ref.shape[3]
    width = 2 * wide
    tokens = 2 * tok
    piece = tokens // n_dp
    n_half = n_dp // 2
    core = (d, r, 1 - c)
    zdev = (d, flip(r), c)
    peers = [(lax.rem(d + k, n_dp), r, cc) for k in range(1, n_dp) for cc in (0, 1)]
    greet(peers + [core, zdev])

    def grp(g):
        return pl.ds(pl.multiple_of(g * piece, piece), piece)

    def send_back(src, back, ss, rs):
        for i in range(n_half):
            s = c * n_half + i
            for cc in range(2):
                ref = src.at[cc, i * piece : (i + 1) * piece, :]
                cp = remote(ref, back.at[grp(d), :], ss.at[i, cc], rs.at[d], (s, r, cc))
                local = (s == d) & (c == cc)

                @pl.when(jnp.logical_not(local))
                def _():
                    cp.start()

                @pl.when(local)
                def _():
                    back[grp(d), :] = src[cc, i * piece : (i + 1) * piece, :]

    def sent_back(src, back, ss, rs):
        for i in range(n_half):
            s = c * n_half + i
            for cc in range(2):
                ref = src.at[cc, i * piece : (i + 1) * piece, :]

                @pl.when(jnp.logical_not((s == d) & (c == cc)))
                def _():
                    remote(ref, back.at[grp(d), :], ss.at[i, cc], rs.at[d], (s, r, cc)).wait_send()

    def got_back(src, back, ss, rs):
        holder = lax.div(d, n_half)
        for g in range(n_dp):

            @pl.when(jnp.logical_not((d == g) & (holder == c)))
            def _():
                remote(
                    src.at[0, 0:piece, :], back.at[grp(g), :], ss.at[0, 0], rs.at[g], (d, r, 1 - c)
                ).wait_recv()

    fin[0, 0] = res_ref[:, :wide]
    fin[0, 1] = res_ref[:, wide:]
    send_back(fin.at[0], back_a, s_a, r_a)

    w0 = wq_ref[0, :wide, :]
    w1 = wq_ref[1, :wide, :]

    def part(h, cc):
        q = h * 2 + cc
        rows = dqkv_ref[pl.ds(pl.multiple_of(q * tok, tok), tok), :]
        return jnp.concatenate([nt(rows, w0), nt(rows, w1)], axis=1)

    tocore[0] = part(1 - half, 1 - c).astype(bf16)
    cp_far = remote(tocore.at[0], fromcore.at[0], s_c.at[0], r_c.at[0], core)
    cp_far.start()
    tocore[1] = part(half, 1 - c).astype(bf16)
    cp_near = remote(tocore.at[1], fromcore.at[1], s_c.at[1], r_c.at[1], core)
    cp_near.start()
    far = part(1 - half, c)
    cp_far.wait_recv()
    toz[...] = (far + fromcore[0].astype(f32)).astype(bf16)
    cp_z = remote(toz, fromz, s_z, r_z, zdev)
    cp_z.start()
    total = part(half, c) + dh1_ref[...]
    n_cols = dqkvt_ref.shape[0]
    length = dqkvt_ref.shape[1]
    for f in range(2):
        g = nn(dqkvt_ref[:, : length // 2], xf_ref[0, f]) + nn(dqkvt_ref[:, length // 2 :], xf_ref[1, f])
        gq_ref[f, :n_cols, :] = g.astype(bf16)
    third = n_cols // 3
    sums = jnp.sum(dqkv_ref[...].astype(f32), axis=0, keepdims=True)
    bias = jnp.concatenate([sums[:, :third], sums[:, 2 * third :]], axis=1)
    pad = gq_ref.shape[1] - n_cols
    row = lax.broadcasted_iota(jnp.int32, (pad, wide), 0)
    tail = jnp.where(row == 0, bias, 0.0).astype(bf16)
    for f in range(2):
        gq_ref[f, n_cols:, :] = tail
    place = (lax.broadcasted_iota(jnp.int32, (tokens, tokens), 0) == deal_ref[...]).astype(bf16)
    got_back(fin.at[0], back_a, s_a, r_a)
    out_ref[...] = nn(place, back_a[...]).astype(bf16)
    cp_near.wait_recv()
    total = total + fromcore[1].astype(f32)
    cp_z.wait_recv()
    total = (total + fromz[...].astype(f32)).astype(bf16)
    fin[1, 0] = total[:, :wide]
    fin[1, 1] = total[:, wide:]
    send_back(fin.at[1], back_b, s_b, r_b)
    got_back(fin.at[1], back_b, s_b, r_b)
    ig_ref[...] = nn(place, back_b[...]).astype(bf16)
    sent_back(fin.at[0], back_a, s_a, r_a)
    sent_back(fin.at[1], back_b, s_b, r_b)
    cp_far.wait_send()
    cp_near.wait_send()
    cp_z.wait_send()


def return_call(n_dp, dqkv, dqkvt, wq, xf, dh1, res, deal_row, gq_rows):
    tok, width = dh1.shape
    wide = width // 2
    tokens = 2 * tok
    n_half = n_dp // 2
    return pl.pallas_call(
        functools.partial(return_kernel, n_dp),
        out_shape=(
            sds((tokens, wide), bf16),
            sds((tokens, wide), bf16),
            sds((2, gq_rows, wide), bf16),
        ),
        in_specs=[VM] * 7,
        out_specs=(VM,) * 3,
        scratch_shapes=[
            pltpu.VMEM((tokens, wide), bf16),
            pltpu.VMEM((tokens, wide), bf16),
            pltpu.VMEM((2, 2, tok, wide), bf16),
            pltpu.VMEM((2, tok, width), bf16),
            pltpu.VMEM((2, tok, width), bf16),
            pltpu.VMEM((tok, width), bf16),
            pltpu.VMEM((tok, width), bf16),
            DMA((n_half, 2)), DMA((n_dp,)),
            DMA((n_half, 2)), DMA((n_dp,)),
            DMA((2,)), DMA((2,)), DMA, DMA,
        ],
        compiler_params=pltpu.CompilerParams(
            collective_id=4, has_side_effects=True, vmem_limit_bytes=VMEM_LIMIT
        ),
        name="return",
    )(dqkv, dqkvt, wq, xf, dh1, res, deal_row)


def round_up(v, m):
    return (v + m - 1) // m * m


def on_device(
    n_dp, inputs, out_grad, deal, seq_lengths, key_trim, query_weight, query_bias, key_weight,
    value_weight, value_bias, out_weight, out_bias, first_gain, first_shift, up_weight, up_bias,
    down_weight, down_bias, second_gain, second_shift,
):
    d, r, c = me()
    wide = inputs.shape[1]
    n_seq = seq_lengths.shape[1]
    unit = 16 * n_dp // math.gcd(16, n_dp)
    step = 16 * n_dp

    blob = jnp.concatenate(
        [up_weight[:, :wide], up_weight[:, wide:], down_weight, out_weight]
        + [v[None, :] for v in (out_bias, first_gain, first_shift, down_bias, second_gain, second_shift)]
        + [up_bias.reshape(2, wide)],
        axis=0,
    )
    rows_w = round_up(BLOCK_ROWS, unit)
    blob = jnp.pad(blob, ((0, rows_w - blob.shape[0]), (0, 0)))
    share = lax.dynamic_slice_in_dim(blob, d * (rows_w // n_dp), rows_w // n_dp, 0)
    gathered = lax.all_gather(share, ("row", "col", "dp"), axis=0, tiled=True)
    gathered = gathered.reshape(4, 2, rows_w, wide)

    third = query_weight.shape[1]
    bias_row = jnp.concatenate([query_bias, jnp.zeros((third,), bf16), value_bias])[None, :]
    wqkv = jnp.concatenate([query_weight, key_weight, value_weight], axis=1)
    wqkv = jnp.concatenate([wqkv, jnp.pad(bias_row, ((0, 15), (0, 0)))], axis=0)
    seq = jnp.pad(jnp.concatenate([seq_lengths, key_trim], axis=0), ((0, 6), (0, 128 - n_seq)))

    xf, dya, dyb, qkv, qkvt, wq, seq = deal_call(n_dp, inputs, out_grad, deal.reshape(-1, 1), wqkv, seq)
    ot, lse = attend_call(n_seq, seq, qkv, qkvt)
    ot_mid = spread_call(ot)
    g_rows = round_up(VEC + 16, step)
    res, dh1, dot_mid, grads = middle_call(ot_mid, xf, dya, dyb, gathered, g_rows)
    dot = gather_call(dot_mid)
    dqkv, dqkvt = attend_back_call(n_seq, seq, qkv, qkvt, dot, ot, lse)
    gq_rows = round_up(3 * third + 16, step)
    output, input_grad, gq = return_call(n_dp, dqkv, dqkvt, wq, xf, dh1, res, deal, gq_rows)

    mine = lax.psum_scatter(grads.reshape(-1, wide), ("row", "col", "dp"), scatter_dimension=0, tiled=True)
    mine = lax.all_gather(mine, "dp", axis=0, tiled=True)
    placed = jnp.where((jnp.arange(4) == shard_of(r, c))[:, None, None, None], gq[None], 0).astype(bf16)
    mine_q = lax.psum_scatter(placed.reshape(-1, wide), ("row", "col", "dp"), scatter_dimension=0, tiled=True)
    mine_q = lax.all_gather(mine_q, "dp", axis=0, tiled=True)

    g = mine.astype(f32)
    up_grad = jnp.concatenate([g[:wide], g[wide : 2 * wide]], axis=1)
    down_grad = g[DOWN:OUT]
    out_grad_w = g[OUT:VEC]
    vec = g[VEC : VEC + 8]
    gqf = mine_q.astype(f32)
    query_grad = gqf[:third].T
    key_grad = gqf[third : 2 * third].T
    value_grad = gqf[2 * third : 3 * third].T
    brow = gqf[3 * third]
    return (
        output, input_grad, query_grad, brow[:third], key_grad, value_grad, brow[third:], out_grad_w,
        vec[0], vec[1], vec[2], up_grad, vec[6:8].reshape(-1), down_grad, vec[3], vec[4], vec[5],
    )


def solution(mesh):
    n_dp = mesh.shape["dp"]
    tok = P(("dp", "row"), "col")
    one = P("col")
    row = P("row")
    a = P("col", "row")
    b = P("row", "col")
    seqs = P(("dp", "col"), None)
    in_specs = (
        tok, tok, P(("dp", "row"), None), seqs, seqs, a, row, a, a, row, b, one, one, one, a, row, b, one, one, one,
    )
    out_specs = (tok, tok, a, row, a, a, row, b, one, one, one, a, row, b, one, one, one)
    return jax.shard_map(
        functools.partial(on_device, n_dp), mesh=mesh, in_specs=in_specs, out_specs=out_specs, check_vma=False
    )
```

```python
import functools

import jax
import jax.numpy as jnp
from jax import lax
from jax.experimental import pallas as pl
from jax.experimental.pallas import tpu as pltpu
from jax.sharding import PartitionSpec as P

MESH = pl.DeviceIdType.MESH
f32 = jnp.float32
bf16 = jnp.bfloat16

HEAD = 64
EPS = 1e-05
FAR = -1e30
INV_ROOT_TWO = 0.7071067811865476
INV_ROOT_TAU = 0.3989422804014327
VMEM_LIMIT = 62 * 1024 * 1024
DOWN, OUT, VEC = 768, 1536, 1728

VM = pl.BlockSpec(memory_space=pltpu.VMEM)
SM = pl.BlockSpec(memory_space=pltpu.SMEM)
ANY = pl.BlockSpec(memory_space=pl.ANY)
DMA = pltpu.SemaphoreType.DMA


def nn(a, b):
    return lax.dot_general(a, b, (((1,), (0,)), ((), ())), preferred_element_type=f32)


def nt(a, b):
    return lax.dot_general(a, b, (((1,), (1,)), ((), ())), preferred_element_type=f32)


def tn(a, b):
    return lax.dot_general(a, b, (((0,), (0,)), ((), ())), preferred_element_type=f32)


def sds(shape, dtype):
    return jax.ShapeDtypeStruct(shape, dtype)


def me():
    return lax.axis_index("dp"), lax.axis_index("row"), lax.axis_index("col")


def flip(v):
    return v + 1 - 2 * lax.rem(v, 2)


def remote(src, dst, ssem, rsem, dev):
    return pltpu.make_async_remote_copy(
        src_ref=src, dst_ref=dst, send_sem=ssem, recv_sem=rsem, device_id=dev, device_id_type=MESH
    )


def greet(devs):
    barrier = pltpu.get_barrier_semaphore()
    for dev in devs:
        pl.semaphore_signal(barrier, inc=1, device_id=dev, device_id_type=MESH)
    pl.semaphore_wait(barrier, len(devs))


def deal_kernel(
    n_dp, rows_w, x_ref, dy_ref, deal_ref, qw_ref, kw_ref, vw_ref, qb_ref, vb_ref, up_ref, dn_ref, ow_ref,
    ob_ref, g1_ref, s1_ref, db_ref, g2_ref, s2_ref, ub_ref, len_ref, trim_ref,
    xf_ref, dys_ref, qkv_ref, qkvt_ref, wq_ref, seqo_ref, wg_ref,
    xs, seq, seqrx, w, bias, biases, blob, col,
    sx, rx, sc, rc, sz, rz, sc2, rc2, sw, rw, sb, rb, sm, rm, ss, rs, sf, rf, sl,
):
    d, r, c = me()
    half = lax.rem(r, 2)
    tokens, wide = x_ref.shape
    piece = tokens // n_dp
    third = qw_ref.shape[0]
    core = (d, r, 1 - c)
    zdev = (d, flip(r), c)
    far_row = lax.rem(r + 2, 4)
    ring = [(lax.rem(d + k, n_dp), r, c) for k in range(1, n_dp)]
    rows_dev = [(d, lax.rem(r + k, 4), c) for k in (1, 2, 3)]
    greet(ring + rows_dev + [core, (d, far_row, 1 - c)])

    blob[0:wide, :] = up_ref[:, :wide]
    blob[wide : 2 * wide, :] = up_ref[:, wide:]
    blob[DOWN:OUT, :] = dn_ref[...]
    blob[OUT:VEC, :] = ow_ref[...]
    vecs = [v[...].reshape(1, wide) for v in (ob_ref, g1_ref, s1_ref, db_ref, g2_ref, s2_ref)]
    vecs += [ub_ref[0:wide].reshape(1, wide), ub_ref[wide : 2 * wide].reshape(1, wide)]
    row = lax.broadcasted_iota(jnp.int32, (16, wide), 0)
    tail = jnp.zeros((16, wide), f32)
    for i, v in enumerate(vecs):
        tail = jnp.where(row == i, v.astype(f32), tail)
    blob[VEC : VEC + 16, :] = tail.astype(bf16)
    blob[VEC + 16 :, :] = jnp.zeros((rows_w - VEC - 16, wide), bf16)
    share = rows_w // n_dp
    my_share = pl.ds(pl.multiple_of(d * share, share), share)
    share_cp = [
        remote(blob.at[my_share, :], wg_ref.at[r, my_share, :], ss.at[k], rs.at[k], dev)
        for k, dev in enumerate(rows_dev)
    ]
    for cp in share_cp:
        cp.start()
    local_w = pltpu.make_async_copy(blob, wg_ref.at[r], sl)
    local_w.start()

    def rows(s):
        return pl.ds(pl.multiple_of(s * piece, piece), piece)

    col[...] = jnp.broadcast_to(deal_ref[...], (8, tokens)).T
    lane = lax.broadcasted_iota(jnp.int32, (piece, tokens), 1)
    sends = []
    for k in list(range(1, n_dp)) + [0]:
        dest = lax.rem(d + k, n_dp)
        pick = (col[rows(dest), 0:1] == lane).astype(bf16)
        px = nn(pick, x_ref[...]).astype(bf16)
        if k:
            xs[k] = px
            cp = remote(xs.at[k], xf_ref.at[half, c, rows(d), :], sx.at[k], rx.at[k], (dest, r, c))
            cp.start()
            sends.append(cp)
        else:
            xf_ref[half, c, rows(d), :] = px

    w[:third, :] = qw_ref[...]
    w[third : 2 * third, :] = kw_ref[...]
    w[2 * third :, :] = vw_ref[...]
    w_far = remote(w, wq_ref.at[c], sw.at[0], rw.at[c], (d, far_row, 1))
    w_far.start()
    w_near = remote(w, wq_ref.at[1], sw.at[1], rw.at[1], (d, r, 0))
    flat = jnp.concatenate(
        [qb_ref[...].reshape(1, third), jnp.zeros((1, third), bf16), vb_ref[...].reshape(1, third)], axis=1
    )
    bias[...] = jnp.broadcast_to(flat.astype(f32), (8, 3 * third))
    b_far = remote(bias, biases.at[1], sb.at[0], rb.at[0], (d, far_row, 1))

    @pl.when(c == 0)
    def _():
        wq_ref[0] = w[...]
        b_far.start()

    @pl.when(c == 1)
    def _():
        w_near.start()

    biases[0] = bias[...]
    seq[...] = jnp.zeros_like(seq)
    seq[0:1, 0 : len_ref.shape[1]] = len_ref[...]
    seq[1:2, 0 : len_ref.shape[1]] = trim_ref[...]
    seq_cp = remote(seq, seqrx, sm.at[0], rm.at[0], core)
    seq_cp.start()

    core_cp, z_cp, core2_cp = [], [], []
    for k in range(n_dp):
        s = lax.rem(d - k + n_dp, n_dp)
        ref = xf_ref.at[half, c, rows(s), :]
        if k:
            sends[k - 1].wait_recv()
        a = remote(ref, ref, sz.at[k], rz.at[k], zdev)
        a.start()
        b = remote(ref, ref, sc.at[k], rc.at[k], core)
        b.start()
        z_cp.append(a)
        core_cp.append(b)

    pass_cp = []
    for k in range(3):
        share_cp[k].wait_recv()
        ref = wg_ref.at[lax.rem(r - k + 3, 4), my_share, :]
        for i, dev in enumerate(ring):
            cp = remote(ref, ref, sf.at[k, i], rf.at[k, i], dev)
            cp.start()
            pass_cp.append(cp)
        if k == 0:
            for dest in range(n_dp):
                pick = (col[dest * piece : (dest + 1) * piece, 0:1] == lane).astype(bf16)
                dys_ref[dest] = nn(pick, dy_ref[...]).astype(bf16)

    for k in range(n_dp):
        s = lax.rem(d - k + n_dp, n_dp)
        z_cp[k].wait_recv()
        ref = xf_ref.at[1 - half, c, rows(s), :]
        b = remote(ref, ref, sc2.at[k], rc2.at[k], core)
        b.start()
        core2_cp.append(b)

    @pl.when(c == 0)
    def _():
        w_near.wait_recv()
        b_far.wait_send()

    @pl.when(c == 1)
    def _():
        w_near.wait_send()
        b_far.wait_recv()
        remote(w, wq_ref.at[0], sw.at[0], rw.at[0], (d, far_row, 1)).wait_recv()
        remote(w, wq_ref.at[1], sw.at[0], rw.at[1], (d, far_row, 1)).wait_recv()

    w_far.wait_send()
    for k in range(n_dp):
        core_cp[k].wait_recv()
        core2_cp[k].wait_recv()
    brow = jnp.where(c == 0, biases[0], biases[1])[0:1, :]

    def project(i, carry):
        h = lax.div(i, 2)
        base = pl.ds(pl.multiple_of(lax.rem(i, 2) * 512, 512), 512)
        y = nt(xf_ref[h, 0, base, :], wq_ref[0]) + nt(xf_ref[h, 1, base, :], wq_ref[1]) + brow
        y = y.astype(bf16)
        out = pl.ds(pl.multiple_of(i * 512, 512), 512)
        qkv_ref[out, :] = y
        qkvt_ref[:, out] = y.T
        return carry

    lax.fori_loop(0, 4, project, 0)
    seq_cp.wait()
    is_mine = lax.div(r, 2) == c
    seqo_ref[...] = jnp.where(is_mine, seq[...], seqrx[...])
    for cp in pass_cp:
        cp.wait()
    for cp in sends + core_cp + z_cp + core2_cp + share_cp:
        cp.wait_send()
    local_w.wait()


def deal_call(n_dp, rows_w, args):
    x, qw = args[0], args[3]
    tokens, wide = x.shape
    piece = tokens // n_dp
    cols = 3 * qw.shape[0]
    return pl.pallas_call(
        functools.partial(deal_kernel, n_dp, rows_w),
        out_shape=(
            sds((2, 2, tokens, wide), bf16),
            sds((n_dp, piece, wide), bf16),
            sds((2 * tokens, cols), bf16),
            sds((cols, 2 * tokens), bf16),
            sds((2, cols, wide), bf16),
            sds((8, 128), jnp.int32),
            sds((4, rows_w, wide), bf16),
        ),
        in_specs=[VM] * len(args),
        out_specs=(VM,) * 6 + (ANY,),
        scratch_shapes=[
            pltpu.VMEM((n_dp, piece, wide), bf16),
            pltpu.VMEM((8, 128), jnp.int32),
            pltpu.VMEM((8, 128), jnp.int32),
            pltpu.VMEM((cols, wide), bf16),
            pltpu.VMEM((8, cols), f32),
            pltpu.VMEM((2, 8, cols), f32),
            pltpu.VMEM((rows_w, wide), bf16),
            pltpu.VMEM((tokens, 8), jnp.int32),
        ]
        + [DMA((n_dp,))] * 8
        + [DMA((2,))] * 6
        + [DMA((3,))] * 2
        + [DMA((3, n_dp - 1))] * 2
        + [DMA],
        compiler_params=pltpu.CompilerParams(
            collective_id=1, has_side_effects=True, vmem_limit_bytes=VMEM_LIMIT
        ),
        name="deal",
    )(*args)


def seq_bounds(seq_ref, n_seq):
    ends, total = [], 0
    for j in range(n_seq):
        total = total + seq_ref[0, j]
        ends.append(total)
    starts = [ends[j] - seq_ref[0, j] for j in range(n_seq)]
    lives = [starts[j] + jnp.maximum(seq_ref[0, j] - seq_ref[1, j], 1) for j in range(n_seq)]
    return starts, ends, lives


def block_range(first, last, starts, ends, block):
    lo, hi = 0, ends[-1]
    for j in range(len(ends)):
        lo = jnp.where((first >= starts[j]) & (first < ends[j]), starts[j], lo)
        hi = jnp.where((last >= starts[j]) & (last < ends[j]), ends[j], hi)
    return lax.div(lo, block), lax.div(hi + block - 1, block)


def key_columns(starts, ends, lives, length, extra):
    pos = lax.broadcasted_iota(jnp.int32, (length, HEAD), 0)
    lane = lax.broadcasted_iota(jnp.int32, (length, HEAD), 1)
    n_seq = len(ends)
    cols = jnp.where(lane < n_seq, FAR, 0.0)
    cols = jnp.where((lane >= n_seq) & (lane < n_seq + extra), -1.0, cols)
    for j in range(n_seq):
        live = (pos >= starts[j]) & (pos < lives[j]) & (lane == j)
        cols = jnp.where(live, 0.0, cols)
    return cols.astype(bf16)


def query_rows(starts, ends, length):
    pos = lax.broadcasted_iota(jnp.int32, (16, length), 1)
    row = lax.broadcasted_iota(jnp.int32, (16, length), 0)
    out = jnp.zeros((16, length), f32)
    for j in range(len(ends)):
        out = jnp.where((row == j) & (pos >= starts[j]) & (pos < ends[j]), 1.0, out)
    return out


def split_three(v):
    hi = v.astype(bf16).astype(f32)
    mid = (v - hi).astype(bf16).astype(f32)
    low = (v - hi - mid).astype(bf16).astype(f32)
    return hi, mid, low


def put_rows(base, values, first):
    row = lax.broadcasted_iota(jnp.int32, base.shape, 0)
    for i, v in enumerate(values):
        base = jnp.where(row == first + i, v, base)
    return base


def attend_kernel(n_seq, block, seq_ref, qkv_ref, qkvt_ref, ot_ref, lse_ref, kaug, qaug, vaug, acc, mx):
    length = qkv_ref.shape[0]
    heads = qkv_ref.shape[1] // (3 * HEAD)
    width = heads * HEAD
    starts, ends, lives = seq_bounds(seq_ref, n_seq)
    kcols = key_columns(starts, ends, lives, length, 0)
    qrows = query_rows(starts, ends, length).astype(bf16)
    ones = (lax.broadcasted_iota(jnp.int32, (16, length), 0) == 0).astype(f32).astype(bf16)
    for h in range(heads):
        kaug[h, :, :HEAD] = qkv_ref[:, width + h * HEAD : width + (h + 1) * HEAD]
        kaug[h, :, HEAD:] = kcols
        qaug[h, :HEAD, :] = qkvt_ref[h * HEAD : (h + 1) * HEAD, :] * 0.125
        qaug[h, HEAD : HEAD + 16, :] = qrows
        qaug[h, HEAD + 16 :, :] = jnp.zeros((HEAD - 16, length), bf16)
        vaug[h, :HEAD, :] = qkvt_ref[2 * width + h * HEAD : 2 * width + (h + 1) * HEAD, :]
        vaug[h, HEAD:, :] = ones
    lse_ref[...] = jnp.zeros_like(lse_ref)

    def q_step(qb, carry):
        qs = pl.ds(pl.multiple_of(qb * block, block), block)
        lo, hi = block_range(qb * block, qb * block + block - 1, starts, ends, block)
        for h in range(heads):
            acc[h] = jnp.zeros((HEAD + 16, block), f32)
            mx[h] = jnp.full((8, block), 2 * FAR, f32)

        def k_step(kb, inner):
            ks = pl.ds(pl.multiple_of(kb * block, block), block)
            for h in range(heads):
                s = nn(kaug[h, ks, :], qaug[h, :, qs])
                old = mx[h, 0:1, :]
                new = jnp.maximum(old, jnp.max(s, axis=0, keepdims=True))
                p = jnp.exp(s - new).astype(bf16)
                acc[h] = acc[h] * jnp.exp(old - new) + nn(vaug[h, :, ks], p)
                mx[h] = jnp.broadcast_to(new, (8, block))
            return inner

        lax.fori_loop(lo, hi, k_step, 0)
        for h in range(heads):
            total = acc[h, HEAD : HEAD + 1, :]
            ot_ref[h * HEAD : (h + 1) * HEAD, qs] = (acc[h, :HEAD, :] / total).astype(bf16)
            lse_ref[h : h + 1, qs] = mx[h, 0:1, :] + jnp.log(total)
        return carry

    lax.fori_loop(0, length // block, q_step, 0)


def attend_call(n_seq, seq, qkv, qkvt):
    length, cols = qkv.shape
    heads = cols // (3 * HEAD)
    block = 256
    return pl.pallas_call(
        functools.partial(attend_kernel, n_seq, block),
        out_shape=(sds((heads * HEAD, length), bf16), sds((8, length), f32)),
        in_specs=[SM, VM, VM],
        out_specs=(VM, VM),
        scratch_shapes=[
            pltpu.VMEM((heads, length, 2 * HEAD), bf16),
            pltpu.VMEM((heads, 2 * HEAD, length), bf16),
            pltpu.VMEM((heads, HEAD + 16, length), bf16),
            pltpu.VMEM((heads, HEAD + 16, block), f32),
            pltpu.VMEM((heads, 8, block), f32),
        ],
        compiler_params=pltpu.CompilerParams(vmem_limit_bytes=VMEM_LIMIT),
        cost_estimate=pl.CostEstimate(flops=4 * 10**9, bytes_accessed=6 * 10**6, transcendentals=10**7),
        name="attend",
    )(seq, qkv, qkvt)


def attend_back_kernel(
    n_seq, block, seq_ref, qkv_ref, qkvt_ref, dot_ref, ot_ref, lse_ref, dqkv_ref, dqkvt_ref,
    kaug, qaug, vaug, doaug, qn, don, dqt, dk, dv,
):
    length = qkv_ref.shape[0]
    heads = qkv_ref.shape[1] // (3 * HEAD)
    width = heads * HEAD
    starts, ends, lives = seq_bounds(seq_ref, n_seq)
    kcols = key_columns(starts, ends, lives, length, 3)
    lane = lax.broadcasted_iota(jnp.int32, (length, HEAD), 1)
    vcols = jnp.where(lane < 3, -1.0, 0.0).astype(bf16)
    qrows = query_rows(starts, ends, length)
    zero = jnp.zeros((HEAD - 16, length), bf16)
    for h in range(heads):
        hs = slice(h * HEAD, (h + 1) * HEAD)
        kaug[h, :, :HEAD] = qkv_ref[:, width + h * HEAD : width + (h + 1) * HEAD]
        kaug[h, :, HEAD:] = kcols
        vaug[h, :, :HEAD] = qkv_ref[:, 2 * width + h * HEAD : 2 * width + (h + 1) * HEAD]
        vaug[h, :, HEAD:] = vcols
        qaug[h, :HEAD, :] = qkvt_ref[hs, :] * 0.125
        qaug[h, HEAD : HEAD + 16, :] = put_rows(qrows, split_three(lse_ref[h : h + 1, :]), n_seq).astype(bf16)
        qaug[h, HEAD + 16 :, :] = zero
        do = dot_ref[hs, :]
        delta = jnp.sum(do.astype(f32) * ot_ref[hs, :].astype(f32), axis=0, keepdims=True)
        doaug[h, :HEAD, :] = do
        doaug[h, HEAD : HEAD + 16, :] = put_rows(
            jnp.zeros((16, length), f32), split_three(delta), 0
        ).astype(bf16)
        doaug[h, HEAD + 16 :, :] = zero
        qn[h] = qkv_ref[:, hs] * 0.125
        don[h] = do.T
        dqt[h] = jnp.zeros((HEAD, length), f32)

    def k_step(kb, carry):
        ks = pl.ds(pl.multiple_of(kb * block, block), block)
        lo, hi = block_range(kb * block, kb * block + block - 1, starts, ends, block)
        dk[...] = jnp.zeros_like(dk)
        dv[...] = jnp.zeros_like(dv)

        def q_step(qb, inner):
            qs = pl.ds(pl.multiple_of(qb * block, block), block)
            for h in range(heads):
                p = jnp.exp(nn(kaug[h, ks, :], qaug[h, :, qs]))
                ds = (p * nn(vaug[h, ks, :], doaug[h, :, qs])).astype(bf16)
                dv[h] = dv[h] + nn(p.astype(bf16), don[h, qs, :])
                dk[h] = dk[h] + nn(ds, qn[h, qs, :])
                kt = qkvt_ref[width + h * HEAD : width + (h + 1) * HEAD, ks]
                dqt[h, :, qs] = dqt[h, :, qs] + nn(kt, ds)
            return inner

        lax.fori_loop(lo, hi, q_step, 0)
        for h in range(heads):
            vk = dk[h].astype(bf16)
            vv = dv[h].astype(bf16)
            a, b = width + h * HEAD, 2 * width + h * HEAD
            dqkv_ref[ks, a : a + HEAD] = vk
            dqkv_ref[ks, b : b + HEAD] = vv
            dqkvt_ref[a : a + HEAD, ks] = vk.T
            dqkvt_ref[b : b + HEAD, ks] = vv.T
        return carry

    lax.fori_loop(0, length // block, k_step, 0)
    for h in range(heads):
        v = (dqt[h] * 0.125).astype(bf16)
        dqkvt_ref[h * HEAD : (h + 1) * HEAD, :] = v
        dqkv_ref[:, h * HEAD : (h + 1) * HEAD] = v.T


def attend_back_call(n_seq, seq, qkv, qkvt, dot, ot, lse):
    length, cols = qkv.shape
    heads = cols // (3 * HEAD)
    block = 256
    nat = pltpu.VMEM((heads, length, 2 * HEAD), bf16)
    tra = pltpu.VMEM((heads, 2 * HEAD, length), bf16)
    return pl.pallas_call(
        functools.partial(attend_back_kernel, n_seq, block),
        out_shape=(sds((length, cols), bf16), sds((cols, length), bf16)),
        in_specs=[SM] + [VM] * 5,
        out_specs=(VM, VM),
        scratch_shapes=[
            nat, tra, nat, tra,
            pltpu.VMEM((heads, length, HEAD), bf16),
            pltpu.VMEM((heads, length, HEAD), bf16),
            pltpu.VMEM((heads, HEAD, length), f32),
            pltpu.VMEM((heads, block, HEAD), f32),
            pltpu.VMEM((heads, block, HEAD), f32),
        ],
        compiler_params=pltpu.CompilerParams(vmem_limit_bytes=VMEM_LIMIT),
        cost_estimate=pl.CostEstimate(flops=10**10, bytes_accessed=12 * 10**6, transcendentals=10**7),
        name="attend_back",
    )(seq, qkv, qkvt, dot, ot, lse)


def shard_of(r, c):
    return lax.rem(r + 2 * c, 4)


def middle_kernel(
    n_dp, oin_ref, xf_ref, dys_ref, w_ref, res_ref, dh1_ref, dout_ref, *rest
):
    g_refs, rest = rest[:n_dp], rest[n_dp:]
    middle_body(n_dp, oin_ref, xf_ref, dys_ref, w_ref, res_ref, dh1_ref, dout_ref, g_refs, *rest)


def middle_body(
    n_dp, oin_ref, xf_ref, dys_ref, w_ref, res_ref, dh1_ref, dout_ref, g_refs,
    dyin, dyb, ot_ref, dot_ref, wup, wdn, wo, vec, ub, hid, slope, gbuf, gin, facc, yacc,
    so, ro, sg, rg, lsem, wss, wrs, sgb, rgb, sgt, rgt, gsem, sd, rd, sm, rm,
):
    d, r, c = me()
    half = lax.rem(r, 2)
    wide = xf_ref.shape[3]
    width = 2 * wide
    tok = dyb.shape[0]
    hrows = oin_ref.shape[0]
    core = (d, r, 1 - c)
    peers = [(d, flip(r), c), (d, flip(r), 1 - c), core]
    ring = [(lax.rem(d + k, n_dp), r, c) for k in range(1, n_dp)]
    greet(peers + ring)
    base = r - half
    shard = shard_of(r, c)
    o_cp = []
    for i, dev in enumerate(peers):
        q = (dev[1] - base) * 2 + dev[2]
        src = oin_ref.at[:, pl.ds(pl.multiple_of(q * tok, tok), tok)]
        cp = remote(src, ot_ref.at[shard], so.at[i], ro.at[i], dev)
        cp.start()
        o_cp.append(cp)
    myq = pl.ds(pl.multiple_of((half * 2 + c) * tok, tok), tok)
    ot_ref[shard] = oin_ref[:, myq]

    piece = dys_ref.shape[1]
    here = pl.ds(pl.multiple_of(d * piece, piece), piece)
    d_cp = []
    for k, dev in enumerate(ring):
        cp = remote(dys_ref.at[dev[0]], dyin.at[here, :], sd.at[k], rd.at[k], dev)
        cp.start()
        d_cp.append(cp)
    dyin[here, :] = dys_ref[d]

    loads = [[], [], []]
    mycols = pl.ds(pl.multiple_of(c * wide, 128), wide)
    for j in range(4):
        js = slice(j * hrows, (j + 1) * hrows)
        loads[0].append((w_ref.at[j, OUT:VEC], wo.at[js, mycols]))
        loads[0].append((w_ref.at[j, VEC : VEC + 16], ub.at[j, c]))
        for h in range(2):
            hs = slice(h * wide, (h + 1) * wide)
            loads[1].append((w_ref.at[j, hs], wup.at[j, mycols, hs]))
        loads[2].append((w_ref.at[j, DOWN:OUT], wdn.at[j, :, mycols]))
    w_cps = []
    for i, group in enumerate(loads):
        cps = []
        for k, (src, dst) in enumerate(group):
            a = pltpu.make_async_copy(src, dst, lsem.at[i, k])
            a.start()
            b = remote(src, dst, wss.at[i, k], wrs.at[i, k], core)
            b.start()
            cps += [a, b]
        w_cps.append(cps)

    def settle(i):
        for cp in w_cps[i]:
            cp.wait()

    for cp in o_cp:
        cp.wait_recv()
    for cp in d_cp:
        cp.wait_recv()
    theirs = pl.ds(pl.multiple_of((1 - c) * tok, tok), tok)
    dy_cp = remote(dyin.at[theirs, :], dyb, sm, rm, core)
    dy_cp.start()
    mine = pl.ds(pl.multiple_of(c * tok, tok), tok)
    x = jnp.concatenate([xf_ref[half, 0, mine, :], xf_ref[half, 1, mine, :]], axis=1).astype(f32)
    settle(0)
    vec[...] = jnp.concatenate([ub[0, 0], ub[0, 1]], axis=1)
    ob, g1, s1, db, g2, s2 = [vec[i : i + 1, :].astype(f32) for i in range(6)]
    o = ot_ref[...].reshape(width, tok).T
    h1 = x + (nn(o, wo[...]) + ob)
    mu = jnp.mean(h1, axis=1, keepdims=True)
    r1 = lax.rsqrt(jnp.mean(h1 * h1, axis=1, keepdims=True) - mu * mu + EPS)
    n1 = (h1 - mu) * r1
    y1 = (n1 * g1 + s1).astype(bf16)
    settle(1)
    settle(2)
    facc[...] = jnp.zeros_like(facc)

    def ahead(j, carry):
        bias = jnp.concatenate([ub[j, 0, 6:7, :], ub[j, 0, 7:8, :]], axis=1).astype(f32)
        u = nn(y1, wup[j]) + bias
        cdf = 0.5 * (1.0 + lax.erf(u * INV_ROOT_TWO))
        hj = (u * cdf).astype(bf16)
        hid[j] = hj
        slope[j] = cdf + u * jnp.exp(-0.5 * u * u) * INV_ROOT_TAU
        facc[...] += nn(hj, wdn[j])
        return carry

    lax.fori_loop(0, 4, ahead, 0)
    h2 = y1.astype(f32) + (facc[...] + db)
    mu2 = jnp.mean(h2, axis=1, keepdims=True)
    r2 = lax.rsqrt(jnp.mean(h2 * h2, axis=1, keepdims=True) - mu2 * mu2 + EPS)
    n2 = (h2 - mu2) * r2
    res_ref[...] = (n2 * g2 + s2).astype(bf16)
    dy_cp.wait_recv()
    own, other = dyin[mine, :], dyb[...]
    left = jnp.where(c == 0, own, other)
    right = jnp.where(c == 0, other, own)
    dy = jnp.concatenate([left, right], axis=1).astype(f32)
    e2 = dy * g2
    dh2 = r2 * (e2 - jnp.mean(e2, axis=1, keepdims=True) - n2 * jnp.mean(e2 * n2, axis=1, keepdims=True))
    g2g = jnp.sum(dy * n2, axis=0, keepdims=True)
    s2g = jnp.sum(dy, axis=0, keepdims=True)
    df = dh2.astype(bf16)
    dbg = jnp.sum(df.astype(f32), axis=0, keepdims=True)
    yacc[...] = dh2
    y1t = y1.T

    def big_cp(j):
        return remote(gbuf.at[j, 1 - c, 0:OUT], gin.at[j, 0:OUT], sgb.at[j], rgb.at[j], core)

    def back(j, carry):
        du = (nt(df, wdn[j]) * slope[j]).astype(bf16)
        ubg = jnp.sum(du.astype(f32), axis=0, keepdims=True)
        gd = tn(hid[j], df).astype(bf16)
        gu = nn(y1t, du).astype(bf16)
        for cc in range(2):
            cs = slice(cc * wide, (cc + 1) * wide)
            for h in range(2):
                gbuf[j, cc, h * wide : (h + 1) * wide, :] = gu[cs, h * wide : (h + 1) * wide]
            gbuf[j, cc, DOWN:OUT, :] = gd[:, cs]
        for cc in range(2):
            gbuf[j, cc, VEC : VEC + 16, :] = jnp.concatenate(
                [jnp.broadcast_to(ubg[:, :wide], (8, wide)), jnp.broadcast_to(ubg[:, wide:], (8, wide))], axis=0
            ).astype(bf16)
        big_cp(j).start()
        yacc[...] += nt(du, wup[j])
        return carry

    lax.fori_loop(0, 4, back, 0)
    dy1 = yacc[...]
    e1 = dy1 * g1
    dh1 = r1 * (e1 - jnp.mean(e1, axis=1, keepdims=True) - n1 * jnp.mean(e1 * n1, axis=1, keepdims=True))
    dh1_ref[...] = dh1
    g1g = jnp.sum(dy1 * n1, axis=0, keepdims=True)
    s1g = jnp.sum(dy1, axis=0, keepdims=True)
    da = dh1.astype(bf16)
    obg = jnp.sum(da.astype(f32), axis=0, keepdims=True)
    dot_ref[...] = nt(da, wo[...]).T.astype(bf16).reshape(dot_ref.shape)
    g_cp = []
    for i, dev in enumerate(peers):
        cp = remote(dot_ref.at[shard_of(dev[1], dev[2])], dout_ref.at[:, myq], sg.at[i], rg.at[i], dev)
        cp.start()
        g_cp.append(cp)
    dout_ref[:, myq] = dot_ref[shard]
    go = nn(ot_ref[...].reshape(width, tok), da).astype(bf16)
    pad = gbuf.shape[2] - VEC
    row = lax.broadcasted_iota(jnp.int32, (pad, wide), 0)
    t_cp = []
    for j in range(4):
        for cc in range(2):
            cs = slice(cc * wide, (cc + 1) * wide)
            gbuf[j, cc, OUT:VEC, :] = go[j * hrows : (j + 1) * hrows, cs]
            tail = jnp.zeros((pad, wide), f32)
            for i, v in enumerate((obg, g1g, s1g, dbg, g2g, s2g)):
                tail = jnp.where(row == i, v[:, cs], tail)
            tail = jnp.where(row == 6, gbuf[j, cc, VEC : VEC + 16, :][0:1].astype(f32), tail)
            tail = jnp.where(row == 7, gbuf[j, cc, VEC : VEC + 16, :][8:9].astype(f32), tail)
            gbuf[j, cc, VEC:, :] = tail.astype(bf16)
        cp = remote(gbuf.at[j, 1 - c, OUT:], gin.at[j, OUT:], sgt.at[j], rgt.at[j], core)
        cp.start()
        t_cp.append(cp)
    rows_q = gbuf.shape[2] // n_dp
    outs = []
    for j in range(4):
        big_cp(j).wait()
        t_cp[j].wait()
        gin[j] = (gin[j].astype(f32) + gbuf[j, c].astype(f32)).astype(bf16)
        for k in range(n_dp):
            dest = lax.rem(d + k, n_dp)
            span = pl.ds(pl.multiple_of(dest * rows_q, rows_q), rows_q)
            cp = pltpu.make_async_copy(gin.at[j, span], g_refs[k].at[j], gsem.at[j, k])
            cp.start()
            outs.append(cp)
    for cp in o_cp + d_cp + [dy_cp]:
        cp.wait_send()
    for cp in g_cp + outs:
        cp.wait()


def middle_call(n_dp, oin, xf, dys, w, g_rows):
    tok, wide = xf.shape[2] // 2, xf.shape[3]
    width = 2 * wide
    hrows = oin.shape[0]
    return pl.pallas_call(
        functools.partial(middle_kernel, n_dp),
        out_shape=(
            sds((tok, width), bf16),
            sds((tok, width), f32),
            sds((hrows, 4 * tok), bf16),
        )
        + (sds((4, g_rows // n_dp, wide), bf16),) * n_dp,
        in_specs=[VM] * 3 + [ANY],
        out_specs=(VM, VM, VM) + (ANY,) * n_dp,
        scratch_shapes=[
            pltpu.VMEM((2 * tok, wide), bf16),
            pltpu.VMEM((tok, wide), bf16),
            pltpu.VMEM((4, hrows, tok), bf16),
            pltpu.VMEM((4, hrows, tok), bf16),
            pltpu.VMEM((4, width, width), bf16),
            pltpu.VMEM((4, width, width), bf16),
            pltpu.VMEM((width, width), bf16),
            pltpu.VMEM((16, width), bf16),
            pltpu.VMEM((4, 2, 16, wide), bf16),
            pltpu.VMEM((4, tok, width), bf16),
            pltpu.VMEM((4, tok, width), f32),
            pltpu.VMEM((4, 2, g_rows, wide), bf16),
            pltpu.VMEM((4, g_rows, wide), bf16),
            pltpu.VMEM((tok, width), f32),
            pltpu.VMEM((tok, width), f32),
            DMA((3,)), DMA((3,)), DMA((3,)), DMA((3,)),
            DMA((3, 8)), DMA((3, 8)), DMA((3, 8)),
            DMA((4,)), DMA((4,)), DMA((4,)), DMA((4,)),
            DMA((4, n_dp)), DMA((n_dp,)), DMA((n_dp,)), DMA, DMA,
        ],
        compiler_params=pltpu.CompilerParams(
            collective_id=2, has_side_effects=True, vmem_limit_bytes=VMEM_LIMIT
        ),
        cost_estimate=pl.CostEstimate(flops=16 * 10**9, bytes_accessed=30 * 10**6, transcendentals=4 * 10**6),
        name="middle",
    )(oin, xf, dys, w)


def return_kernel(
    n_dp, dqkv_ref, dqkvt_ref, wq_ref, xf_ref, dh1_ref, res_ref, deal_ref, *rest
):
    parts, rest = rest[:n_dp], rest[n_dp:]
    return_body(n_dp, dqkv_ref, dqkvt_ref, wq_ref, xf_ref, dh1_ref, res_ref, deal_ref, parts, *rest)


def return_body(
    n_dp, dqkv_ref, dqkvt_ref, wq_ref, xf_ref, dh1_ref, res_ref, deal_ref, parts,
    out_ref, ig_ref, gout_ref, gall_ref,
    rsum, zin, rfin, s_r, r_r, s_t, r_t,
    back_a, back_b, fin, tocore, fromcore, toz, fromz, gq_ref, gqin, gsum, xq, gfin,
    s_a, r_a, s_b, r_b, s_c, r_c, s_z, r_z, s_q, r_q, s_x, r_x, s_g, r_g,
):
    d, r, c = me()
    half = lax.rem(r, 2)
    tok = dh1_ref.shape[0]
    wide = xf_ref.shape[3]
    width = 2 * wide
    tokens = 2 * tok
    piece = tokens // n_dp
    n_half = n_dp // 2
    core = (d, r, 1 - c)
    zdev = (d, flip(r), c)
    peers = [(lax.rem(d + k, n_dp), r, cc) for k in range(1, n_dp) for cc in (0, 1)]
    far_row = lax.rem(r + 2, 4)
    rows_dev = [(d, lax.rem(r + k, 4), c) for k in (1, 2, 3)]
    greet(peers + rows_dev + [core, (d, far_row, 1 - c)])

    total = parts[0][...].astype(f32)
    for k in range(1, n_dp):
        total = total + parts[k][...].astype(f32)
    rsum[...] = total.astype(bf16)
    row_cp = []
    for k, dev in enumerate(rows_dev):
        cp = remote(rsum.at[dev[1]], zin.at[k], s_r.at[k], r_r.at[k], dev)
        cp.start()
        row_cp.append(cp)

    def grp(g):
        return pl.ds(pl.multiple_of(g * piece, piece), piece)

    def send_back(src, back, ss, rs):
        for i in range(n_half):
            s = c * n_half + i
            for cc in range(2):
                ref = src.at[cc, i * piece : (i + 1) * piece, :]
                cp = remote(ref, back.at[grp(d), :], ss.at[i, cc], rs.at[d], (s, r, cc))
                local = (s == d) & (c == cc)

                @pl.when(jnp.logical_not(local))
                def _():
                    cp.start()

                @pl.when(local)
                def _():
                    back[grp(d), :] = src[cc, i * piece : (i + 1) * piece, :]

    def sent_back(src, back, ss, rs):
        for i in range(n_half):
            s = c * n_half + i
            for cc in range(2):
                ref = src.at[cc, i * piece : (i + 1) * piece, :]

                @pl.when(jnp.logical_not((s == d) & (c == cc)))
                def _():
                    remote(ref, back.at[grp(d), :], ss.at[i, cc], rs.at[d], (s, r, cc)).wait_send()

    def got_back(src, back, ss, rs):
        holder = lax.div(d, n_half)
        for g in range(n_dp):

            @pl.when(jnp.logical_not((d == g) & (holder == c)))
            def _():
                remote(
                    src.at[0, 0:piece, :], back.at[grp(g), :], ss.at[0, 0], rs.at[g], (d, r, 1 - c)
                ).wait_recv()

    fin[0, 0] = res_ref[:, :wide]
    fin[0, 1] = res_ref[:, wide:]
    send_back(fin.at[0], back_a, s_a, r_a)

    w0 = wq_ref[0]
    w1 = wq_ref[1]

    def part(h, cc):
        q = h * 2 + cc
        rows = dqkv_ref[pl.ds(pl.multiple_of(q * tok, tok), tok), :]
        return jnp.concatenate([nn(rows, w0), nn(rows, w1)], axis=1)

    tocore[0] = part(1 - half, 1 - c).astype(bf16)
    cp_far = remote(tocore.at[0], fromcore.at[0], s_c.at[0], r_c.at[0], core)
    cp_far.start()
    tocore[1] = part(half, 1 - c).astype(bf16)
    cp_near = remote(tocore.at[1], fromcore.at[1], s_c.at[1], r_c.at[1], core)
    cp_near.start()
    far = part(1 - half, c)
    cp_far.wait_recv()
    toz[...] = (far + fromcore[0].astype(f32)).astype(bf16)
    cp_z = remote(toz, fromz, s_z, r_z, zdev)
    cp_z.start()
    total = part(half, c) + dh1_ref[...]
    n_cols = dqkvt_ref.shape[0]
    length = dqkvt_ref.shape[1]
    for f in range(2):
        g = nn(dqkvt_ref[:, : length // 2], xf_ref[0, f]) + nn(dqkvt_ref[:, length // 2 :], xf_ref[1, f])
        gq_ref[f, :n_cols, :] = g.astype(bf16)
    third = n_cols // 3
    sums = jnp.sum(dqkv_ref[...].astype(f32), axis=0, keepdims=True)
    bias = jnp.concatenate([sums[:, :third], sums[:, 2 * third :]], axis=1)
    pad = gq_ref.shape[1] - n_cols
    row = lax.broadcasted_iota(jnp.int32, (pad, wide), 0)
    tail = jnp.where(row == 0, bias, 0.0).astype(bf16)
    for f in range(2):
        gq_ref[f, n_cols:, :] = tail
    rq = gq_ref.shape[1] // n_dp

    def quarter(s):
        return pl.ds(pl.multiple_of(s * rq, rq), rq)

    q_cp = []
    for k in range(1, n_dp):
        dest = lax.rem(d + k, n_dp)
        cp = remote(gq_ref.at[:, quarter(dest), :], gqin.at[k], s_q.at[k], r_q.at[k], (dest, r, c))
        cp.start()
        q_cp.append(cp)
    place = (lax.broadcasted_iota(jnp.int32, (tokens, tokens), 0) == deal_ref[...]).astype(bf16)
    got_back(fin.at[0], back_a, s_a, r_a)
    out_ref[...] = nn(place, back_a[...]).astype(bf16)
    acc = gq_ref[:, quarter(d), :].astype(f32)
    for k in range(1, n_dp):
        q_cp[k - 1].wait_recv()
        acc = acc + gqin[k].astype(f32)
    gsum[...] = acc.astype(bf16)
    to_one = remote(gsum.at[1], xq.at[1], s_x.at[1], r_x.at[1], (d, r, 1))
    far_0 = remote(gsum.at[0], xq.at[0], s_x.at[0], r_x.at[0], (d, far_row, 0))
    far_1 = remote(gsum.at[1], xq.at[0], s_x.at[1], r_x.at[0], (d, far_row, 1))

    @pl.when(c == 0)
    def _():
        to_one.start()

    @pl.when(c == 1)
    def _():
        far_0.start()
        far_1.start()

    held = rsum[r].astype(f32)
    for k in range(3):
        row_cp[k].wait_recv()
        held = held + zin[k].astype(f32)
    rfin[...] = held.astype(bf16)
    n_keep = rfin.shape[0]
    keep = pl.ds(pl.multiple_of(d * n_keep, n_keep), n_keep)
    gall_ref[keep, :] = rfin[...]
    t_cp = []
    for k in range(1, n_dp):
        dest = lax.rem(d + k, n_dp)
        cp = remote(rfin, gall_ref.at[keep, :], s_t.at[k], r_t.at[k], (dest, r, c))
        cp.start()
        t_cp.append(cp)

    cp_near.wait_recv()
    total = total + fromcore[1].astype(f32)
    cp_z.wait_recv()
    total = (total + fromz[...].astype(f32)).astype(bf16)
    fin[1, 0] = total[:, :wide]
    fin[1, 1] = total[:, wide:]
    send_back(fin.at[1], back_b, s_b, r_b)
    far_0.wait_recv()

    @pl.when(c == 0)
    def _():
        gfin[...] = (gsum[0].astype(f32) + xq[0].astype(f32)).astype(bf16)

    @pl.when(c == 1)
    def _():
        to_one.wait_recv()
        gfin[...] = (xq[0].astype(f32) + xq[1].astype(f32)).astype(bf16)

    g_cp = []
    for k in range(1, n_dp):
        dest = lax.rem(d + k, n_dp)
        cp = remote(gfin, gout_ref.at[quarter(d), :], s_g.at[k], r_g.at[k], (dest, r, c))
        cp.start()
        g_cp.append(cp)
    gout_ref[quarter(d), :] = gfin[...]
    got_back(fin.at[1], back_b, s_b, r_b)
    ig_ref[...] = nn(place, back_b[...]).astype(bf16)
    sent_back(fin.at[0], back_a, s_a, r_a)
    sent_back(fin.at[1], back_b, s_b, r_b)
    cp_far.wait_send()
    cp_near.wait_send()
    cp_z.wait_send()
    for cp in q_cp:
        cp.wait_send()
    for cp in row_cp:
        cp.wait_send()
    for cp in g_cp + t_cp:
        cp.wait()

    @pl.when(c == 0)
    def _():
        to_one.wait_send()

    @pl.when(c == 1)
    def _():
        far_0.wait_send()
        far_1.wait_send()


def return_call(n_dp, dqkv, dqkvt, wq, xf, dh1, res, deal_row, parts, gq_rows):
    share = parts[0].shape[1]
    tok, width = dh1.shape
    wide = width // 2
    tokens = 2 * tok
    n_half = n_dp // 2
    return pl.pallas_call(
        functools.partial(return_kernel, n_dp),
        out_shape=(
            sds((tokens, wide), bf16),
            sds((tokens, wide), bf16),
            sds((gq_rows, wide), bf16),
            sds((n_dp * share, wide), bf16),
        ),
        in_specs=[VM] * (7 + n_dp),
        out_specs=(VM,) * 4,
        scratch_shapes=[
            pltpu.VMEM((4, share, wide), bf16),
            pltpu.VMEM((3, share, wide), bf16),
            pltpu.VMEM((share, wide), bf16),
            DMA((3,)), DMA((3,)), DMA((n_dp,)), DMA((n_dp,)),
            pltpu.VMEM((tokens, wide), bf16),
            pltpu.VMEM((tokens, wide), bf16),
            pltpu.VMEM((2, 2, tok, wide), bf16),
            pltpu.VMEM((2, tok, width), bf16),
            pltpu.VMEM((2, tok, width), bf16),
            pltpu.VMEM((tok, width), bf16),
            pltpu.VMEM((tok, width), bf16),
            pltpu.VMEM((2, gq_rows, wide), bf16),
            pltpu.VMEM((n_dp, 2, gq_rows // n_dp, wide), bf16),
            pltpu.VMEM((2, gq_rows // n_dp, wide), bf16),
            pltpu.VMEM((2, gq_rows // n_dp, wide), bf16),
            pltpu.VMEM((gq_rows // n_dp, wide), bf16),
            DMA((n_half, 2)), DMA((n_dp,)),
            DMA((n_half, 2)), DMA((n_dp,)),
            DMA((2,)), DMA((2,)), DMA, DMA,
            DMA((n_dp,)), DMA((n_dp,)), DMA((2,)), DMA((2,)), DMA((n_dp,)), DMA((n_dp,)),
        ],
        compiler_params=pltpu.CompilerParams(
            collective_id=4, has_side_effects=True, vmem_limit_bytes=VMEM_LIMIT
        ),
        name="return",
    )(dqkv, dqkvt, wq, xf, dh1, res, deal_row, *parts)


def round_up(v, m):
    return (v + m - 1) // m * m


def on_device(
    n_dp, inputs, out_grad, deal, seq_lengths, key_trim, query_weight, query_bias, key_weight,
    value_weight, value_bias, out_weight, out_bias, first_gain, first_shift, up_weight, up_bias,
    down_weight, down_bias, second_gain, second_shift,
):
    wide = inputs.shape[1]
    n_seq = seq_lengths.shape[1]
    step = 16 * n_dp
    third = query_weight.shape[1]
    rows_w = round_up(VEC + 16, step)
    xf, dys, qkv, qkvt, wq, seq, wg = deal_call(
        n_dp, rows_w,
        (
            inputs, out_grad, deal, query_weight.T, key_weight.T, value_weight.T, query_bias, value_bias, up_weight,
            down_weight, out_weight, out_bias, first_gain, first_shift, down_bias, second_gain, second_shift, up_bias,
            seq_lengths, key_trim,
        ),
    )
    ot, lse = attend_call(n_seq, seq, qkv, qkvt)
    res, dh1, dot, *grads = middle_call(n_dp, ot, xf, dys, wg, rows_w)
    parts = [grads[0]]
    for k in range(1, n_dp):
        parts.append(lax.ppermute(grads[k], "dp", [(i, (i + k) % n_dp) for i in range(n_dp)]))
    dqkv, dqkvt = attend_back_call(n_seq, seq, qkv, qkvt, dot, ot, lse)
    gq_rows = round_up(3 * third + 16, step)
    output, input_grad, mine_q, mine = return_call(
        n_dp, dqkv, dqkvt, wq, xf, dh1, res, deal, parts, gq_rows
    )

    g = mine.astype(f32)
    up_grad = jnp.concatenate([g[:wide], g[wide : 2 * wide]], axis=1)
    down_grad = g[DOWN:OUT]
    out_grad_w = g[OUT:VEC]
    vec = g[VEC : VEC + 8]
    gqf = mine_q.astype(f32)
    query_grad = gqf[:third].T
    key_grad = gqf[third : 2 * third].T
    value_grad = gqf[2 * third : 3 * third].T
    brow = gqf[3 * third]
    return (
        output, input_grad, query_grad, brow[:third], key_grad, value_grad, brow[third:], out_grad_w,
        vec[0], vec[1], vec[2], up_grad, vec[6:8].reshape(-1), down_grad, vec[3], vec[4], vec[5],
    )


def solution(mesh):
    n_dp = mesh.shape["dp"]
    tok = P(("dp", "row"), "col")
    one = P("col")
    row = P("row")
    a = P("col", "row")
    b = P("row", "col")
    seqs = P(("dp", "col"), None)
    in_specs = (
        tok, tok, P(("dp", "row"), None), seqs, seqs, a, row, a, a, row, b, one, one, one, a, row, b, one, one, one,
    )
    out_specs = (tok, tok, a, row, a, a, row, b, one, one, one, a, row, b, one, one, one)
    return jax.shard_map(
        functools.partial(on_device, n_dp), mesh=mesh, in_specs=in_specs, out_specs=out_specs, check_vma=False
    )
```

```python
import functools

import jax
import jax.numpy as jnp
from jax import lax
from jax.experimental import pallas as pl
from jax.experimental.pallas import tpu as pltpu
from jax.sharding import PartitionSpec as P

MESH = pl.DeviceIdType.MESH
f32 = jnp.float32
bf16 = jnp.bfloat16

HEAD = 64
EPS = 1e-05
FAR = -1e30
INV_ROOT_TWO = 0.7071067811865476
INV_ROOT_TAU = 0.3989422804014327
VMEM_LIMIT = 62 * 1024 * 1024
DOWN, OUT, VEC = 768, 1536, 1728

VM = pl.BlockSpec(memory_space=pltpu.VMEM)
SM = pl.BlockSpec(memory_space=pltpu.SMEM)
ANY = pl.BlockSpec(memory_space=pl.ANY)
DMA = pltpu.SemaphoreType.DMA


def nn(a, b):
    return lax.dot_general(a, b, (((1,), (0,)), ((), ())), preferred_element_type=f32)


def nt(a, b):
    return lax.dot_general(a, b, (((1,), (1,)), ((), ())), preferred_element_type=f32)


def tn(a, b):
    return lax.dot_general(a, b, (((0,), (0,)), ((), ())), preferred_element_type=f32)


def sds(shape, dtype):
    return jax.ShapeDtypeStruct(shape, dtype)


def me():
    return lax.axis_index("dp"), lax.axis_index("row"), lax.axis_index("col")


def flip(v):
    return v + 1 - 2 * lax.rem(v, 2)


def remote(src, dst, ssem, rsem, dev):
    return pltpu.make_async_remote_copy(
        src_ref=src, dst_ref=dst, send_sem=ssem, recv_sem=rsem, device_id=dev, device_id_type=MESH
    )


def greet(devs):
    barrier = pltpu.get_barrier_semaphore()
    for dev in devs:
        pl.semaphore_signal(barrier, inc=1, device_id=dev, device_id_type=MESH)
    pl.semaphore_wait(barrier, len(devs))


def send_back(n_dp, src, back, ss, rs):
    d, r, c = me()
    n_half = n_dp // 2
    piece = back.shape[0] // n_dp
    here = pl.ds(pl.multiple_of(d * piece, piece), piece)
    for i in range(n_half):
        s = c * n_half + i
        for cc in range(2):
            ref = src.at[cc, i * piece : (i + 1) * piece, :]
            cp = remote(ref, back.at[here, :], ss.at[i, cc], rs.at[d], (s, r, cc))
            local = (s == d) & (c == cc)

            @pl.when(jnp.logical_not(local))
            def _():
                cp.start()

            @pl.when(local)
            def _():
                back[here, :] = src[cc, i * piece : (i + 1) * piece, :]


def sent_back(n_dp, src, back, ss, rs):
    d, r, c = me()
    n_half = n_dp // 2
    piece = back.shape[0] // n_dp
    for i in range(n_half):
        s = c * n_half + i
        for cc in range(2):
            ref = src.at[cc, i * piece : (i + 1) * piece, :]

            @pl.when(jnp.logical_not((s == d) & (c == cc)))
            def _():
                remote(ref, back.at[0:piece, :], ss.at[i, cc], rs.at[0], (s, r, cc)).wait_send()


def got_back(n_dp, src, back, ss, rs):
    d, r, c = me()
    holder = lax.div(d, n_dp // 2)
    piece = back.shape[0] // n_dp
    for g in range(n_dp):

        @pl.when(jnp.logical_not((d == g) & (holder == c)))
        def _():
            remote(
                src.at[0, 0:piece, :], back.at[g * piece : (g + 1) * piece, :], ss.at[0, 0], rs.at[g], (d, r, 1 - c)
            ).wait_recv()


def deal_kernel(
    n_dp, rows_w, x_ref, dy_ref, deal_ref, qw_ref, kw_ref, vw_ref, qb_ref, vb_ref, up_ref, dn_ref, ow_ref,
    ob_ref, g1_ref, s1_ref, db_ref, g2_ref, s2_ref, ub_ref, len_ref, trim_ref,
    xf_out, dys_out, qkv_out, qkvt_out, wq_out, seqo_ref, wg_ref,
    xf_ref, dys_ref, qkv_ref, qkvt_ref, wq_ref, so,
    xs, seq, seqrx, w, bias, biases, blob, col,
    sx, rx, sc, rc, sz, rz, sc2, rc2, sw, rw, sb, rb, sm, rm, ss, rs, sf, rf, sl,
):
    d, r, c = me()
    half = lax.rem(r, 2)
    tokens, wide = x_ref.shape
    piece = tokens // n_dp
    third = qw_ref.shape[0]
    core = (d, r, 1 - c)
    zdev = (d, flip(r), c)
    far_row = lax.rem(r + 2, 4)
    ring = [(lax.rem(d + k, n_dp), r, c) for k in range(1, n_dp)]
    rows_dev = [(d, lax.rem(r + k, 4), c) for k in (1, 2, 3)]
    greet(ring + rows_dev + [core, (d, far_row, 1 - c)])

    blob[0:wide, :] = up_ref[:, :wide]
    blob[wide : 2 * wide, :] = up_ref[:, wide:]
    blob[DOWN:OUT, :] = dn_ref[...]
    blob[OUT:VEC, :] = ow_ref[...]
    vecs = [v[...].reshape(1, wide) for v in (ob_ref, g1_ref, s1_ref, db_ref, g2_ref, s2_ref)]
    vecs += [ub_ref[0:wide].reshape(1, wide), ub_ref[wide : 2 * wide].reshape(1, wide)]
    row = lax.broadcasted_iota(jnp.int32, (16, wide), 0)
    tail = jnp.zeros((16, wide), f32)
    for i, v in enumerate(vecs):
        tail = jnp.where(row == i, v.astype(f32), tail)
    blob[VEC : VEC + 16, :] = tail.astype(bf16)
    blob[VEC + 16 :, :] = jnp.zeros((rows_w - VEC - 16, wide), bf16)
    share = rows_w // n_dp
    my_share = pl.ds(pl.multiple_of(d * share, share), share)
    share_cp = [
        remote(blob.at[my_share, :], wg_ref.at[r, my_share, :], ss.at[k], rs.at[k], dev)
        for k, dev in enumerate(rows_dev)
    ]
    for cp in share_cp:
        cp.start()
    local_w = pltpu.make_async_copy(blob, wg_ref.at[r], sl)
    local_w.start()

    def rows(s):
        return pl.ds(pl.multiple_of(s * piece, piece), piece)

    col[...] = jnp.broadcast_to(deal_ref[...], (8, tokens)).T
    lane = lax.broadcasted_iota(jnp.int32, (piece, tokens), 1)
    sends = []
    for k in list(range(1, n_dp)) + [0]:
        dest = lax.rem(d + k, n_dp)
        pick = (col[rows(dest), 0:1] == lane).astype(bf16)
        px = nn(pick, x_ref[...]).astype(bf16)
        if k:
            xs[k] = px
            cp = remote(xs.at[k], xf_ref.at[half, c, rows(d), :], sx.at[k], rx.at[k], (dest, r, c))
            cp.start()
            sends.append(cp)
        else:
            xf_ref[half, c, rows(d), :] = px

    w[:third, :] = qw_ref[...]
    w[third : 2 * third, :] = kw_ref[...]
    w[2 * third :, :] = vw_ref[...]
    w_far = remote(w, wq_ref.at[c], sw.at[0], rw.at[c], (d, far_row, 1))
    w_far.start()
    w_near = remote(w, wq_ref.at[1], sw.at[1], rw.at[1], (d, r, 0))
    flat = jnp.concatenate(
        [qb_ref[...].reshape(1, third), jnp.zeros((1, third), bf16), vb_ref[...].reshape(1, third)], axis=1
    )
    bias[...] = jnp.broadcast_to(flat.astype(f32), (8, 3 * third))
    b_far = remote(bias, biases.at[1], sb.at[0], rb.at[0], (d, far_row, 1))

    @pl.when(c == 0)
    def _():
        wq_ref[0] = w[...]
        b_far.start()

    @pl.when(c == 1)
    def _():
        w_near.start()

    biases[0] = bias[...]
    seq[...] = jnp.zeros_like(seq)
    seq[0:1, 0 : len_ref.shape[1]] = len_ref[...]
    seq[1:2, 0 : len_ref.shape[1]] = trim_ref[...]
    seq_cp = remote(seq, seqrx, sm.at[0], rm.at[0], core)
    seq_cp.start()

    core_cp, z_cp, core2_cp = [], [], []
    for k in range(n_dp):
        s = lax.rem(d - k + n_dp, n_dp)
        ref = xf_ref.at[half, c, rows(s), :]
        if k:
            sends[k - 1].wait_recv()
        a = remote(ref, ref, sz.at[k], rz.at[k], zdev)
        a.start()
        b = remote(ref, ref, sc.at[k], rc.at[k], core)
        b.start()
        z_cp.append(a)
        core_cp.append(b)

    pass_cp = []
    for k in range(3):
        share_cp[k].wait_recv()
        ref = wg_ref.at[lax.rem(r - k + 3, 4), my_share, :]
        for i, dev in enumerate(ring):
            cp = remote(ref, ref, sf.at[k, i], rf.at[k, i], dev)
            cp.start()
            pass_cp.append(cp)
        if k == 0:
            for dest in range(n_dp):
                pick = (col[dest * piece : (dest + 1) * piece, 0:1] == lane).astype(bf16)
                dys_ref[dest] = nn(pick, dy_ref[...]).astype(bf16)

    for k in range(n_dp):
        s = lax.rem(d - k + n_dp, n_dp)
        z_cp[k].wait_recv()
        ref = xf_ref.at[1 - half, c, rows(s), :]
        b = remote(ref, ref, sc2.at[k], rc2.at[k], core)
        b.start()
        core2_cp.append(b)

    @pl.when(c == 0)
    def _():
        w_near.wait_recv()
        b_far.wait_send()

    @pl.when(c == 1)
    def _():
        w_near.wait_send()
        b_far.wait_recv()
        remote(w, wq_ref.at[0], sw.at[0], rw.at[0], (d, far_row, 1)).wait_recv()
        remote(w, wq_ref.at[1], sw.at[0], rw.at[1], (d, far_row, 1)).wait_recv()

    w_far.wait_send()
    for k in range(n_dp):
        core_cp[k].wait_recv()
        core2_cp[k].wait_recv()
    stores = [
        pltpu.make_async_copy(xf_ref, xf_out, so.at[0]),
        pltpu.make_async_copy(wq_ref, wq_out, so.at[1]),
        pltpu.make_async_copy(dys_ref, dys_out, so.at[2]),
    ]
    for cp in stores:
        cp.start()
    brow = jnp.where(c == 0, biases[0], biases[1])[0:1, :]

    def project(i, carry):
        h = lax.div(i, 2)
        base = pl.ds(pl.multiple_of(lax.rem(i, 2) * 512, 512), 512)
        y = nt(xf_ref[h, 0, base, :], wq_ref[0]) + nt(xf_ref[h, 1, base, :], wq_ref[1]) + brow
        y = y.astype(bf16)
        out = pl.ds(pl.multiple_of(i * 512, 512), 512)
        qkv_ref[out, :] = y
        qkvt_ref[:, out] = y.T
        return carry

    lax.fori_loop(0, 4, project, 0)
    stores += [pltpu.make_async_copy(qkv_ref, qkv_out, so.at[3]), pltpu.make_async_copy(qkvt_ref, qkvt_out, so.at[4])]
    stores[3].start()
    stores[4].start()
    seq_cp.wait()
    is_mine = lax.div(r, 2) == c
    seqo_ref[...] = jnp.where(is_mine, seq[...], seqrx[...])
    for cp in pass_cp:
        cp.wait()
    for cp in sends + core_cp + z_cp + core2_cp + share_cp:
        cp.wait_send()
    for cp in stores:
        cp.wait()
    local_w.wait()


def deal_call(n_dp, rows_w, args):
    x, qw = args[0], args[3]
    tokens, wide = x.shape
    piece = tokens // n_dp
    cols = 3 * qw.shape[0]
    return pl.pallas_call(
        functools.partial(deal_kernel, n_dp, rows_w),
        out_shape=(
            sds((2, 2, tokens, wide), bf16),
            sds((n_dp, piece, wide), bf16),
            sds((2 * tokens, cols), bf16),
            sds((cols, 2 * tokens), bf16),
            sds((2, cols, wide), bf16),
            sds((8, 128), jnp.int32),
            sds((4, rows_w, wide), bf16),
        ),
        in_specs=[VM] * len(args),
        out_specs=(ANY,) * 5 + (VM, ANY),
        scratch_shapes=[
            pltpu.VMEM((2, 2, tokens, wide), bf16),
            pltpu.VMEM((n_dp, piece, wide), bf16),
            pltpu.VMEM((2 * tokens, cols), bf16),
            pltpu.VMEM((cols, 2 * tokens), bf16),
            pltpu.VMEM((2, cols, wide), bf16),
            DMA((5,)),
            pltpu.VMEM((n_dp, piece, wide), bf16),
            pltpu.VMEM((8, 128), jnp.int32),
            pltpu.VMEM((8, 128), jnp.int32),
            pltpu.VMEM((cols, wide), bf16),
            pltpu.VMEM((8, cols), f32),
            pltpu.VMEM((2, 8, cols), f32),
            pltpu.VMEM((rows_w, wide), bf16),
            pltpu.VMEM((tokens, 8), jnp.int32),
        ]
        + [DMA((n_dp,))] * 8
        + [DMA((2,))] * 6
        + [DMA((3,))] * 2
        + [DMA((3, n_dp - 1))] * 2
        + [DMA],
        compiler_params=pltpu.CompilerParams(
            collective_id=1, has_side_effects=True, vmem_limit_bytes=VMEM_LIMIT
        ),
        name="deal",
    )(*args)


def seq_bounds(seq_ref, n_seq):
    ends, total = [], 0
    for j in range(n_seq):
        total = total + seq_ref[0, j]
        ends.append(total)
    starts = [ends[j] - seq_ref[0, j] for j in range(n_seq)]
    lives = [starts[j] + jnp.maximum(seq_ref[0, j] - seq_ref[1, j], 1) for j in range(n_seq)]
    return starts, ends, lives


def block_range(first, last, starts, ends, block):
    lo, hi = 0, ends[-1]
    for j in range(len(ends)):
        lo = jnp.where((first >= starts[j]) & (first < ends[j]), starts[j], lo)
        hi = jnp.where((last >= starts[j]) & (last < ends[j]), ends[j], hi)
    return lax.div(lo, block), lax.div(hi + block - 1, block)


def key_columns(starts, ends, lives, length, extra):
    pos = lax.broadcasted_iota(jnp.int32, (length, HEAD), 0)
    lane = lax.broadcasted_iota(jnp.int32, (length, HEAD), 1)
    n_seq = len(ends)
    cols = jnp.where(lane < n_seq, FAR, 0.0)
    cols = jnp.where((lane >= n_seq) & (lane < n_seq + extra), -1.0, cols)
    for j in range(n_seq):
        live = (pos >= starts[j]) & (pos < lives[j]) & (lane == j)
        cols = jnp.where(live, 0.0, cols)
    return cols.astype(bf16)


def query_rows(starts, ends, length):
    pos = lax.broadcasted_iota(jnp.int32, (16, length), 1)
    row = lax.broadcasted_iota(jnp.int32, (16, length), 0)
    out = jnp.zeros((16, length), f32)
    for j in range(len(ends)):
        out = jnp.where((row == j) & (pos >= starts[j]) & (pos < ends[j]), 1.0, out)
    return out


def split_three(v):
    hi = v.astype(bf16).astype(f32)
    mid = (v - hi).astype(bf16).astype(f32)
    low = (v - hi - mid).astype(bf16).astype(f32)
    return hi, mid, low


def put_rows(base, values, first):
    row = lax.broadcasted_iota(jnp.int32, base.shape, 0)
    for i, v in enumerate(values):
        base = jnp.where(row == first + i, v, base)
    return base


def attend_kernel(n_seq, block, seq_ref, qkv_ref, qkvt_ref, ot_ref, lse_ref, kaug, qaug, vaug, acc, mx):
    length = qkv_ref.shape[0]
    heads = qkv_ref.shape[1] // (3 * HEAD)
    width = heads * HEAD
    span = 2 * block
    starts, ends, lives = seq_bounds(seq_ref, n_seq)
    kcols = key_columns(starts, ends, lives, length, 3)
    qrows = query_rows(starts, ends, length)
    ones = (lax.broadcasted_iota(jnp.int32, (16, length), 0) == 0).astype(f32).astype(bf16)
    lane = lax.broadcasted_iota(jnp.int32, (block, 2 * HEAD), 1)
    dead = jnp.where((lane >= HEAD) & (lane < HEAD + n_seq), FAR, 0.0).astype(bf16)
    for h in range(heads):
        kaug[h, :length, :HEAD] = qkv_ref[:, width + h * HEAD : width + (h + 1) * HEAD]
        kaug[h, :length, HEAD:] = kcols
        kaug[h, length:, :] = dead
        qaug[h, :HEAD, :] = qkvt_ref[h * HEAD : (h + 1) * HEAD, :] * 0.125
        qaug[h, HEAD : HEAD + 16, :] = qrows.astype(bf16)
        qaug[h, HEAD + 16 :, :] = jnp.zeros((HEAD - 16, length), bf16)
        vaug[h, :HEAD, :length] = qkvt_ref[2 * width + h * HEAD : 2 * width + (h + 1) * HEAD, :]
        vaug[h, HEAD:, :length] = ones
        vaug[h, :, length:] = jnp.zeros((HEAD + 16, block), bf16)
    lse_ref[...] = jnp.zeros_like(lse_ref)

    def q_step(qb, carry):
        qs = pl.ds(pl.multiple_of(qb * block, block), block)
        lo, hi = block_range(qb * block, qb * block + block - 1, starts, ends, block)
        count = lax.div(hi - lo + 1, 2)
        for h in range(heads):
            acc[h] = jnp.zeros((HEAD + 16, block), f32)
            mx[h] = jnp.full((8, block), 2 * FAR, f32)

        def max_step(i, inner):
            ks = pl.ds(pl.multiple_of((lo + 2 * i) * block, block), span)
            for h in range(heads):
                s = nn(kaug[h, ks, :], qaug[h, :, qs])
                mx[h] = jnp.maximum(mx[h], jnp.max(s.reshape(span // 8, 8, block), axis=0))
            return inner

        lax.fori_loop(0, count, max_step, 0)
        tops = []
        for h in range(heads):
            top = jnp.max(mx[h], axis=0, keepdims=True)
            rows = put_rows(
                qaug[h, HEAD : HEAD + 16, qs].astype(f32), [jnp.broadcast_to(v, (16, block)) for v in split_three(top)], n_seq
            )
            qaug[h, HEAD : HEAD + 16, qs] = rows.astype(bf16)
            tops.append(top)

        def sum_step(i, inner):
            ks = pl.ds(pl.multiple_of((lo + 2 * i) * block, block), span)
            for h in range(heads):
                p = jnp.exp(nn(kaug[h, ks, :], qaug[h, :, qs])).astype(bf16)
                acc[h] = acc[h] + nn(vaug[h, :, ks], p)
            return inner

        lax.fori_loop(0, count, sum_step, 0)
        for h in range(heads):
            total = acc[h, HEAD : HEAD + 1, :]
            ot_ref[h * HEAD : (h + 1) * HEAD, qs] = (acc[h, :HEAD, :] / total).astype(bf16)
            lse_ref[h : h + 1, qs] = tops[h] + jnp.log(total)
        return carry

    lax.fori_loop(0, length // block, q_step, 0)


def attend_call(n_seq, seq, qkv, qkvt):
    length, cols = qkv.shape
    heads = cols // (3 * HEAD)
    block = 256
    return pl.pallas_call(
        functools.partial(attend_kernel, n_seq, block),
        out_shape=(sds((heads * HEAD, length), bf16), sds((8, length), f32)),
        in_specs=[SM, VM, VM],
        out_specs=(VM, VM),
        scratch_shapes=[
            pltpu.VMEM((heads, length + block, 2 * HEAD), bf16),
            pltpu.VMEM((heads, 2 * HEAD, length), bf16),
            pltpu.VMEM((heads, HEAD + 16, length + block), bf16),
            pltpu.VMEM((heads, HEAD + 16, block), f32),
            pltpu.VMEM((heads, 8, block), f32),
        ],
        compiler_params=pltpu.CompilerParams(vmem_limit_bytes=VMEM_LIMIT),
        cost_estimate=pl.CostEstimate(flops=4 * 10**9, bytes_accessed=6 * 10**6, transcendentals=10**7),
        name="attend",
    )(seq, qkv, qkvt)


def attend_back_kernel(
    n_seq, block, seq_ref, qkv_ref, qkvt_ref, dot_ref, ot_ref, lse_ref, dqkv_ref, dqkvt_ref,
    kaug, qaug, vaug, doaug, qn, don, dqt, dk, dv,
):
    length = qkv_ref.shape[0]
    heads = qkv_ref.shape[1] // (3 * HEAD)
    width = heads * HEAD
    starts, ends, lives = seq_bounds(seq_ref, n_seq)
    kcols = key_columns(starts, ends, lives, length, 3)
    lane = lax.broadcasted_iota(jnp.int32, (length, HEAD), 1)
    vcols = jnp.where(lane < 3, -1.0, 0.0).astype(bf16)
    qrows = query_rows(starts, ends, length)
    zero = jnp.zeros((HEAD - 16, length), bf16)
    pad = jnp.zeros((2 * HEAD, block), bf16)
    flat = jnp.zeros((block, HEAD), bf16)
    span = 2 * block
    for h in range(heads):
        hs = slice(h * HEAD, (h + 1) * HEAD)
        kaug[h, :, :HEAD] = qkv_ref[:, width + h * HEAD : width + (h + 1) * HEAD]
        kaug[h, :, HEAD:] = kcols
        vaug[h, :, :HEAD] = qkv_ref[:, 2 * width + h * HEAD : 2 * width + (h + 1) * HEAD]
        vaug[h, :, HEAD:] = vcols
        qaug[h, :HEAD, :length] = qkvt_ref[hs, :] * 0.125
        qaug[h, HEAD : HEAD + 16, :length] = put_rows(qrows, split_three(lse_ref[h : h + 1, :]), n_seq).astype(bf16)
        qaug[h, HEAD + 16 :, :length] = zero
        qaug[h, :, length:] = pad
        doaug[h, :, length:] = pad
        don[h, length:, :] = flat
        qn[h, length:, :] = flat
        do = dot_ref[hs, :]
        delta = jnp.sum(do.astype(f32) * ot_ref[hs, :].astype(f32), axis=0, keepdims=True)
        doaug[h, :HEAD, :length] = do
        doaug[h, HEAD : HEAD + 16, :length] = put_rows(
            jnp.zeros((16, length), f32), split_three(delta), 0
        ).astype(bf16)
        doaug[h, HEAD + 16 :, :length] = zero
        qn[h, :length, :] = qkv_ref[:, hs] * 0.125
        don[h, :length, :] = do.T
        dqt[h] = jnp.zeros((HEAD, length + block), f32)

    def k_step(kb, carry):
        ks = pl.ds(pl.multiple_of(kb * block, block), block)
        lo, hi = block_range(kb * block, kb * block + block - 1, starts, ends, block)
        dk[...] = jnp.zeros_like(dk)
        dv[...] = jnp.zeros_like(dv)

        def q_step(i, inner):
            qs = pl.ds(pl.multiple_of((lo + 2 * i) * block, block), span)
            for h in range(heads):
                p = jnp.exp(nn(kaug[h, ks, :], qaug[h, :, qs]))
                ds = (p * nn(vaug[h, ks, :], doaug[h, :, qs])).astype(bf16)
                dv[h] = dv[h] + nn(p.astype(bf16), don[h, qs, :])
                dk[h] = dk[h] + nn(ds, qn[h, qs, :])
                kt = qkvt_ref[width + h * HEAD : width + (h + 1) * HEAD, ks]
                dqt[h, :, qs] = dqt[h, :, qs] + nn(kt, ds)
            return inner

        lax.fori_loop(0, lax.div(hi - lo + 1, 2), q_step, 0)
        for h in range(heads):
            vk = dk[h].astype(bf16)
            vv = dv[h].astype(bf16)
            a, b = width + h * HEAD, 2 * width + h * HEAD
            dqkv_ref[ks, a : a + HEAD] = vk
            dqkv_ref[ks, b : b + HEAD] = vv
            dqkvt_ref[a : a + HEAD, ks] = vk.T
            dqkvt_ref[b : b + HEAD, ks] = vv.T
        return carry

    lax.fori_loop(0, length // block, k_step, 0)
    for h in range(heads):
        v = (dqt[h, :, :length] * 0.125).astype(bf16)
        dqkvt_ref[h * HEAD : (h + 1) * HEAD, :] = v
        dqkv_ref[:, h * HEAD : (h + 1) * HEAD] = v.T


def attend_back_call(n_seq, seq, qkv, qkvt, dot, ot, lse):
    length, cols = qkv.shape
    heads = cols // (3 * HEAD)
    block = 256
    nat = pltpu.VMEM((heads, length, 2 * HEAD), bf16)
    tra = pltpu.VMEM((heads, 2 * HEAD, length + block), bf16)
    return pl.pallas_call(
        functools.partial(attend_back_kernel, n_seq, block),
        out_shape=(sds((length, cols), bf16), sds((cols, length), bf16)),
        in_specs=[SM] + [VM] * 5,
        out_specs=(VM, VM),
        scratch_shapes=[
            nat, tra, nat, tra,
            pltpu.VMEM((heads, length + block, HEAD), bf16),
            pltpu.VMEM((heads, length + block, HEAD), bf16),
            pltpu.VMEM((heads, HEAD, length + block), f32),
            pltpu.VMEM((heads, block, HEAD), f32),
            pltpu.VMEM((heads, block, HEAD), f32),
        ],
        compiler_params=pltpu.CompilerParams(vmem_limit_bytes=VMEM_LIMIT),
        cost_estimate=pl.CostEstimate(flops=10**10, bytes_accessed=12 * 10**6, transcendentals=10**7),
        name="attend_back",
    )(seq, qkv, qkvt, dot, ot, lse)


def levels(n_dp):
    n_in = 2 if n_dp < 16 else 4
    return n_in, n_dp // n_in


def shard_of(r, c):
    return lax.rem(r + 2 * c, 4)


def middle_kernel(
    n_dp, oin_ref, xf_any, dys_ref, w_ref, back_ref, dh1_ref, dout_ref, *rest
):
    n_in, n_out = levels(n_dp)
    a_refs, b_refs, rest = rest[:n_in], rest[n_in : n_in + n_out], rest[n_in + n_out :]
    middle_body(n_dp, oin_ref, xf_any, dys_ref, w_ref, back_ref, dh1_ref, dout_ref, a_refs, b_refs, *rest)


def middle_body(
    n_dp, oin_ref, xf_any, dys_ref, w_ref, back_ref, dh1_ref, dout_ref, a_refs, b_refs,
    xv, xsem, fin, s_a, r_a, dyin, dyb, ot_ref, dot_ref, wup, wdn, wo, vec, ub, hid, slope, gbuf, gin, facc, yacc,
    so, ro, sg, rg, lsem, wss, wrs, sgb, rgb, sgt, rgt, gsem, sd, rd, sm, rm,
):
    d, r, c = me()
    half = lax.rem(r, 2)
    wide = xf_any.shape[3]
    width = 2 * wide
    tok = dyb.shape[0]
    mine = pl.ds(pl.multiple_of(c * tok, tok), tok)
    x_cp = pltpu.make_async_copy(xf_any.at[half, :, mine, :], xv, xsem)
    x_cp.start()
    hrows = oin_ref.shape[0]
    core = (d, r, 1 - c)
    peers = [(d, flip(r), c), (d, flip(r), 1 - c), core]
    ring = [(lax.rem(d + k, n_dp), r, c) for k in range(1, n_dp)]
    greet(peers + ring + [(dev[0], r, 1 - c) for dev in ring])
    base = r - half
    shard = shard_of(r, c)
    o_cp = []
    for i, dev in enumerate(peers):
        q = (dev[1] - base) * 2 + dev[2]
        src = oin_ref.at[:, pl.ds(pl.multiple_of(q * tok, tok), tok)]
        cp = remote(src, ot_ref.at[shard], so.at[i], ro.at[i], dev)
        cp.start()
        o_cp.append(cp)
    myq = pl.ds(pl.multiple_of((half * 2 + c) * tok, tok), tok)
    ot_ref[shard] = oin_ref[:, myq]

    piece = dys_ref.shape[1]
    here = pl.ds(pl.multiple_of(d * piece, piece), piece)
    d_cp = []
    for k, dev in enumerate(ring):
        cp = remote(dys_ref.at[dev[0]], dyin.at[here, :], sd.at[k], rd.at[k], dev)
        cp.start()
        d_cp.append(cp)
    dyin[here, :] = dys_ref[d]

    loads = [[], [], []]
    mycols = pl.ds(pl.multiple_of(c * wide, 128), wide)
    for j in range(4):
        js = slice(j * hrows, (j + 1) * hrows)
        loads[0].append((w_ref.at[j, OUT:VEC], wo.at[js, mycols]))
        loads[0].append((w_ref.at[j, VEC : VEC + 16], ub.at[j, c]))
        for h in range(2):
            hs = slice(h * wide, (h + 1) * wide)
            loads[1].append((w_ref.at[j, hs], wup.at[j, mycols, hs]))
        loads[2].append((w_ref.at[j, DOWN:OUT], wdn.at[j, :, mycols]))
    w_cps = []
    for i, group in enumerate(loads):
        cps = []
        for k, (src, dst) in enumerate(group):
            a = pltpu.make_async_copy(src, dst, lsem.at[i, k])
            a.start()
            b = remote(src, dst, wss.at[i, k], wrs.at[i, k], core)
            b.start()
            cps += [a, b]
        w_cps.append(cps)

    def settle(i):
        for cp in w_cps[i]:
            cp.wait()

    for cp in o_cp:
        cp.wait_recv()
    for cp in d_cp:
        cp.wait_recv()
    theirs = pl.ds(pl.multiple_of((1 - c) * tok, tok), tok)
    dy_cp = remote(dyin.at[theirs, :], dyb, sm, rm, core)
    dy_cp.start()
    x_cp.wait()
    x = jnp.concatenate([xv[0], xv[1]], axis=1).astype(f32)
    settle(0)
    vec[...] = jnp.concatenate([ub[0, 0], ub[0, 1]], axis=1)
    ob, g1, s1, db, g2, s2 = [vec[i : i + 1, :].astype(f32) for i in range(6)]
    o = ot_ref[...].reshape(width, tok).T
    h1 = x + (nn(o, wo[...]) + ob)
    mu = jnp.mean(h1, axis=1, keepdims=True)
    r1 = lax.rsqrt(jnp.mean(h1 * h1, axis=1, keepdims=True) - mu * mu + EPS)
    n1 = (h1 - mu) * r1
    y1 = (n1 * g1 + s1).astype(bf16)
    settle(1)
    settle(2)
    facc[...] = jnp.zeros_like(facc)

    def ahead(j, carry):
        bias = jnp.concatenate([ub[j, 0, 6:7, :], ub[j, 0, 7:8, :]], axis=1).astype(f32)
        u = nn(y1, wup[j]) + bias
        cdf = 0.5 * (1.0 + lax.erf(u * INV_ROOT_TWO))
        hj = (u * cdf).astype(bf16)
        hid[j] = hj
        slope[j] = cdf + u * jnp.exp(-0.5 * u * u) * INV_ROOT_TAU
        facc[...] += nn(hj, wdn[j])
        return carry

    lax.fori_loop(0, 4, ahead, 0)
    h2 = y1.astype(f32) + (facc[...] + db)
    mu2 = jnp.mean(h2, axis=1, keepdims=True)
    r2 = lax.rsqrt(jnp.mean(h2 * h2, axis=1, keepdims=True) - mu2 * mu2 + EPS)
    n2 = (h2 - mu2) * r2
    res = (n2 * g2 + s2).astype(bf16)
    fin[0] = res[:, :wide]
    fin[1] = res[:, wide:]
    send_back(n_dp, fin, back_ref, s_a, r_a)
    dy_cp.wait_recv()
    own, other = dyin[mine, :], dyb[...]
    left = jnp.where(c == 0, own, other)
    right = jnp.where(c == 0, other, own)
    dy = jnp.concatenate([left, right], axis=1).astype(f32)
    e2 = dy * g2
    dh2 = r2 * (e2 - jnp.mean(e2, axis=1, keepdims=True) - n2 * jnp.mean(e2 * n2, axis=1, keepdims=True))
    g2g = jnp.sum(dy * n2, axis=0, keepdims=True)
    s2g = jnp.sum(dy, axis=0, keepdims=True)
    df = dh2.astype(bf16)
    dbg = jnp.sum(df.astype(f32), axis=0, keepdims=True)
    yacc[...] = dh2
    y1t = y1.T

    def big_cp(j):
        return remote(gbuf.at[j, 1 - c, 0:OUT], gin.at[j, 0:OUT], sgb.at[j], rgb.at[j], core)

    def back(j, carry):
        du = (nt(df, wdn[j]) * slope[j]).astype(bf16)
        ubg = jnp.sum(du.astype(f32), axis=0, keepdims=True)
        gd = tn(hid[j], df).astype(bf16)
        gu = nn(y1t, du).astype(bf16)
        for cc in range(2):
            cs = slice(cc * wide, (cc + 1) * wide)
            for h in range(2):
                gbuf[j, cc, h * wide : (h + 1) * wide, :] = gu[cs, h * wide : (h + 1) * wide]
            gbuf[j, cc, DOWN:OUT, :] = gd[:, cs]
        for cc in range(2):
            gbuf[j, cc, VEC : VEC + 16, :] = jnp.concatenate(
                [jnp.broadcast_to(ubg[:, :wide], (8, wide)), jnp.broadcast_to(ubg[:, wide:], (8, wide))], axis=0
            ).astype(bf16)
        big_cp(j).start()
        yacc[...] += nt(du, wup[j])
        return carry

    lax.fori_loop(0, 4, back, 0)
    dy1 = yacc[...]
    e1 = dy1 * g1
    dh1 = r1 * (e1 - jnp.mean(e1, axis=1, keepdims=True) - n1 * jnp.mean(e1 * n1, axis=1, keepdims=True))
    dh1_ref[...] = dh1
    g1g = jnp.sum(dy1 * n1, axis=0, keepdims=True)
    s1g = jnp.sum(dy1, axis=0, keepdims=True)
    da = dh1.astype(bf16)
    obg = jnp.sum(da.astype(f32), axis=0, keepdims=True)
    dot_ref[...] = nt(da, wo[...]).T.astype(bf16).reshape(dot_ref.shape)
    g_cp = []
    for i, dev in enumerate(peers):
        cp = remote(dot_ref.at[shard_of(dev[1], dev[2])], dout_ref.at[:, myq], sg.at[i], rg.at[i], dev)
        cp.start()
        g_cp.append(cp)
    dout_ref[:, myq] = dot_ref[shard]
    go = nn(ot_ref[...].reshape(width, tok), da).astype(bf16)
    pad = gbuf.shape[2] - VEC
    row = lax.broadcasted_iota(jnp.int32, (pad, wide), 0)
    t_cp = []
    for j in range(4):
        for cc in range(2):
            cs = slice(cc * wide, (cc + 1) * wide)
            gbuf[j, cc, OUT:VEC, :] = go[j * hrows : (j + 1) * hrows, cs]
            tail = jnp.zeros((pad, wide), f32)
            for i, v in enumerate((obg, g1g, s1g, dbg, g2g, s2g)):
                tail = jnp.where(row == i, v[:, cs], tail)
            tail = jnp.where(row == 6, gbuf[j, cc, VEC : VEC + 16, :][0:1].astype(f32), tail)
            tail = jnp.where(row == 7, gbuf[j, cc, VEC : VEC + 16, :][8:9].astype(f32), tail)
            gbuf[j, cc, VEC:, :] = tail.astype(bf16)
        cp = remote(gbuf.at[j, 1 - c, OUT:], gin.at[j, OUT:], sgt.at[j], rgt.at[j], core)
        cp.start()
        t_cp.append(cp)
    rows_q = gbuf.shape[2] // n_dp
    n_in, n_out = levels(n_dp)
    outs = []
    for j in range(4):
        big_cp(j).wait()
        t_cp[j].wait()
        gin[j] = (gin[j].astype(f32) + gbuf[j, c].astype(f32)).astype(bf16)
        n_first, n_second, refs = (n_in, n_out, a_refs) if j < 2 else (n_out, n_in, b_refs)
        for k in range(n_first):
            for m in range(n_second):
                if j < 2:
                    s = m * n_in + lax.rem(lax.rem(d, n_in) + k, n_in)
                else:
                    s = lax.rem(lax.div(d, n_in) + k, n_out) * n_in + m
                span = pl.ds(pl.multiple_of(s * rows_q, rows_q), rows_q)
                cp = pltpu.make_async_copy(gin.at[j, span], refs[k].at[m, j % 2], gsem.at[j, k * n_second + m])
                cp.start()
                outs.append(cp)
    got_back(n_dp, fin, back_ref, s_a, r_a)
    sent_back(n_dp, fin, back_ref, s_a, r_a)
    for cp in o_cp + d_cp + [dy_cp]:
        cp.wait_send()
    for cp in g_cp + outs:
        cp.wait()


def middle_call(n_dp, oin, xf, dys, w, g_rows):
    tok, wide = xf.shape[2] // 2, xf.shape[3]
    width = 2 * wide
    hrows = oin.shape[0]
    n_in, n_out = levels(n_dp)
    return pl.pallas_call(
        functools.partial(middle_kernel, n_dp),
        out_shape=(
            sds((2 * tok, wide), bf16),
            sds((tok, width), f32),
            sds((hrows, 4 * tok), bf16),
        )
        + (sds((n_out, 2, g_rows // n_dp, wide), bf16),) * n_in
        + (sds((n_in, 2, g_rows // n_dp, wide), bf16),) * n_out,
        in_specs=[VM, ANY, VM, ANY],
        out_specs=(VM, VM, VM) + (ANY,) * (n_in + n_out),
        scratch_shapes=[
            pltpu.VMEM((2, tok, wide), bf16),
            DMA,
            pltpu.VMEM((2, tok, wide), bf16),
            DMA((n_dp // 2, 2)), DMA((n_dp,)),
            pltpu.VMEM((2 * tok, wide), bf16),
            pltpu.VMEM((tok, wide), bf16),
            pltpu.VMEM((4, hrows, tok), bf16),
            pltpu.VMEM((4, hrows, tok), bf16),
            pltpu.VMEM((4, width, width), bf16),
            pltpu.VMEM((4, width, width), bf16),
            pltpu.VMEM((width, width), bf16),
            pltpu.VMEM((16, width), bf16),
            pltpu.VMEM((4, 2, 16, wide), bf16),
            pltpu.VMEM((4, tok, width), bf16),
            pltpu.VMEM((4, tok, width), f32),
            pltpu.VMEM((4, 2, g_rows, wide), bf16),
            pltpu.VMEM((4, g_rows, wide), bf16),
            pltpu.VMEM((tok, width), f32),
            pltpu.VMEM((tok, width), f32),
            DMA((3,)), DMA((3,)), DMA((3,)), DMA((3,)),
            DMA((3, 8)), DMA((3, 8)), DMA((3, 8)),
            DMA((4,)), DMA((4,)), DMA((4,)), DMA((4,)),
            DMA((4, n_dp)), DMA((n_dp,)), DMA((n_dp,)), DMA, DMA,
        ],
        compiler_params=pltpu.CompilerParams(
            collective_id=2, has_side_effects=True, vmem_limit_bytes=VMEM_LIMIT
        ),
        cost_estimate=pl.CostEstimate(flops=16 * 10**9, bytes_accessed=30 * 10**6, transcendentals=4 * 10**6),
        name="middle",
    )(oin, xf, dys, w)


def return_kernel(n_dp, dqkv_ref, dqkvt_ref, wq_any, xf_any, dh1_any, *rest):
    n_in, n_out = levels(n_dp)
    a_parts, b_parts, rest = rest[:n_in], rest[n_in : n_in + n_out], rest[n_in + n_out :]
    return_body(n_dp, dqkv_ref, dqkvt_ref, wq_any, xf_any, dh1_any, a_parts, b_parts, *rest)


def return_body(
    n_dp, dqkv_ref, dqkvt_ref, wq_any, xf_any, dh1_any, a_parts, b_parts,
    back_ref, gout_ref, gall_ref,
    wq, xf, dh1, apart, bpart, lsem,
    asum, bsum, ain, bin_, rsum, zin, rfin, fin, tocore, fromcore, toz, fromz, gq_ref, gqin, gsum, xq, gfin,
    s_1, r_1, s_2, r_2, s_r, r_r, s_t, r_t, s_b, r_b, s_c, r_c, s_z, r_z, s_q, r_q, s_x, r_x, s_g, r_g,
):
    d, r, c = me()
    n_in, n_out = levels(n_dp)
    o, i = lax.div(d, n_in), lax.rem(d, n_in)
    half = lax.rem(r, 2)
    tok, width = dh1_any.shape
    wide = width // 2
    core = (d, r, 1 - c)
    zdev = (d, flip(r), c)
    far_row = lax.rem(r + 2, 4)
    rows_dev = [(d, lax.rem(r + k, 4), c) for k in (1, 2, 3)]
    loads = [pltpu.make_async_copy(wq_any, wq, lsem.at[0])]
    for k in range(n_in):
        loads.append(pltpu.make_async_copy(a_parts[k], apart.at[k], lsem.at[3 + k]))
    for k in range(n_out):
        loads.append(pltpu.make_async_copy(b_parts[k], bpart.at[k], lsem.at[3 + n_in + k]))
    loads.append(pltpu.make_async_copy(dh1_any, dh1, lsem.at[1]))
    loads.append(pltpu.make_async_copy(xf_any, xf, lsem.at[2]))
    for cp in loads:
        cp.start()
    peers = [(lax.rem(d + k, n_dp), r, cc) for k in range(1, n_dp) for cc in (0, 1)]
    greet(peers + rows_dev + [core, (d, far_row, 1 - c)])

    def part(h, cc):
        q = h * 2 + cc
        rows = dqkv_ref[pl.ds(pl.multiple_of(q * tok, tok), tok), :]
        return jnp.concatenate([nn(rows, wq[0]), nn(rows, wq[1])], axis=1)

    loads[0].wait()
    tocore[0] = part(1 - half, 1 - c).astype(bf16)
    cp_far = remote(tocore.at[0], fromcore.at[0], s_c.at[0], r_c.at[0], core)
    cp_far.start()

    for cp in loads[1:-2]:
        cp.wait()
    total = apart[0].astype(f32)
    for k in range(1, n_in):
        total = total + apart[k].astype(f32)
    asum[...] = total.astype(bf16)
    total = bpart[0].astype(f32)
    for k in range(1, n_out):
        total = total + bpart[k].astype(f32)
    bsum[...] = total.astype(bf16)
    a_cp, b_cp = [], []
    for k in range(1, n_out):
        dest = lax.rem(o + k, n_out)
        cp = remote(asum.at[dest], ain.at[k], s_1.at[k], r_1.at[k], (dest * n_in + i, r, c))
        cp.start()
        a_cp.append(cp)
    for k in range(1, n_in):
        dest = lax.rem(i + k, n_in)
        cp = remote(bsum.at[dest], bin_.at[k], s_2.at[k], r_2.at[k], (o * n_in + dest, r, c))
        cp.start()
        b_cp.append(cp)

    far = part(1 - half, c)
    cp_far.wait_recv()
    toz[...] = (far + fromcore[0].astype(f32)).astype(bf16)
    cp_z = remote(toz, fromz, s_z, r_z, zdev)
    cp_z.start()

    n_cols, length = dqkvt_ref.shape
    loads[-1].wait()
    for f in range(2):
        g = nn(dqkvt_ref[:, : length // 2], xf[0, f]) + nn(dqkvt_ref[:, length // 2 :], xf[1, f])
        gq_ref[f, :n_cols, :] = g.astype(bf16)
    third = n_cols // 3
    sums = jnp.sum(dqkv_ref[...].astype(f32), axis=0, keepdims=True)
    bias = jnp.concatenate([sums[:, :third], sums[:, 2 * third :]], axis=1)
    pad = gq_ref.shape[1] - n_cols
    row = lax.broadcasted_iota(jnp.int32, (pad, wide), 0)
    tail = jnp.where(row == 0, bias, 0.0).astype(bf16)
    for f in range(2):
        gq_ref[f, n_cols:, :] = tail
    rq = gq_ref.shape[1] // n_dp

    def quarter(s):
        return pl.ds(pl.multiple_of(s * rq, rq), rq)

    q_cp = []
    for k in range(1, n_dp):
        dest = lax.rem(d + k, n_dp)
        cp = remote(gq_ref.at[:, quarter(dest), :], gqin.at[k], s_q.at[k], r_q.at[k], (dest, r, c))
        cp.start()
        q_cp.append(cp)

    tocore[1] = part(half, 1 - c).astype(bf16)
    cp_near = remote(tocore.at[1], fromcore.at[1], s_c.at[1], r_c.at[1], core)
    cp_near.start()

    total = asum[o].astype(f32)
    for cp in a_cp:
        cp.wait_recv()
    for k in range(1, n_out):
        total = total + ain[k].astype(f32)
    rsum[0:2] = total.astype(bf16)
    total = bsum[i].astype(f32)
    for cp in b_cp:
        cp.wait_recv()
    for k in range(1, n_in):
        total = total + bin_[k].astype(f32)
    rsum[2:4] = total.astype(bf16)
    row_cp = []
    for k, dev in enumerate(rows_dev):
        cp = remote(rsum.at[dev[1]], zin.at[k], s_r.at[k], r_r.at[k], dev)
        cp.start()
        row_cp.append(cp)

    loads[-2].wait()
    total = part(half, c) + dh1[...]
    cp_near.wait_recv()
    total = total + fromcore[1].astype(f32)

    acc = gq_ref[:, quarter(d), :].astype(f32)
    for k in range(1, n_dp):
        q_cp[k - 1].wait_recv()
        acc = acc + gqin[k].astype(f32)
    gsum[...] = acc.astype(bf16)
    to_one = remote(gsum.at[1], xq.at[1], s_x.at[1], r_x.at[1], (d, r, 1))
    far_0 = remote(gsum.at[0], xq.at[0], s_x.at[0], r_x.at[0], (d, far_row, 0))
    far_1 = remote(gsum.at[1], xq.at[0], s_x.at[1], r_x.at[0], (d, far_row, 1))

    @pl.when(c == 0)
    def _():
        to_one.start()

    @pl.when(c == 1)
    def _():
        far_0.start()
        far_1.start()

    cp_z.wait_recv()
    total = (total + fromz[...].astype(f32)).astype(bf16)
    fin[0] = total[:, :wide]
    fin[1] = total[:, wide:]
    send_back(n_dp, fin, back_ref, s_b, r_b)

    held = rsum[r].astype(f32)
    for k in range(3):
        row_cp[k].wait_recv()
        held = held + zin[k].astype(f32)
    rfin[...] = held.astype(bf16)
    n_keep = rfin.shape[0]
    keep = pl.ds(pl.multiple_of(d * n_keep, n_keep), n_keep)
    gall_ref[keep, :] = rfin[...]
    t_cp = []
    for k in range(1, n_dp):
        dest = lax.rem(d + k, n_dp)
        cp = remote(rfin, gall_ref.at[keep, :], s_t.at[k], r_t.at[k], (dest, r, c))
        cp.start()
        t_cp.append(cp)

    far_0.wait_recv()

    @pl.when(c == 0)
    def _():
        gfin[...] = (gsum[0].astype(f32) + xq[0].astype(f32)).astype(bf16)

    @pl.when(c == 1)
    def _():
        to_one.wait_recv()
        gfin[...] = (xq[0].astype(f32) + xq[1].astype(f32)).astype(bf16)

    for k in range(1, n_dp):
        dest = lax.rem(d + k, n_dp)
        cp = remote(gfin, gout_ref.at[quarter(d), :], s_g.at[k], r_g.at[k], (dest, r, c))
        cp.start()
        t_cp.append(cp)
    gout_ref[quarter(d), :] = gfin[...]
    got_back(n_dp, fin, back_ref, s_b, r_b)
    sent_back(n_dp, fin, back_ref, s_b, r_b)
    for cp in [cp_far, cp_near, cp_z] + q_cp + a_cp + b_cp + row_cp:
        cp.wait_send()
    for cp in t_cp:
        cp.wait()

    @pl.when(c == 0)
    def _():
        to_one.wait_send()

    @pl.when(c == 1)
    def _():
        far_0.wait_send()
        far_1.wait_send()


def return_call(n_dp, dqkv, dqkvt, wq, xf, dh1, a_parts, b_parts, gq_rows):
    n_in, n_out = levels(n_dp)
    tok, width = dh1.shape
    wide = width // 2
    share = a_parts[0].shape[2]
    tokens = 2 * tok

    def vm(*shape):
        return pltpu.VMEM(shape, bf16)

    return pl.pallas_call(
        functools.partial(return_kernel, n_dp),
        out_shape=(sds((tokens, wide), bf16), sds((gq_rows, wide), bf16), sds((n_dp * share, wide), bf16)),
        in_specs=[VM, VM] + [ANY] * (3 + n_in + n_out),
        out_specs=(VM,) * 3,
        scratch_shapes=[
            vm(*wq.shape), vm(*xf.shape), pltpu.VMEM(dh1.shape, f32),
            vm(n_in, n_out, 2, share, wide), vm(n_out, n_in, 2, share, wide), DMA((3 + n_in + n_out,)),
            vm(n_out, 2, share, wide), vm(n_in, 2, share, wide), vm(n_out, 2, share, wide), vm(n_in, 2, share, wide),
            vm(4, share, wide), vm(3, share, wide), vm(share, wide),
            vm(2, tok, wide), vm(2, tok, width), vm(2, tok, width), vm(tok, width), vm(tok, width),
            vm(2, gq_rows, wide), vm(n_dp, 2, gq_rows // n_dp, wide), vm(2, gq_rows // n_dp, wide),
            vm(2, gq_rows // n_dp, wide), vm(gq_rows // n_dp, wide),
            DMA((n_out,)), DMA((n_out,)), DMA((n_in,)), DMA((n_in,)),
            DMA((3,)), DMA((3,)), DMA((n_dp,)), DMA((n_dp,)),
            DMA((n_dp // 2, 2)), DMA((n_dp,)),
            DMA((2,)), DMA((2,)), DMA, DMA,
            DMA((n_dp,)), DMA((n_dp,)), DMA((2,)), DMA((2,)), DMA((n_dp,)), DMA((n_dp,)),
        ],
        compiler_params=pltpu.CompilerParams(
            collective_id=4, has_side_effects=True, vmem_limit_bytes=VMEM_LIMIT
        ),
        name="return",
    )(dqkv, dqkvt, wq, xf, dh1, *a_parts, *b_parts)


def finish_kernel(
    a_ref, b_ref, deal_ref, g_ref, q_ref,
    out_ref, ig_ref, qw_ref, qb_ref, kw_ref, vw_ref, vb_ref, ow_ref, ob_ref, g1_ref, s1_ref, up_ref, ub_ref, dn_ref,
    db_ref, g2_ref, s2_ref,
):
    tokens, wide = a_ref.shape
    third = qw_ref.shape[0]
    place = (lax.broadcasted_iota(jnp.int32, (tokens, tokens), 0) == deal_ref[...]).astype(bf16)
    out_ref[...] = nn(place, a_ref[...]).astype(bf16)
    ig_ref[...] = nn(place, b_ref[...]).astype(bf16)
    qw_ref[...] = q_ref[:third, :].astype(f32)
    kw_ref[...] = q_ref[third : 2 * third, :].astype(f32)
    vw_ref[...] = q_ref[2 * third : 3 * third, :].astype(f32)
    bias = q_ref[3 * third : 3 * third + 16, :].astype(f32)[0:1]
    qb_ref[...] = bias[0, :third]
    vb_ref[...] = bias[0, third:]
    up_ref[:, :wide] = g_ref[:wide, :].astype(f32)
    up_ref[:, wide:] = g_ref[wide : 2 * wide, :].astype(f32)
    dn_ref[...] = g_ref[DOWN:OUT, :].astype(f32)
    ow_ref[...] = g_ref[OUT:VEC, :].astype(f32)
    vec = g_ref[VEC : VEC + 16, :].astype(f32)
    for i, ref in enumerate((ob_ref, g1_ref, s1_ref, db_ref, g2_ref, s2_ref)):
        ref[...] = vec[i]
    ub_ref[0:wide] = vec[6]
    ub_ref[wide : 2 * wide] = vec[7]


def finish_call(back_a, back_b, deal, gall, gq, third):
    tokens, wide = back_a.shape
    one = sds((wide,), f32)
    row = sds((third,), f32)
    head = sds((third, wide), f32)
    tok = sds((tokens, wide), bf16)
    return pl.pallas_call(
        finish_kernel,
        out_shape=(
            tok, tok, head, row, head, head, row, head, one, one, one, sds((wide, 2 * wide), f32),
            sds((2 * wide,), f32), sds((2 * wide, wide), f32), one, one, one,
        ),
        in_specs=[VM] * 5,
        out_specs=(VM,) * 17,
        compiler_params=pltpu.CompilerParams(vmem_limit_bytes=VMEM_LIMIT),
        name="finish",
    )(back_a, back_b, deal, gall, gq)


def round_up(v, m):
    return (v + m - 1) // m * m


def on_device(
    n_dp, inputs, out_grad, deal, seq_lengths, key_trim, query_weight, query_bias, key_weight,
    value_weight, value_bias, out_weight, out_bias, first_gain, first_shift, up_weight, up_bias,
    down_weight, down_bias, second_gain, second_shift,
):
    wide = inputs.shape[1]
    n_seq = seq_lengths.shape[1]
    step = 16 * n_dp
    third = query_weight.shape[1]
    rows_w = round_up(VEC + 16, step)
    xf, dys, qkv, qkvt, wq, seq, wg = deal_call(
        n_dp, rows_w,
        (
            inputs, out_grad, deal, query_weight.T, key_weight.T, value_weight.T, query_bias, value_bias, up_weight,
            down_weight, out_weight, out_bias, first_gain, first_shift, down_bias, second_gain, second_shift, up_bias,
            seq_lengths, key_trim,
        ),
    )
    ot, lse = attend_call(n_seq, seq, qkv, qkvt)
    back_a, dh1, dot, *grads = middle_call(n_dp, ot, xf, dys, wg, rows_w)
    n_in, n_out = levels(n_dp)
    a_parts, b_parts = grads[:n_in], grads[n_in:]
    for k in range(1, n_in):
        a_parts[k] = lax.ppermute(
            a_parts[k], "dp", [(o * n_in + i, o * n_in + (i + k) % n_in) for o in range(n_out) for i in range(n_in)]
        )
    for k in range(1, n_out):
        b_parts[k] = lax.ppermute(
            b_parts[k], "dp", [(o * n_in + i, (o + k) % n_out * n_in + i) for o in range(n_out) for i in range(n_in)]
        )
    dqkv, dqkvt = attend_back_call(n_seq, seq, qkv, qkvt, dot, ot, lse)
    gq_rows = round_up(3 * third + 16, step)
    back_b, gq, gall = return_call(n_dp, dqkv, dqkvt, wq, xf, dh1, a_parts, b_parts, gq_rows)
    outs = list(finish_call(back_a, back_b, deal, gall, gq, third))
    for i in (2, 4, 5):
        outs[i] = outs[i].T
    return tuple(outs)


def solution(mesh):
    n_dp = mesh.shape["dp"]
    tok = P(("dp", "row"), "col")
    one = P("col")
    row = P("row")
    a = P("col", "row")
    b = P("row", "col")
    seqs = P(("dp", "col"), None)
    in_specs = (
        tok, tok, P(("dp", "row"), None), seqs, seqs, a, row, a, a, row, b, one, one, one, a, row, b, one, one, one,
    )
    out_specs = (tok, tok, a, row, a, a, row, b, one, one, one, a, row, b, one, one, one)
    return jax.shard_map(
        functools.partial(on_device, n_dp), mesh=mesh, in_specs=in_specs, out_specs=out_specs, check_vma=False
    )
```

```python
import functools

import jax
import jax.numpy as jnp
from jax import lax
from jax.experimental import pallas as pl
from jax.experimental.pallas import tpu as pltpu
from jax.sharding import PartitionSpec as P

MESH = pl.DeviceIdType.MESH
f32 = jnp.float32
bf16 = jnp.bfloat16

HEAD = 64
EPS = 1e-05
FAR = -1e30
INV_ROOT_TWO = 0.7071067811865476
INV_ROOT_TAU = 0.3989422804014327
VMEM_LIMIT = 62 * 1024 * 1024
DOWN, OUT, VEC = 768, 1536, 1728

VM = pl.BlockSpec(memory_space=pltpu.VMEM)
SM = pl.BlockSpec(memory_space=pltpu.SMEM)
ANY = pl.BlockSpec(memory_space=pl.ANY)
DMA = pltpu.SemaphoreType.DMA


def nn(a, b):
    return lax.dot_general(a, b, (((1,), (0,)), ((), ())), preferred_element_type=f32)


def nt(a, b):
    return lax.dot_general(a, b, (((1,), (1,)), ((), ())), preferred_element_type=f32)


def tn(a, b):
    return lax.dot_general(a, b, (((0,), (0,)), ((), ())), preferred_element_type=f32)


def sds(shape, dtype):
    return jax.ShapeDtypeStruct(shape, dtype)


def me():
    return lax.axis_index("dp"), lax.axis_index("row"), lax.axis_index("col")


def flip(v):
    return v + 1 - 2 * lax.rem(v, 2)


def remote(src, dst, ssem, rsem, dev):
    return pltpu.make_async_remote_copy(
        src_ref=src, dst_ref=dst, send_sem=ssem, recv_sem=rsem, device_id=dev, device_id_type=MESH
    )


def greet(devs):
    barrier = pltpu.get_barrier_semaphore()
    for dev in devs:
        pl.semaphore_signal(barrier, inc=1, device_id=dev, device_id_type=MESH)
    pl.semaphore_wait(barrier, len(devs))


def send_back(n_dp, src, back, ss, rs):
    d, r, c = me()
    n_half = n_dp // 2
    piece = back.shape[0] // n_dp
    here = pl.ds(pl.multiple_of(d * piece, piece), piece)
    for i in range(n_half):
        s = c * n_half + i
        for cc in range(2):
            ref = src.at[cc, i * piece : (i + 1) * piece, :]
            cp = remote(ref, back.at[here, :], ss.at[i, cc], rs.at[d], (s, r, cc))
            local = (s == d) & (c == cc)

            @pl.when(jnp.logical_not(local))
            def _():
                cp.start()

            @pl.when(local)
            def _():
                back[here, :] = src[cc, i * piece : (i + 1) * piece, :]


def sent_back(n_dp, src, back, ss, rs):
    d, r, c = me()
    n_half = n_dp // 2
    piece = back.shape[0] // n_dp
    for i in range(n_half):
        s = c * n_half + i
        for cc in range(2):
            ref = src.at[cc, i * piece : (i + 1) * piece, :]

            @pl.when(jnp.logical_not((s == d) & (c == cc)))
            def _():
                remote(ref, back.at[0:piece, :], ss.at[i, cc], rs.at[0], (s, r, cc)).wait_send()


def got_back(n_dp, src, back, ss, rs):
    d, r, c = me()
    holder = lax.div(d, n_dp // 2)
    piece = back.shape[0] // n_dp
    for g in range(n_dp):

        @pl.when(jnp.logical_not((d == g) & (holder == c)))
        def _():
            remote(
                src.at[0, 0:piece, :], back.at[g * piece : (g + 1) * piece, :], ss.at[0, 0], rs.at[g], (d, r, 1 - c)
            ).wait_recv()


def deal_kernel(
    n_dp, rows_w, x_ref, dy_ref, deal_ref, qw_ref, kw_ref, vw_ref, qb_ref, vb_ref, up_ref, dn_ref, ow_ref,
    ob_ref, g1_ref, s1_ref, db_ref, g2_ref, s2_ref, ub_ref, len_ref, trim_ref,
    xf_out, dys_out, qkv_out, qkvt_out, wq_out, seqo_ref, wg_ref,
    xf_ref, dys_ref, qkv_ref, qkvt_ref, wq_ref, so,
    xs, seq, seqrx, w, bias, biases, blob, col,
    sx, rx, sc, rc, sz, rz, sc2, rc2, sw, rw, sb, rb, sm, rm, ss, rs, sf, rf, sl,
):
    d, r, c = me()
    half = lax.rem(r, 2)
    tokens, wide = x_ref.shape
    piece = tokens // n_dp
    third = qw_ref.shape[0]
    core = (d, r, 1 - c)
    zdev = (d, flip(r), c)
    far_row = lax.rem(r + 2, 4)
    ring = [(lax.rem(d + k, n_dp), r, c) for k in range(1, n_dp)]
    rows_dev = [(d, lax.rem(r + k, 4), c) for k in (1, 2, 3)]
    greet(ring + rows_dev + [core, (d, far_row, 1 - c)])

    blob[0:wide, :] = up_ref[:, :wide]
    blob[wide : 2 * wide, :] = up_ref[:, wide:]
    blob[DOWN:OUT, :] = dn_ref[...]
    blob[OUT:VEC, :] = ow_ref[...]
    vecs = [v[...].reshape(1, wide) for v in (ob_ref, g1_ref, s1_ref, db_ref, g2_ref, s2_ref)]
    vecs += [ub_ref[0:wide].reshape(1, wide), ub_ref[wide : 2 * wide].reshape(1, wide)]
    row = lax.broadcasted_iota(jnp.int32, (16, wide), 0)
    tail = jnp.zeros((16, wide), f32)
    for i, v in enumerate(vecs):
        tail = jnp.where(row == i, v.astype(f32), tail)
    blob[VEC : VEC + 16, :] = tail.astype(bf16)
    blob[VEC + 16 :, :] = jnp.zeros((rows_w - VEC - 16, wide), bf16)
    share = rows_w // n_dp
    my_share = pl.ds(pl.multiple_of(d * share, share), share)
    share_cp = [
        remote(blob.at[my_share, :], wg_ref.at[r, my_share, :], ss.at[k], rs.at[k], dev)
        for k, dev in enumerate(rows_dev)
    ]
    for cp in share_cp:
        cp.start()
    local_w = pltpu.make_async_copy(blob, wg_ref.at[r], sl)
    local_w.start()

    def rows(s):
        return pl.ds(pl.multiple_of(s * piece, piece), piece)

    col[...] = jnp.broadcast_to(deal_ref[...], (8, tokens)).T
    lane = lax.broadcasted_iota(jnp.int32, (piece, tokens), 1)
    sends = []
    for k in list(range(1, n_dp)) + [0]:
        dest = lax.rem(d + k, n_dp)
        pick = (col[rows(dest), 0:1] == lane).astype(bf16)
        px = nn(pick, x_ref[...]).astype(bf16)
        if k:
            xs[k] = px
            cp = remote(xs.at[k], xf_ref.at[half, c, rows(d), :], sx.at[k], rx.at[k], (dest, r, c))
            cp.start()
            sends.append(cp)
        else:
            xf_ref[half, c, rows(d), :] = px

    w[:third, :] = qw_ref[...]
    w[third : 2 * third, :] = kw_ref[...]
    w[2 * third :, :] = vw_ref[...]
    w_far = remote(w, wq_ref.at[c], sw.at[0], rw.at[c], (d, far_row, 1))
    w_far.start()
    w_near = remote(w, wq_ref.at[1], sw.at[1], rw.at[1], (d, r, 0))
    flat = jnp.concatenate(
        [qb_ref[...].reshape(1, third), jnp.zeros((1, third), bf16), vb_ref[...].reshape(1, third)], axis=1
    )
    bias[...] = jnp.broadcast_to(flat.astype(f32), (8, 3 * third))
    b_far = remote(bias, biases.at[1], sb.at[0], rb.at[0], (d, far_row, 1))

    @pl.when(c == 0)
    def _():
        wq_ref[0] = w[...]
        b_far.start()

    @pl.when(c == 1)
    def _():
        w_near.start()

    biases[0] = bias[...]
    seq[...] = jnp.zeros_like(seq)
    seq[0:1, 0 : len_ref.shape[1]] = len_ref[...]
    seq[1:2, 0 : len_ref.shape[1]] = trim_ref[...]
    seq_cp = remote(seq, seqrx, sm.at[0], rm.at[0], core)
    seq_cp.start()

    core_cp, z_cp, core2_cp = [], [], []
    for k in range(n_dp):
        s = lax.rem(d - k + n_dp, n_dp)
        ref = xf_ref.at[half, c, rows(s), :]
        if k:
            sends[k - 1].wait_recv()
        a = remote(ref, ref, sz.at[k], rz.at[k], zdev)
        a.start()
        b = remote(ref, ref, sc.at[k], rc.at[k], core)
        b.start()
        z_cp.append(a)
        core_cp.append(b)

    pass_cp = []
    for k in range(3):
        share_cp[k].wait_recv()
        ref = wg_ref.at[lax.rem(r - k + 3, 4), my_share, :]
        for i, dev in enumerate(ring):
            cp = remote(ref, ref, sf.at[k, i], rf.at[k, i], dev)
            cp.start()
            pass_cp.append(cp)
        if k == 0:
            for dest in range(n_dp):
                pick = (col[dest * piece : (dest + 1) * piece, 0:1] == lane).astype(bf16)
                dys_ref[dest] = nn(pick, dy_ref[...]).astype(bf16)

    for k in range(n_dp):
        s = lax.rem(d - k + n_dp, n_dp)
        z_cp[k].wait_recv()
        ref = xf_ref.at[1 - half, c, rows(s), :]
        b = remote(ref, ref, sc2.at[k], rc2.at[k], core)
        b.start()
        core2_cp.append(b)

    @pl.when(c == 0)
    def _():
        w_near.wait_recv()
        b_far.wait_send()

    @pl.when(c == 1)
    def _():
        w_near.wait_send()
        b_far.wait_recv()
        remote(w, wq_ref.at[0], sw.at[0], rw.at[0], (d, far_row, 1)).wait_recv()
        remote(w, wq_ref.at[1], sw.at[0], rw.at[1], (d, far_row, 1)).wait_recv()

    w_far.wait_send()
    for k in range(n_dp):
        core_cp[k].wait_recv()
        core2_cp[k].wait_recv()
    stores = [
        pltpu.make_async_copy(xf_ref, xf_out, so.at[0]),
        pltpu.make_async_copy(wq_ref, wq_out, so.at[1]),
        pltpu.make_async_copy(dys_ref, dys_out, so.at[2]),
    ]
    for cp in stores:
        cp.start()
    brow = jnp.where(c == 0, biases[0], biases[1])[0:1, :]

    def project(i, carry):
        h = lax.div(i, 2)
        base = pl.ds(pl.multiple_of(lax.rem(i, 2) * 512, 512), 512)
        y = nt(xf_ref[h, 0, base, :], wq_ref[0]) + nt(xf_ref[h, 1, base, :], wq_ref[1]) + brow
        y = y.astype(bf16)
        out = pl.ds(pl.multiple_of(i * 512, 512), 512)
        qkv_ref[out, :] = y
        qkvt_ref[:, out] = y.T
        return carry

    lax.fori_loop(0, 4, project, 0)
    stores += [pltpu.make_async_copy(qkv_ref, qkv_out, so.at[3]), pltpu.make_async_copy(qkvt_ref, qkvt_out, so.at[4])]
    stores[3].start()
    stores[4].start()
    seq_cp.wait()
    is_mine = lax.div(r, 2) == c
    seqo_ref[...] = jnp.where(is_mine, seq[...], seqrx[...])
    for cp in pass_cp:
        cp.wait()
    for cp in sends + core_cp + z_cp + core2_cp + share_cp:
        cp.wait_send()
    for cp in stores:
        cp.wait()
    local_w.wait()


def deal_call(n_dp, rows_w, args):
    x, qw = args[0], args[3]
    tokens, wide = x.shape
    piece = tokens // n_dp
    cols = 3 * qw.shape[0]
    return pl.pallas_call(
        functools.partial(deal_kernel, n_dp, rows_w),
        out_shape=(
            sds((2, 2, tokens, wide), bf16),
            sds((n_dp, piece, wide), bf16),
            sds((2 * tokens, cols), bf16),
            sds((cols, 2 * tokens), bf16),
            sds((2, cols, wide), bf16),
            sds((8, 128), jnp.int32),
            sds((4, rows_w, wide), bf16),
        ),
        in_specs=[VM] * len(args),
        out_specs=(ANY,) * 5 + (VM, ANY),
        scratch_shapes=[
            pltpu.VMEM((2, 2, tokens, wide), bf16),
            pltpu.VMEM((n_dp, piece, wide), bf16),
            pltpu.VMEM((2 * tokens, cols), bf16),
            pltpu.VMEM((cols, 2 * tokens), bf16),
            pltpu.VMEM((2, cols, wide), bf16),
            DMA((5,)),
            pltpu.VMEM((n_dp, piece, wide), bf16),
            pltpu.VMEM((8, 128), jnp.int32),
            pltpu.VMEM((8, 128), jnp.int32),
            pltpu.VMEM((cols, wide), bf16),
            pltpu.VMEM((8, cols), f32),
            pltpu.VMEM((2, 8, cols), f32),
            pltpu.VMEM((rows_w, wide), bf16),
            pltpu.VMEM((tokens, 8), jnp.int32),
        ]
        + [DMA((n_dp,))] * 8
        + [DMA((2,))] * 6
        + [DMA((3,))] * 2
        + [DMA((3, n_dp - 1))] * 2
        + [DMA],
        compiler_params=pltpu.CompilerParams(
            collective_id=1, has_side_effects=True, vmem_limit_bytes=VMEM_LIMIT
        ),
        name="deal",
    )(*args)


def seq_bounds(seq_ref, n_seq):
    ends, total = [], 0
    for j in range(n_seq):
        total = total + seq_ref[0, j]
        ends.append(total)
    starts = [ends[j] - seq_ref[0, j] for j in range(n_seq)]
    lives = [starts[j] + jnp.maximum(seq_ref[0, j] - seq_ref[1, j], 1) for j in range(n_seq)]
    return starts, ends, lives


def block_range(first, last, starts, ends, block):
    lo, hi = 0, ends[-1]
    for j in range(len(ends)):
        lo = jnp.where((first >= starts[j]) & (first < ends[j]), starts[j], lo)
        hi = jnp.where((last >= starts[j]) & (last < ends[j]), ends[j], hi)
    return lax.div(lo, block), lax.div(hi + block - 1, block)


def key_columns(starts, ends, lives, length, extra):
    pos = lax.broadcasted_iota(jnp.int32, (length, HEAD), 0)
    lane = lax.broadcasted_iota(jnp.int32, (length, HEAD), 1)
    n_seq = len(ends)
    cols = jnp.where(lane < n_seq, FAR, 0.0)
    cols = jnp.where((lane >= n_seq) & (lane < n_seq + extra), -1.0, cols)
    for j in range(n_seq):
        live = (pos >= starts[j]) & (pos < lives[j]) & (lane == j)
        cols = jnp.where(live, 0.0, cols)
    return cols.astype(bf16)


def query_rows(starts, ends, length):
    pos = lax.broadcasted_iota(jnp.int32, (16, length), 1)
    row = lax.broadcasted_iota(jnp.int32, (16, length), 0)
    out = jnp.zeros((16, length), f32)
    for j in range(len(ends)):
        out = jnp.where((row == j) & (pos >= starts[j]) & (pos < ends[j]), 1.0, out)
    return out


def split_three(v):
    hi = v.astype(bf16).astype(f32)
    mid = (v - hi).astype(bf16).astype(f32)
    low = (v - hi - mid).astype(bf16).astype(f32)
    return hi, mid, low


def put_rows(base, values, first):
    row = lax.broadcasted_iota(jnp.int32, base.shape, 0)
    for i, v in enumerate(values):
        base = jnp.where(row == first + i, v, base)
    return base


def attend_kernel(n_seq, block, seq_ref, qkv_ref, qkvt_ref, ot_ref, lse_ref, kaug, qaug, vaug, acc, mx, sbuf):
    length = qkv_ref.shape[0]
    heads = qkv_ref.shape[1] // (3 * HEAD)
    width = heads * HEAD
    span = 2 * block
    starts, ends, lives = seq_bounds(seq_ref, n_seq)
    kcols = key_columns(starts, ends, lives, length, 0)
    qrows = query_rows(starts, ends, length)
    ones = (lax.broadcasted_iota(jnp.int32, (16, length), 0) == 0).astype(f32).astype(bf16)
    for h in range(heads):
        kaug[h, :, :HEAD] = qkv_ref[:, width + h * HEAD : width + (h + 1) * HEAD]
        kaug[h, :, HEAD:] = kcols
        qaug[h, :HEAD, :] = qkvt_ref[h * HEAD : (h + 1) * HEAD, :] * 0.125
        qaug[h, HEAD : HEAD + 16, :] = qrows.astype(bf16)
        qaug[h, HEAD + 16 :, :] = jnp.zeros((HEAD - 16, length), bf16)
        vaug[h, :HEAD, :] = qkvt_ref[2 * width + h * HEAD : 2 * width + (h + 1) * HEAD, :]
        vaug[h, HEAD:, :] = ones
    lse_ref[...] = jnp.zeros_like(lse_ref)

    def q_step(qb, carry):
        qs = pl.ds(pl.multiple_of(qb * block, block), block)
        lo, hi = block_range(qb * block, qb * block + block - 1, starts, ends, block)
        for h in range(heads):
            acc[h] = jnp.zeros((HEAD + 16, block), f32)
            mx[h] = jnp.full((8, block), 2 * FAR, f32)

        def max_step(size, i, inner):
            ks = pl.ds(pl.multiple_of((lo + 2 * i) * block, block), size)
            at = pl.ds(pl.multiple_of(i * span, span), size)
            ss = [nn(kaug[h, ks, :], qaug[h, :, qs]) for h in range(heads)]
            for h in range(heads):
                sbuf[h, at, :] = ss[h]
                mx[h] = jnp.maximum(mx[h], jnp.max(ss[h].reshape(size // 8, 8, block), axis=0))
            return inner

        pairs, odd = lax.div(hi - lo, 2), lax.rem(hi - lo, 2)
        lax.fori_loop(0, pairs, functools.partial(max_step, span), 0)
        lax.fori_loop(pairs, pairs + odd, functools.partial(max_step, block), 0)
        tops = []
        for h in range(heads):
            top = jnp.max(mx[h], axis=0, keepdims=True)
            tops.append(top)

        def sum_step(size, i, inner):
            ks = pl.ds(pl.multiple_of((lo + 2 * i) * block, block), size)
            at = pl.ds(pl.multiple_of(i * span, span), size)
            ps = [jnp.exp(sbuf[h, at, :] - tops[h]).astype(bf16) for h in range(heads)]
            for h in range(heads):
                acc[h] = acc[h] + nn(vaug[h, :, ks], ps[h])
            return inner

        lax.fori_loop(0, pairs, functools.partial(sum_step, span), 0)
        lax.fori_loop(pairs, pairs + odd, functools.partial(sum_step, block), 0)
        for h in range(heads):
            total = acc[h, HEAD : HEAD + 1, :]
            ot_ref[h * HEAD : (h + 1) * HEAD, qs] = (acc[h, :HEAD, :] / total).astype(bf16)
            lse_ref[h : h + 1, qs] = tops[h] + jnp.log(total)
        return carry

    lax.fori_loop(0, length // block, q_step, 0)


def attend_call(n_seq, seq, qkv, qkvt):
    length, cols = qkv.shape
    heads = cols // (3 * HEAD)
    block = 256
    return pl.pallas_call(
        functools.partial(attend_kernel, n_seq, block),
        out_shape=(sds((heads * HEAD, length), bf16), sds((8, length), f32)),
        in_specs=[SM, VM, VM],
        out_specs=(VM, VM),
        scratch_shapes=[
            pltpu.VMEM((heads, length, 2 * HEAD), bf16),
            pltpu.VMEM((heads, 2 * HEAD, length), bf16),
            pltpu.VMEM((heads, HEAD + 16, length), bf16),
            pltpu.VMEM((heads, HEAD + 16, block), f32),
            pltpu.VMEM((heads, 8, block), f32),
            pltpu.VMEM((heads, length, block), f32),
        ],
        compiler_params=pltpu.CompilerParams(vmem_limit_bytes=VMEM_LIMIT),
        cost_estimate=pl.CostEstimate(flops=4 * 10**9, bytes_accessed=6 * 10**6, transcendentals=10**7),
        name="attend",
    )(seq, qkv, qkvt)


def attend_back_kernel(
    n_seq, block, seq_ref, qkv_ref, qkvt_ref, dot_ref, ot_ref, lse_ref, dqkv_ref, dqkvt_ref,
    kaug, qaug, vaug, doaug, qn, don, dqt, dk, dv,
):
    length = qkv_ref.shape[0]
    heads = qkv_ref.shape[1] // (3 * HEAD)
    width = heads * HEAD
    starts, ends, lives = seq_bounds(seq_ref, n_seq)
    kcols = key_columns(starts, ends, lives, length, 3)
    lane = lax.broadcasted_iota(jnp.int32, (length, HEAD), 1)
    vcols = jnp.where(lane < 3, -1.0, 0.0).astype(bf16)
    qrows = query_rows(starts, ends, length)
    zero = jnp.zeros((HEAD - 16, length), bf16)
    span = 2 * block
    for h in range(heads):
        hs = slice(h * HEAD, (h + 1) * HEAD)
        kaug[h, :, :HEAD] = qkv_ref[:, width + h * HEAD : width + (h + 1) * HEAD]
        kaug[h, :, HEAD:] = kcols
        vaug[h, :, :HEAD] = qkv_ref[:, 2 * width + h * HEAD : 2 * width + (h + 1) * HEAD]
        vaug[h, :, HEAD:] = vcols
        qaug[h, :HEAD, :] = qkvt_ref[hs, :] * 0.125
        qaug[h, HEAD : HEAD + 16, :] = put_rows(qrows, split_three(lse_ref[h : h + 1, :]), n_seq).astype(bf16)
        qaug[h, HEAD + 16 :, :] = zero
        do = dot_ref[hs, :]
        delta = jnp.sum(do.astype(f32) * ot_ref[hs, :].astype(f32), axis=0, keepdims=True)
        doaug[h, :HEAD, :] = do
        doaug[h, HEAD : HEAD + 16, :] = put_rows(
            jnp.zeros((16, length), f32), split_three(delta), 0
        ).astype(bf16)
        doaug[h, HEAD + 16 :, :] = zero
        qn[h] = qkv_ref[:, hs] * 0.125
        don[h] = do.T
        dqt[h] = jnp.zeros((HEAD, length), f32)

    def k_step(kb, carry):
        ks = pl.ds(pl.multiple_of(kb * block, block), block)
        lo, hi = block_range(kb * block, kb * block + block - 1, starts, ends, block)
        dk[...] = jnp.zeros_like(dk)
        dv[...] = jnp.zeros_like(dv)

        def q_step(size, i, inner):
            qs = pl.ds(pl.multiple_of((lo + 2 * i) * block, block), size)
            for h in range(heads):
                p = jnp.exp(nn(kaug[h, ks, :], qaug[h, :, qs]))
                ds = (p * nn(vaug[h, ks, :], doaug[h, :, qs])).astype(bf16)
                dv[h] = dv[h] + nn(p.astype(bf16), don[h, qs, :])
                dk[h] = dk[h] + nn(ds, qn[h, qs, :])
                kt = qkvt_ref[width + h * HEAD : width + (h + 1) * HEAD, ks]
                dqt[h, :, qs] = dqt[h, :, qs] + nn(kt, ds)
            return inner

        pairs, odd = lax.div(hi - lo, 2), lax.rem(hi - lo, 2)
        lax.fori_loop(0, pairs, functools.partial(q_step, span), 0)
        lax.fori_loop(pairs, pairs + odd, functools.partial(q_step, block), 0)
        for h in range(heads):
            vk = dk[h].astype(bf16)
            vv = dv[h].astype(bf16)
            a, b = width + h * HEAD, 2 * width + h * HEAD
            dqkv_ref[ks, a : a + HEAD] = vk
            dqkv_ref[ks, b : b + HEAD] = vv
            dqkvt_ref[a : a + HEAD, ks] = vk.T
            dqkvt_ref[b : b + HEAD, ks] = vv.T
        return carry

    lax.fori_loop(0, length // block, k_step, 0)
    for h in range(heads):
        v = (dqt[h] * 0.125).astype(bf16)
        dqkvt_ref[h * HEAD : (h + 1) * HEAD, :] = v
        dqkv_ref[:, h * HEAD : (h + 1) * HEAD] = v.T


def attend_back_call(n_seq, seq, qkv, qkvt, dot, ot, lse):
    length, cols = qkv.shape
    heads = cols // (3 * HEAD)
    block = 256
    nat = pltpu.VMEM((heads, length, 2 * HEAD), bf16)
    tra = pltpu.VMEM((heads, 2 * HEAD, length), bf16)
    return pl.pallas_call(
        functools.partial(attend_back_kernel, n_seq, block),
        out_shape=(sds((length, cols), bf16), sds((cols, length), bf16)),
        in_specs=[SM] + [VM] * 5,
        out_specs=(VM, VM),
        scratch_shapes=[
            nat, tra, nat, tra,
            pltpu.VMEM((heads, length, HEAD), bf16),
            pltpu.VMEM((heads, length, HEAD), bf16),
            pltpu.VMEM((heads, HEAD, length), f32),
            pltpu.VMEM((heads, block, HEAD), f32),
            pltpu.VMEM((heads, block, HEAD), f32),
        ],
        compiler_params=pltpu.CompilerParams(vmem_limit_bytes=VMEM_LIMIT),
        cost_estimate=pl.CostEstimate(flops=10**10, bytes_accessed=12 * 10**6, transcendentals=10**7),
        name="attend_back",
    )(seq, qkv, qkvt, dot, ot, lse)


def levels(n_dp):
    n_in = 2 if n_dp < 16 else 4
    return n_in, n_dp // n_in


def shard_of(r, c):
    return lax.rem(r + 2 * c, 4)


def middle_kernel(
    n_dp, oin_ref, xf_any, dys_ref, w_ref, back_ref, dh1_ref, dout_ref, *rest
):
    n_in, n_out = levels(n_dp)
    a_refs, b_refs, rest = rest[:n_in], rest[n_in : n_in + n_out], rest[n_in + n_out :]
    middle_body(n_dp, oin_ref, xf_any, dys_ref, w_ref, back_ref, dh1_ref, dout_ref, a_refs, b_refs, *rest)


def middle_body(
    n_dp, oin_ref, xf_any, dys_ref, w_ref, back_ref, dh1_ref, dout_ref, a_refs, b_refs,
    xv, xsem, fin, s_a, r_a, dyin, dyb, ot_ref, dot_ref, wup, wdn, wo, vec, ub, hid, slope, dub, sums, gbuf, gin, facc, yacc,
    so, ro, sg, rg, lsem, wss, wrs, sgb, rgb, sgt, rgt, gsem, sd, rd, sm, rm,
):
    d, r, c = me()
    half = lax.rem(r, 2)
    wide = xf_any.shape[3]
    width = 2 * wide
    tok = dyb.shape[0]
    mine = pl.ds(pl.multiple_of(c * tok, tok), tok)
    x_cp = pltpu.make_async_copy(xf_any.at[half, :, mine, :], xv, xsem)
    x_cp.start()
    hrows = oin_ref.shape[0]
    core = (d, r, 1 - c)
    peers = [(d, flip(r), c), (d, flip(r), 1 - c), core]
    ring = [(lax.rem(d + k, n_dp), r, c) for k in range(1, n_dp)]
    greet(peers + ring + [(dev[0], r, 1 - c) for dev in ring])
    base = r - half
    shard = shard_of(r, c)
    o_cp = []
    for i, dev in enumerate(peers):
        q = (dev[1] - base) * 2 + dev[2]
        src = oin_ref.at[:, pl.ds(pl.multiple_of(q * tok, tok), tok)]
        cp = remote(src, ot_ref.at[shard], so.at[i], ro.at[i], dev)
        cp.start()
        o_cp.append(cp)
    myq = pl.ds(pl.multiple_of((half * 2 + c) * tok, tok), tok)
    ot_ref[shard] = oin_ref[:, myq]

    piece = dys_ref.shape[1]
    here = pl.ds(pl.multiple_of(d * piece, piece), piece)
    d_cp = []
    for k, dev in enumerate(ring):
        cp = remote(dys_ref.at[dev[0]], dyin.at[here, :], sd.at[k], rd.at[k], dev)
        cp.start()
        d_cp.append(cp)
    dyin[here, :] = dys_ref[d]

    loads = [[], [], []]
    mycols = pl.ds(pl.multiple_of(c * wide, 128), wide)
    for j in range(4):
        js = slice(j * hrows, (j + 1) * hrows)
        loads[0].append((w_ref.at[j, OUT:VEC], wo.at[js, mycols]))
        loads[0].append((w_ref.at[j, VEC : VEC + 16], ub.at[j, c]))
        for h in range(2):
            hs = slice(h * wide, (h + 1) * wide)
            loads[1].append((w_ref.at[j, hs], wup.at[j, mycols, hs]))
        loads[2].append((w_ref.at[j, DOWN:OUT], wdn.at[j, :, mycols]))
    w_cps = []
    for i, group in enumerate(loads):
        cps = []
        for k, (src, dst) in enumerate(group):
            a = pltpu.make_async_copy(src, dst, lsem.at[i, k])
            a.start()
            b = remote(src, dst, wss.at[i, k], wrs.at[i, k], core)
            b.start()
            cps += [a, b]
        w_cps.append(cps)

    def settle(i):
        for cp in w_cps[i]:
            cp.wait()

    for cp in o_cp:
        cp.wait_recv()
    x_cp.wait()
    x = jnp.concatenate([xv[0], xv[1]], axis=1).astype(f32)
    settle(0)
    vec[...] = jnp.concatenate([ub[0, 0], ub[0, 1]], axis=1)
    ob, g1, s1, db, g2, s2 = [vec[i : i + 1, :].astype(f32) for i in range(6)]
    o = ot_ref[...].reshape(width, tok).T
    h1 = x + (nn(o, wo[...]) + ob)
    mu = jnp.mean(h1, axis=1, keepdims=True)
    r1 = lax.rsqrt(jnp.mean(h1 * h1, axis=1, keepdims=True) - mu * mu + EPS)
    n1 = (h1 - mu) * r1
    y1 = (n1 * g1 + s1).astype(bf16)
    for cp in d_cp:
        cp.wait_recv()
    theirs = pl.ds(pl.multiple_of((1 - c) * tok, tok), tok)
    dy_cp = remote(dyin.at[theirs, :], dyb, sm, rm, core)
    dy_cp.start()
    settle(1)
    settle(2)
    facc[...] = jnp.zeros_like(facc)

    def ahead(j, carry):
        bias = jnp.concatenate([ub[j, 0, 6:7, :], ub[j, 0, 7:8, :]], axis=1).astype(f32)
        u = nn(y1, wup[j]) + bias
        cdf = 0.5 * (1.0 + lax.erf(u * INV_ROOT_TWO))
        hj = (u * cdf).astype(bf16)
        hid[j] = hj
        slope[j] = cdf + u * jnp.exp(-0.5 * u * u) * INV_ROOT_TAU
        facc[...] += nn(hj, wdn[j])
        return carry

    lax.fori_loop(0, 4, ahead, 0)
    h2 = y1.astype(f32) + (facc[...] + db)
    mu2 = jnp.mean(h2, axis=1, keepdims=True)
    r2 = lax.rsqrt(jnp.mean(h2 * h2, axis=1, keepdims=True) - mu2 * mu2 + EPS)
    n2 = (h2 - mu2) * r2
    res = (n2 * g2 + s2).astype(bf16)
    fin[0] = res[:, :wide]
    fin[1] = res[:, wide:]
    send_back(n_dp, fin, back_ref, s_a, r_a)
    dy_cp.wait_recv()
    own, other = dyin[mine, :], dyb[...]
    left = jnp.where(c == 0, own, other)
    right = jnp.where(c == 0, other, own)
    dy = jnp.concatenate([left, right], axis=1).astype(f32)
    e2 = dy * g2
    dh2 = r2 * (e2 - jnp.mean(e2, axis=1, keepdims=True) - n2 * jnp.mean(e2 * n2, axis=1, keepdims=True))
    g2g = jnp.sum(dy * n2, axis=0, keepdims=True)
    s2g = jnp.sum(dy, axis=0, keepdims=True)
    df = dh2.astype(bf16)
    dbg = jnp.sum(df.astype(f32), axis=0, keepdims=True)
    yacc[...] = dh2
    def big_cp(j):
        return remote(gbuf.at[j, 1 - c, 0:OUT], gin.at[j, 0:OUT], sgb.at[j], rgb.at[j], core)

    def back(j, carry):
        du = (nt(df, wdn[j]) * slope[j]).astype(bf16)
        dub[j] = du
        sums[j] = jnp.broadcast_to(jnp.sum(du.astype(f32), axis=0, keepdims=True), (8, width))
        yacc[...] += nt(du, wup[j])
        return carry

    lax.fori_loop(0, 4, back, 0)
    dy1 = yacc[...]
    e1 = dy1 * g1
    dh1 = r1 * (e1 - jnp.mean(e1, axis=1, keepdims=True) - n1 * jnp.mean(e1 * n1, axis=1, keepdims=True))
    dh1_ref[...] = dh1
    g1g = jnp.sum(dy1 * n1, axis=0, keepdims=True)
    s1g = jnp.sum(dy1, axis=0, keepdims=True)
    da = dh1.astype(bf16)
    obg = jnp.sum(da.astype(f32), axis=0, keepdims=True)
    dot_ref[...] = nt(da, wo[...]).T.astype(bf16).reshape(dot_ref.shape)
    g_cp = []
    for i, dev in enumerate(peers):
        cp = remote(dot_ref.at[shard_of(dev[1], dev[2])], dout_ref.at[:, myq], sg.at[i], rg.at[i], dev)
        cp.start()
        g_cp.append(cp)
    dout_ref[:, myq] = dot_ref[shard]
    y1t = y1.T

    def grads(j, carry):
        gd = tn(hid[j], df).astype(bf16)
        gu = nn(y1t, dub[j]).astype(bf16)
        for cc in range(2):
            cs = slice(cc * wide, (cc + 1) * wide)
            for h in range(2):
                gbuf[j, cc, h * wide : (h + 1) * wide, :] = gu[cs, h * wide : (h + 1) * wide]
            gbuf[j, cc, DOWN:OUT, :] = gd[:, cs]
        big_cp(j).start()
        return carry

    lax.fori_loop(0, 4, grads, 0)
    go = nn(ot_ref[...].reshape(width, tok), da).astype(bf16)
    pad = gbuf.shape[2] - VEC
    row = lax.broadcasted_iota(jnp.int32, (pad, wide), 0)
    t_cp = []
    for j in range(4):
        for cc in range(2):
            cs = slice(cc * wide, (cc + 1) * wide)
            gbuf[j, cc, OUT:VEC, :] = go[j * hrows : (j + 1) * hrows, cs]
            tail = jnp.zeros((pad, wide), f32)
            for i, v in enumerate((obg, g1g, s1g, dbg, g2g, s2g)):
                tail = jnp.where(row == i, v[:, cs], tail)
            tail = jnp.where(row == 6, sums[j, 0:1, :wide], tail)
            tail = jnp.where(row == 7, sums[j, 0:1, wide:], tail)
            gbuf[j, cc, VEC:, :] = tail.astype(bf16)
        cp = remote(gbuf.at[j, 1 - c, OUT:], gin.at[j, OUT:], sgt.at[j], rgt.at[j], core)
        cp.start()
        t_cp.append(cp)
    rows_q = gbuf.shape[2] // n_dp
    n_in, n_out = levels(n_dp)
    outs = []
    for j in range(4):
        big_cp(j).wait()
        t_cp[j].wait()
        gin[j] = (gin[j].astype(f32) + gbuf[j, c].astype(f32)).astype(bf16)
        n_first, n_second, refs = (n_in, n_out, a_refs) if j < 2 else (n_out, n_in, b_refs)
        for k in range(n_first):
            for m in range(n_second):
                if j < 2:
                    s = m * n_in + lax.rem(lax.rem(d, n_in) + k, n_in)
                else:
                    s = lax.rem(lax.div(d, n_in) + k, n_out) * n_in + m
                span = pl.ds(pl.multiple_of(s * rows_q, rows_q), rows_q)
                cp = pltpu.make_async_copy(gin.at[j, span], refs[k].at[m, j % 2], gsem.at[j, k * n_second + m])
                cp.start()
                outs.append(cp)
    got_back(n_dp, fin, back_ref, s_a, r_a)
    sent_back(n_dp, fin, back_ref, s_a, r_a)
    for cp in o_cp + d_cp + [dy_cp]:
        cp.wait_send()
    for cp in g_cp + outs:
        cp.wait()


def middle_call(n_dp, oin, xf, dys, w, g_rows):
    tok, wide = xf.shape[2] // 2, xf.shape[3]
    width = 2 * wide
    hrows = oin.shape[0]
    n_in, n_out = levels(n_dp)
    return pl.pallas_call(
        functools.partial(middle_kernel, n_dp),
        out_shape=(
            sds((2 * tok, wide), bf16),
            sds((tok, width), f32),
            sds((hrows, 4 * tok), bf16),
        )
        + (sds((n_out, 2, g_rows // n_dp, wide), bf16),) * n_in
        + (sds((n_in, 2, g_rows // n_dp, wide), bf16),) * n_out,
        in_specs=[VM, ANY, VM, ANY],
        out_specs=(VM, VM, VM) + (ANY,) * (n_in + n_out),
        scratch_shapes=[
            pltpu.VMEM((2, tok, wide), bf16),
            DMA,
            pltpu.VMEM((2, tok, wide), bf16),
            DMA((n_dp // 2, 2)), DMA((n_dp,)),
            pltpu.VMEM((2 * tok, wide), bf16),
            pltpu.VMEM((tok, wide), bf16),
            pltpu.VMEM((4, hrows, tok), bf16),
            pltpu.VMEM((4, hrows, tok), bf16),
            pltpu.VMEM((4, width, width), bf16),
            pltpu.VMEM((4, width, width), bf16),
            pltpu.VMEM((width, width), bf16),
            pltpu.VMEM((16, width), bf16),
            pltpu.VMEM((4, 2, 16, wide), bf16),
            pltpu.VMEM((4, tok, width), bf16),
            pltpu.VMEM((4, tok, width), f32),
            pltpu.VMEM((4, tok, width), bf16),
            pltpu.VMEM((4, 8, width), f32),
            pltpu.VMEM((4, 2, g_rows, wide), bf16),
            pltpu.VMEM((4, g_rows, wide), bf16),
            pltpu.VMEM((tok, width), f32),
            pltpu.VMEM((tok, width), f32),
            DMA((3,)), DMA((3,)), DMA((3,)), DMA((3,)),
            DMA((3, 8)), DMA((3, 8)), DMA((3, 8)),
            DMA((4,)), DMA((4,)), DMA((4,)), DMA((4,)),
            DMA((4, n_dp)), DMA((n_dp,)), DMA((n_dp,)), DMA, DMA,
        ],
        compiler_params=pltpu.CompilerParams(
            collective_id=2, has_side_effects=True, vmem_limit_bytes=VMEM_LIMIT
        ),
        cost_estimate=pl.CostEstimate(flops=16 * 10**9, bytes_accessed=30 * 10**6, transcendentals=4 * 10**6),
        name="middle",
    )(oin, xf, dys, w)


def return_kernel(n_dp, dqkv_ref, dqkvt_ref, wq_any, xf_any, dh1_any, *rest):
    n_in, n_out = levels(n_dp)
    a_parts, b_parts, rest = rest[:n_in], rest[n_in : n_in + n_out], rest[n_in + n_out :]
    return_body(n_dp, dqkv_ref, dqkvt_ref, wq_any, xf_any, dh1_any, a_parts, b_parts, *rest)


def return_body(
    n_dp, dqkv_ref, dqkvt_ref, wq_any, xf_any, dh1_any, a_parts, b_parts,
    back_ref, gout_ref, gall_ref,
    wq, xf, dh1, apart, bpart, lsem,
    asum, bsum, ain, bin_, rsum, zin, rfin, fin, tocore, fromcore, toz, fromz, gq_ref, gqin, gsum, xq, gfin,
    s_1, r_1, s_2, r_2, s_r, r_r, s_t, r_t, s_b, r_b, s_c, r_c, s_z, r_z, s_q, r_q, s_x, r_x, s_g, r_g,
):
    d, r, c = me()
    n_in, n_out = levels(n_dp)
    o, i = lax.div(d, n_in), lax.rem(d, n_in)
    half = lax.rem(r, 2)
    tok, width = dh1_any.shape
    wide = width // 2
    core = (d, r, 1 - c)
    zdev = (d, flip(r), c)
    far_row = lax.rem(r + 2, 4)
    rows_dev = [(d, lax.rem(r + k, 4), c) for k in (1, 2, 3)]
    loads = [pltpu.make_async_copy(wq_any, wq, lsem.at[0])]
    for k in range(n_in):
        loads.append(pltpu.make_async_copy(a_parts[k], apart.at[k], lsem.at[3 + k]))
    for k in range(n_out):
        loads.append(pltpu.make_async_copy(b_parts[k], bpart.at[k], lsem.at[3 + n_in + k]))
    loads.append(pltpu.make_async_copy(dh1_any, dh1, lsem.at[1]))
    loads.append(pltpu.make_async_copy(xf_any, xf, lsem.at[2]))
    for cp in loads:
        cp.start()
    peers = [(lax.rem(d + k, n_dp), r, cc) for k in range(1, n_dp) for cc in (0, 1)]
    greet(peers + rows_dev + [core, (d, far_row, 1 - c)])

    def part(h, cc):
        q = h * 2 + cc
        rows = dqkv_ref[pl.ds(pl.multiple_of(q * tok, tok), tok), :]
        return jnp.concatenate([nn(rows, wq[0]), nn(rows, wq[1])], axis=1)

    loads[0].wait()
    tocore[0] = part(1 - half, 1 - c).astype(bf16)
    cp_far = remote(tocore.at[0], fromcore.at[0], s_c.at[0], r_c.at[0], core)
    cp_far.start()

    for cp in loads[1:-2]:
        cp.wait()
    n_ch = s_r.shape[1]
    chunk = rsum.shape[1] // n_ch
    a_cp, b_cp = [], []
    for t in range(n_ch):
        ts = slice(t * chunk, (t + 1) * chunk)
        total = apart[0, :, :, ts].astype(f32)
        for k in range(1, n_in):
            total = total + apart[k, :, :, ts].astype(f32)
        asum[:, :, ts] = total.astype(bf16)
        total = bpart[0, :, :, ts].astype(f32)
        for k in range(1, n_out):
            total = total + bpart[k, :, :, ts].astype(f32)
        bsum[:, :, ts] = total.astype(bf16)
        for k in range(1, n_out):
            dest = lax.rem(o + k, n_out)
            cp = remote(
                asum.at[dest, :, ts], ain.at[k, :, ts], s_1.at[k, t], r_1.at[k, t], (dest * n_in + i, r, c)
            )
            cp.start()
            a_cp.append(cp)
        for k in range(1, n_in):
            dest = lax.rem(i + k, n_in)
            cp = remote(
                bsum.at[dest, :, ts], bin_.at[k, :, ts], s_2.at[k, t], r_2.at[k, t], (o * n_in + dest, r, c)
            )
            cp.start()
            b_cp.append(cp)

    far = part(1 - half, c)
    cp_far.wait_recv()
    toz[...] = (far + fromcore[0].astype(f32)).astype(bf16)
    cp_z = remote(toz, fromz, s_z, r_z, zdev)
    cp_z.start()

    row_cp = []

    def to_rows(t):
        ts = slice(t * chunk, (t + 1) * chunk)
        total = asum[o, :, ts].astype(f32)
        for k in range(1, n_out):
            a_cp[t * (n_out - 1) + k - 1].wait_recv()
            total = total + ain[k, :, ts].astype(f32)
        rsum[0:2, ts] = total.astype(bf16)
        total = bsum[i, :, ts].astype(f32)
        for k in range(1, n_in):
            b_cp[t * (n_in - 1) + k - 1].wait_recv()
            total = total + bin_[k, :, ts].astype(f32)
        rsum[2:4, ts] = total.astype(bf16)
        for k, dev in enumerate(rows_dev):
            cp = remote(rsum.at[dev[1], ts], zin.at[k, ts], s_r.at[k, t], r_r.at[k, t], dev)
            cp.start()
            row_cp.append(cp)

    to_rows(0)

    n_cols, length = dqkvt_ref.shape
    loads[-1].wait()
    for f in range(2):
        g = nn(dqkvt_ref[:, : length // 2], xf[0, f]) + nn(dqkvt_ref[:, length // 2 :], xf[1, f])
        gq_ref[f, :n_cols, :] = g.astype(bf16)
        to_rows(1 + f)
    third = n_cols // 3
    sums = jnp.sum(dqkv_ref[...].astype(f32), axis=0, keepdims=True)
    bias = jnp.concatenate([sums[:, :third], sums[:, 2 * third :]], axis=1)
    pad = gq_ref.shape[1] - n_cols
    row = lax.broadcasted_iota(jnp.int32, (pad, wide), 0)
    tail = jnp.where(row == 0, bias, 0.0).astype(bf16)
    for f in range(2):
        gq_ref[f, n_cols:, :] = tail
    rq = gq_ref.shape[1] // n_dp

    def quarter(s):
        return pl.ds(pl.multiple_of(s * rq, rq), rq)

    q_cp = []
    for k in range(1, n_dp):
        dest = lax.rem(d + k, n_dp)
        cp = remote(gq_ref.at[:, quarter(dest), :], gqin.at[k], s_q.at[k], r_q.at[k], (dest, r, c))
        cp.start()
        q_cp.append(cp)

    tocore[1] = part(half, 1 - c).astype(bf16)
    cp_near = remote(tocore.at[1], fromcore.at[1], s_c.at[1], r_c.at[1], core)
    cp_near.start()

    for t in range(3, n_ch):
        to_rows(t)

    loads[-2].wait()
    total = part(half, c) + dh1[...]
    cp_near.wait_recv()
    total = total + fromcore[1].astype(f32)

    acc = gq_ref[:, quarter(d), :].astype(f32)
    for k in range(1, n_dp):
        q_cp[k - 1].wait_recv()
        acc = acc + gqin[k].astype(f32)
    gsum[...] = acc.astype(bf16)
    to_one = remote(gsum.at[1], xq.at[1], s_x.at[1], r_x.at[1], (d, r, 1))
    far_0 = remote(gsum.at[0], xq.at[0], s_x.at[0], r_x.at[0], (d, far_row, 0))
    far_1 = remote(gsum.at[1], xq.at[0], s_x.at[1], r_x.at[0], (d, far_row, 1))

    @pl.when(c == 0)
    def _():
        to_one.start()

    @pl.when(c == 1)
    def _():
        far_0.start()
        far_1.start()

    cp_z.wait_recv()
    total = (total + fromz[...].astype(f32)).astype(bf16)
    fin[0] = total[:, :wide]
    fin[1] = total[:, wide:]
    send_back(n_dp, fin, back_ref, s_b, r_b)

    n_keep = rfin.shape[0]
    t_cp = []
    for t in range(n_ch):
        ts = slice(t * chunk, (t + 1) * chunk)
        held = rsum[r, ts].astype(f32)
        for k in range(3):
            row_cp[t * 3 + k].wait_recv()
            held = held + zin[k, ts].astype(f32)
        rfin[ts] = held.astype(bf16)
        keep = pl.ds(pl.multiple_of(d * n_keep + t * chunk, chunk), chunk)
        gall_ref[keep, :] = rfin[ts]
        for k in range(1, n_dp):
            dest = lax.rem(d + k, n_dp)
            cp = remote(rfin.at[ts], gall_ref.at[keep, :], s_t.at[k, t], r_t.at[k, t], (dest, r, c))
            cp.start()
            t_cp.append(cp)

    far_0.wait_recv()

    @pl.when(c == 0)
    def _():
        gfin[...] = (gsum[0].astype(f32) + xq[0].astype(f32)).astype(bf16)

    @pl.when(c == 1)
    def _():
        to_one.wait_recv()
        gfin[...] = (xq[0].astype(f32) + xq[1].astype(f32)).astype(bf16)

    for k in range(1, n_dp):
        dest = lax.rem(d + k, n_dp)
        cp = remote(gfin, gout_ref.at[quarter(d), :], s_g.at[k], r_g.at[k], (dest, r, c))
        cp.start()
        t_cp.append(cp)
    gout_ref[quarter(d), :] = gfin[...]
    got_back(n_dp, fin, back_ref, s_b, r_b)
    sent_back(n_dp, fin, back_ref, s_b, r_b)
    for cp in [cp_far, cp_near, cp_z] + q_cp + a_cp + b_cp + row_cp:
        cp.wait_send()
    for cp in t_cp:
        cp.wait()

    @pl.when(c == 0)
    def _():
        to_one.wait_send()

    @pl.when(c == 1)
    def _():
        far_0.wait_send()
        far_1.wait_send()


def return_call(n_dp, dqkv, dqkvt, wq, xf, dh1, a_parts, b_parts, gq_rows):
    n_in, n_out = levels(n_dp)
    tok, width = dh1.shape
    wide = width // 2
    share = a_parts[0].shape[2]
    tokens = 2 * tok

    def vm(*shape):
        return pltpu.VMEM(shape, bf16)

    return pl.pallas_call(
        functools.partial(return_kernel, n_dp),
        out_shape=(sds((tokens, wide), bf16), sds((gq_rows, wide), bf16), sds((n_dp * share, wide), bf16)),
        in_specs=[VM, VM] + [ANY] * (3 + n_in + n_out),
        out_specs=(VM,) * 3,
        scratch_shapes=[
            vm(*wq.shape), vm(*xf.shape), pltpu.VMEM(dh1.shape, f32),
            vm(n_in, n_out, 2, share, wide), vm(n_out, n_in, 2, share, wide), DMA((3 + n_in + n_out,)),
            vm(n_out, 2, share, wide), vm(n_in, 2, share, wide), vm(n_out, 2, share, wide), vm(n_in, 2, share, wide),
            vm(4, share, wide), vm(3, share, wide), vm(share, wide),
            vm(2, tok, wide), vm(2, tok, width), vm(2, tok, width), vm(tok, width), vm(tok, width),
            vm(2, gq_rows, wide), vm(n_dp, 2, gq_rows // n_dp, wide), vm(2, gq_rows // n_dp, wide),
            vm(2, gq_rows // n_dp, wide), vm(gq_rows // n_dp, wide),
            DMA((n_out, 4)), DMA((n_out, 4)), DMA((n_in, 4)), DMA((n_in, 4)),
            DMA((3, 4)), DMA((3, 4)), DMA((n_dp, 4)), DMA((n_dp, 4)),
            DMA((n_dp // 2, 2)), DMA((n_dp,)),
            DMA((2,)), DMA((2,)), DMA, DMA,
            DMA((n_dp,)), DMA((n_dp,)), DMA((2,)), DMA((2,)), DMA((n_dp,)), DMA((n_dp,)),
        ],
        compiler_params=pltpu.CompilerParams(
            collective_id=4, has_side_effects=True, vmem_limit_bytes=VMEM_LIMIT
        ),
        name="return",
    )(dqkv, dqkvt, wq, xf, dh1, *a_parts, *b_parts)


def finish_kernel(
    a_ref, b_ref, deal_ref, g_ref, q_ref,
    out_ref, ig_ref, qw_ref, qb_ref, kw_ref, vw_ref, vb_ref, ow_ref, ob_ref, g1_ref, s1_ref, up_ref, ub_ref, dn_ref,
    db_ref, g2_ref, s2_ref,
):
    tokens, wide = a_ref.shape
    third = qw_ref.shape[0]
    place = (lax.broadcasted_iota(jnp.int32, (tokens, tokens), 0) == deal_ref[...]).astype(bf16)
    out_ref[...] = nn(place, a_ref[...]).astype(bf16)
    ig_ref[...] = nn(place, b_ref[...]).astype(bf16)
    qw_ref[...] = q_ref[:third, :].astype(f32)
    kw_ref[...] = q_ref[third : 2 * third, :].astype(f32)
    vw_ref[...] = q_ref[2 * third : 3 * third, :].astype(f32)
    bias = q_ref[3 * third : 3 * third + 16, :].astype(f32)[0:1]
    qb_ref[...] = bias[0, :third]
    vb_ref[...] = bias[0, third:]
    up_ref[:, :wide] = g_ref[:wide, :].astype(f32)
    up_ref[:, wide:] = g_ref[wide : 2 * wide, :].astype(f32)
    dn_ref[...] = g_ref[DOWN:OUT, :].astype(f32)
    ow_ref[...] = g_ref[OUT:VEC, :].astype(f32)
    vec = g_ref[VEC : VEC + 16, :].astype(f32)
    for i, ref in enumerate((ob_ref, g1_ref, s1_ref, db_ref, g2_ref, s2_ref)):
        ref[...] = vec[i]
    ub_ref[0:wide] = vec[6]
    ub_ref[wide : 2 * wide] = vec[7]


def finish_call(back_a, back_b, deal, gall, gq, third):
    tokens, wide = back_a.shape
    one = sds((wide,), f32)
    row = sds((third,), f32)
    head = sds((third, wide), f32)
    tok = sds((tokens, wide), bf16)
    return pl.pallas_call(
        finish_kernel,
        out_shape=(
            tok, tok, head, row, head, head, row, head, one, one, one, sds((wide, 2 * wide), f32),
            sds((2 * wide,), f32), sds((2 * wide, wide), f32), one, one, one,
        ),
        in_specs=[VM] * 5,
        out_specs=(VM,) * 17,
        compiler_params=pltpu.CompilerParams(vmem_limit_bytes=VMEM_LIMIT),
        name="finish",
    )(back_a, back_b, deal, gall, gq)


def round_up(v, m):
    return (v + m - 1) // m * m


def on_device(
    n_dp, inputs, out_grad, deal, seq_lengths, key_trim, query_weight, query_bias, key_weight,
    value_weight, value_bias, out_weight, out_bias, first_gain, first_shift, up_weight, up_bias,
    down_weight, down_bias, second_gain, second_shift,
):
    wide = inputs.shape[1]
    n_seq = seq_lengths.shape[1]
    step = 16 * n_dp
    third = query_weight.shape[1]
    rows_w = round_up(VEC + 16, step)
    xf, dys, qkv, qkvt, wq, seq, wg = deal_call(
        n_dp, rows_w,
        (
            inputs, out_grad, deal, query_weight.T, key_weight.T, value_weight.T, query_bias, value_bias, up_weight,
            down_weight, out_weight, out_bias, first_gain, first_shift, down_bias, second_gain, second_shift, up_bias,
            seq_lengths, key_trim,
        ),
    )
    ot, lse = attend_call(n_seq, seq, qkv, qkvt)
    back_a, dh1, dot, *grads = middle_call(n_dp, ot, xf, dys, wg, rows_w)
    n_in, n_out = levels(n_dp)
    a_parts, b_parts = grads[:n_in], grads[n_in:]
    for k in range(1, n_in):
        a_parts[k] = lax.ppermute(
            a_parts[k], "dp", [(o * n_in + i, o * n_in + (i + k) % n_in) for o in range(n_out) for i in range(n_in)]
        )
    for k in range(1, n_out):
        b_parts[k] = lax.ppermute(
            b_parts[k], "dp", [(o * n_in + i, (o + k) % n_out * n_in + i) for o in range(n_out) for i in range(n_in)]
        )
    dqkv, dqkvt = attend_back_call(n_seq, seq, qkv, qkvt, dot, ot, lse)
    gq_rows = round_up(3 * third + 16, step)
    back_b, gq, gall = return_call(n_dp, dqkv, dqkvt, wq, xf, dh1, a_parts, b_parts, gq_rows)
    outs = list(finish_call(back_a, back_b, deal, gall, gq, third))
    for i in (2, 4, 5):
        outs[i] = outs[i].T
    return tuple(outs)


def solution(mesh):
    n_dp = mesh.shape["dp"]
    tok = P(("dp", "row"), "col")
    one = P("col")
    row = P("row")
    a = P("col", "row")
    b = P("row", "col")
    seqs = P(("dp", "col"), None)
    in_specs = (
        tok, tok, P(("dp", "row"), None), seqs, seqs, a, row, a, a, row, b, one, one, one, a, row, b, one, one, one,
    )
    out_specs = (tok, tok, a, row, a, a, row, b, one, one, one, a, row, b, one, one, one)
    return jax.shard_map(
        functools.partial(on_device, n_dp), mesh=mesh, in_specs=in_specs, out_specs=out_specs, check_vma=False
    )
```

```python
import functools

import jax
import jax.numpy as jnp
from jax import lax
from jax.experimental import pallas as pl
from jax.experimental.pallas import tpu as pltpu
from jax.sharding import PartitionSpec as P

MESH = pl.DeviceIdType.MESH
f32 = jnp.float32
bf16 = jnp.bfloat16

HEAD = 64
EPS = 1e-05
FAR = -1e30
INV_ROOT_TWO = 0.7071067811865476
INV_ROOT_TAU = 0.3989422804014327
VMEM_LIMIT = 62 * 1024 * 1024
DOWN, OUT, VEC = 768, 1536, 1728

VM = pl.BlockSpec(memory_space=pltpu.VMEM)
SM = pl.BlockSpec(memory_space=pltpu.SMEM)
ANY = pl.BlockSpec(memory_space=pl.ANY)
DMA = pltpu.SemaphoreType.DMA


def nn(a, b):
    return lax.dot_general(a, b, (((1,), (0,)), ((), ())), preferred_element_type=f32)


def nt(a, b):
    return lax.dot_general(a, b, (((1,), (1,)), ((), ())), preferred_element_type=f32)


def tn(a, b):
    return lax.dot_general(a, b, (((0,), (0,)), ((), ())), preferred_element_type=f32)


def sds(shape, dtype):
    return jax.ShapeDtypeStruct(shape, dtype)


def me():
    return lax.axis_index("dp"), lax.axis_index("row"), lax.axis_index("col")


def flip(v):
    return v + 1 - 2 * lax.rem(v, 2)


def remote(src, dst, ssem, rsem, dev):
    return pltpu.make_async_remote_copy(
        src_ref=src, dst_ref=dst, send_sem=ssem, recv_sem=rsem, device_id=dev, device_id_type=MESH
    )


def greet(devs):
    barrier = pltpu.get_barrier_semaphore()
    for dev in devs:
        pl.semaphore_signal(barrier, inc=1, device_id=dev, device_id_type=MESH)
    pl.semaphore_wait(barrier, len(devs))


def send_back(n_dp, src, back, ss, rs):
    d, r, c = me()
    n_half = n_dp // 2
    piece = back.shape[0] // n_dp
    here = pl.ds(pl.multiple_of(d * piece, piece), piece)
    for i in range(n_half):
        s = c * n_half + i
        for cc in range(2):
            ref = src.at[cc, i * piece : (i + 1) * piece, :]
            cp = remote(ref, back.at[here, :], ss.at[i, cc], rs.at[d], (s, r, cc))
            local = (s == d) & (c == cc)

            @pl.when(jnp.logical_not(local))
            def _():
                cp.start()

            @pl.when(local)
            def _():
                back[here, :] = src[cc, i * piece : (i + 1) * piece, :]


def sent_back(n_dp, src, back, ss, rs):
    d, r, c = me()
    n_half = n_dp // 2
    piece = back.shape[0] // n_dp
    for i in range(n_half):
        s = c * n_half + i
        for cc in range(2):
            ref = src.at[cc, i * piece : (i + 1) * piece, :]

            @pl.when(jnp.logical_not((s == d) & (c == cc)))
            def _():
                remote(ref, back.at[0:piece, :], ss.at[i, cc], rs.at[0], (s, r, cc)).wait_send()


def got_back(n_dp, src, back, ss, rs):
    d, r, c = me()
    holder = lax.div(d, n_dp // 2)
    piece = back.shape[0] // n_dp
    for g in range(n_dp):

        @pl.when(jnp.logical_not((d == g) & (holder == c)))
        def _():
            remote(
                src.at[0, 0:piece, :], back.at[g * piece : (g + 1) * piece, :], ss.at[0, 0], rs.at[g], (d, r, 1 - c)
            ).wait_recv()


def levels(n_dp):
    n_in = 2 if n_dp < 16 else 4
    return n_in, n_dp // n_in


class Fan:
    def __init__(self, n_dp, piece, sems, outer_first):
        self.n_in, self.n_out = levels(n_dp)
        d, self.r, self.c = me()
        self.o, self.i = lax.div(d, self.n_in), lax.rem(d, self.n_in)
        self.piece, self.outer_first = piece, outer_first
        self.sems = sems

    def out(self, m):
        return lax.rem(self.o + m + self.n_out, self.n_out)

    def inn(self, m):
        return lax.rem(self.i + m + self.n_in, self.n_in)

    def at(self, o, i):
        return self.piece(o * self.n_in + i)

    def own(self, which, m):
        ref = self.at(self.o, self.i)
        ss, rs = self.sems[which]
        dev = (self.out(m), self.i) if which == 0 else (self.o, self.inn(m))
        return remote(ref, ref, ss.at[m], rs.at[m], (dev[0] * self.n_in + dev[1], self.r, self.c))

    def passed(self, mo, mi, outer_first):
        ss, rs = self.sems[2]
        if outer_first:
            ref, dev = self.at(self.out(-mo), self.i), (self.o, self.inn(mi))
        else:
            ref, dev = self.at(self.o, self.inn(-mi)), (self.out(mo), self.i)
        return remote(ref, ref, ss.at[mo, mi], rs.at[mo, mi], (dev[0] * self.n_in + dev[1], self.r, self.c))

    def counts(self):
        return range(1, self.n_out), range(1, self.n_in)

    def send(self):
        outs, ins = self.counts()
        for m in outs:
            self.own(0, m).start()
        for m in ins:
            self.own(1, m).start()

    def pass_on(self):
        outs, ins = self.counts()

        def way(outer_first):
            for m in outs if outer_first else ins:
                self.own(0 if outer_first else 1, m).wait_recv()
                for n in ins if outer_first else outs:
                    self.passed(m if outer_first else n, n if outer_first else m, outer_first).start()
            for m in ins if outer_first else outs:
                self.own(1 if outer_first else 0, m).wait_recv()

        if isinstance(self.outer_first, bool):
            way(self.outer_first)
        else:

            @pl.when(self.outer_first)
            def _():
                way(True)

            @pl.when(jnp.logical_not(self.outer_first))
            def _():
                way(False)

    def finish(self):
        outs, ins = self.counts()
        for m in outs:
            self.own(0, m).wait_send()
        for m in ins:
            self.own(1, m).wait_send()
        for mo in outs:
            for mi in ins:
                self.passed(mo, mi, True).wait()


def deal_kernel(
    n_dp, rows_w, x_ref, dy_ref, deal_ref, qw_ref, kw_ref, vw_ref, qb_ref, vb_ref, up_ref, dn_ref, ow_ref,
    ob_ref, g1_ref, s1_ref, db_ref, g2_ref, s2_ref, ub_ref, len_ref, trim_ref,
    xf_out, dys_out, qkv_out, qkvt_out, wq_out, seqo_ref, wg_ref,
    xf_ref, dys_ref, qkv_ref, qkvt_ref, wq_ref, so, sq,
    xs, seq, seqrx, w, bias, biases, blob, col,
    sx, rx, sc, rc, sz, rz, sc2, rc2, sw, rw, sb, rb, sm, rm, ss, rs, sf, rf, sp, rp, sl,
):
    d, r, c = me()
    half = lax.rem(r, 2)
    tokens, wide = x_ref.shape
    piece = tokens // n_dp
    third = qw_ref.shape[0]
    core = (d, r, 1 - c)
    zdev = (d, flip(r), c)
    far_row = lax.rem(r + 2, 4)
    ring = [(lax.rem(d + k, n_dp), r, c) for k in range(1, n_dp)]
    rows_dev = [(d, lax.rem(r + k, 4), c) for k in (1, 2, 3)]
    greet(ring + rows_dev + [core, (d, far_row, 1 - c)])

    blob[0:wide, :] = up_ref[:, :wide]
    blob[wide : 2 * wide, :] = up_ref[:, wide:]
    blob[DOWN:OUT, :] = dn_ref[...]
    blob[OUT:VEC, :] = ow_ref[...]
    vecs = [v[...].reshape(1, wide) for v in (ob_ref, g1_ref, s1_ref, db_ref, g2_ref, s2_ref)]
    vecs += [ub_ref[0:wide].reshape(1, wide), ub_ref[wide : 2 * wide].reshape(1, wide)]
    row = lax.broadcasted_iota(jnp.int32, (16, wide), 0)
    tail = jnp.zeros((16, wide), f32)
    for i, v in enumerate(vecs):
        tail = jnp.where(row == i, v.astype(f32), tail)
    blob[VEC : VEC + 16, :] = tail.astype(bf16)
    blob[VEC + 16 :, :] = jnp.zeros((rows_w - VEC - 16, wide), bf16)
    share = rows_w // n_dp
    my_share = pl.ds(pl.multiple_of(d * share, share), share)
    share_cp = [
        remote(blob.at[my_share, :], wg_ref.at[r, my_share, :], ss.at[k], rs.at[k], dev)
        for k, dev in enumerate(rows_dev)
    ]
    for cp in share_cp:
        cp.start()
    local_w = pltpu.make_async_copy(blob, wg_ref.at[r], sl)
    local_w.start()

    def rows(s):
        return pl.ds(pl.multiple_of(s * piece, piece), piece)

    col[...] = jnp.broadcast_to(deal_ref[...], (8, tokens)).T
    lane = lax.broadcasted_iota(jnp.int32, (piece, tokens), 1)
    sends = []
    for k in list(range(1, n_dp)) + [0]:
        dest = lax.rem(d + k, n_dp)
        pick = (col[rows(dest), 0:1] == lane).astype(bf16)
        px = nn(pick, x_ref[...]).astype(bf16)
        if k:
            xs[k] = px
            cp = remote(xs.at[k], xf_ref.at[half, c, rows(d), :], sx.at[k], rx.at[k], (dest, r, c))
            cp.start()
            sends.append(cp)
        else:
            xf_ref[half, c, rows(d), :] = px

    w[:third, :] = qw_ref[...]
    w[third : 2 * third, :] = kw_ref[...]
    w[2 * third :, :] = vw_ref[...]
    w_far = remote(w, wq_ref.at[c], sw.at[0], rw.at[c], (d, far_row, 1))
    w_far.start()
    w_near = remote(w, wq_ref.at[1], sw.at[1], rw.at[1], (d, r, 0))
    flat = jnp.concatenate(
        [qb_ref[...].reshape(1, third), jnp.zeros((1, third), bf16), vb_ref[...].reshape(1, third)], axis=1
    )
    bias[...] = jnp.broadcast_to(flat.astype(f32), (8, 3 * third))
    b_far = remote(bias, biases.at[1], sb.at[0], rb.at[0], (d, far_row, 1))

    @pl.when(c == 0)
    def _():
        wq_ref[0] = w[...]
        b_far.start()

    @pl.when(c == 1)
    def _():
        w_near.start()

    biases[0] = bias[...]
    seq[...] = jnp.zeros_like(seq)
    seq[0:1, 0 : len_ref.shape[1]] = len_ref[...]
    seq[1:2, 0 : len_ref.shape[1]] = trim_ref[...]
    seq_cp = remote(seq, seqrx, sm.at[0], rm.at[0], core)
    seq_cp.start()

    core_cp, z_cp, core2_cp = [], [], []
    for k in range(n_dp):
        s = lax.rem(d - k + n_dp, n_dp)
        ref = xf_ref.at[half, c, rows(s), :]
        if k:
            sends[k - 1].wait_recv()
        a = remote(ref, ref, sz.at[k], rz.at[k], zdev)
        a.start()
        b = remote(ref, ref, sc.at[k], rc.at[k], core)
        b.start()
        z_cp.append(a)
        core_cp.append(b)

    fans = []
    for k in range(3):
        share_cp[k].wait_recv()
        j = lax.rem(r - k + 3, 4)
        fan = Fan(
            n_dp,
            lambda s, j=j: wg_ref.at[j, pl.ds(pl.multiple_of(s * share, share), share), :],
            [(sf.at[k, 0], rf.at[k, 0]), (sf.at[k, 1], rf.at[k, 1]), (sp.at[k], rp.at[k])],
            j < 2,
        )
        fan.send()
        fans.append(fan)
        if k == 0:
            for dest in range(n_dp):
                pick = (col[dest * piece : (dest + 1) * piece, 0:1] == lane).astype(bf16)
                dys_ref[dest] = nn(pick, dy_ref[...]).astype(bf16)
        else:
            fans[k - 1].pass_on()

    @pl.when(c == 0)
    def _():
        w_near.wait_recv()
        b_far.wait_send()

    @pl.when(c == 1)
    def _():
        w_near.wait_send()
        b_far.wait_recv()
        remote(w, wq_ref.at[0], sw.at[0], rw.at[0], (d, far_row, 1)).wait_recv()
        remote(w, wq_ref.at[1], sw.at[0], rw.at[1], (d, far_row, 1)).wait_recv()

    for k in range(n_dp):
        core_cp[k].wait_recv()
    stores = [
        pltpu.make_async_copy(xf_ref.at[half], xf_out.at[half], so.at[0]),
        pltpu.make_async_copy(wq_ref, wq_out, so.at[1]),
        pltpu.make_async_copy(dys_ref, dys_out, so.at[2]),
    ]
    for cp in stores:
        cp.start()
    brow = jnp.where(c == 0, biases[0], biases[1])[0:1, :]

    def project(h, i):
        base = slice(i * 512, (i + 1) * 512)
        y = nt(xf_ref[h, 0, base, :], wq_ref[0]) + nt(xf_ref[h, 1, base, :], wq_ref[1]) + brow
        y = y.astype(bf16)
        out = pl.ds(pl.multiple_of(h * tokens + i * 512, 512), 512)
        qkv_ref[out, :] = y
        qkvt_ref[:, out] = y.T
        for src, dst, sem in (
            (qkv_ref.at[out, :], qkv_out.at[out, :], sq.at[i]), (qkvt_ref.at[:, out], qkvt_out.at[:, out], sq.at[2 + i])
        ):
            stores.append(pltpu.make_async_copy(src, dst, sem.at[h]))
            stores[-1].start()

    project(half, 0)
    project(half, 1)
    fans[2].pass_on()

    for k in range(n_dp):
        s = lax.rem(d - k + n_dp, n_dp)
        z_cp[k].wait_recv()
        ref = xf_ref.at[1 - half, c, rows(s), :]
        b = remote(ref, ref, sc2.at[k], rc2.at[k], core)
        b.start()
        core2_cp.append(b)

    w_far.wait_send()
    for k in range(n_dp):
        core2_cp[k].wait_recv()
    stores.append(pltpu.make_async_copy(xf_ref.at[1 - half], xf_out.at[1 - half], so.at[5]))
    stores[-1].start()
    project(1 - half, 0)
    project(1 - half, 1)
    seq_cp.wait()
    is_mine = lax.div(r, 2) == c
    seqo_ref[...] = jnp.where(is_mine, seq[...], seqrx[...])
    for fan in fans:
        fan.finish()
    for cp in sends + core_cp + z_cp + core2_cp + share_cp:
        cp.wait_send()
    for cp in stores:
        cp.wait()
    local_w.wait()


def deal_call(n_dp, rows_w, args):
    x, qw = args[0], args[3]
    tokens, wide = x.shape
    piece = tokens // n_dp
    cols = 3 * qw.shape[0]
    return pl.pallas_call(
        functools.partial(deal_kernel, n_dp, rows_w),
        out_shape=(
            sds((2, 2, tokens, wide), bf16),
            sds((n_dp, piece, wide), bf16),
            sds((2 * tokens, cols), bf16),
            sds((cols, 2 * tokens), bf16),
            sds((2, cols, wide), bf16),
            sds((8, 128), jnp.int32),
            sds((4, rows_w, wide), bf16),
        ),
        in_specs=[VM] * len(args),
        out_specs=(ANY,) * 5 + (VM, ANY),
        scratch_shapes=[
            pltpu.VMEM((2, 2, tokens, wide), bf16),
            pltpu.VMEM((n_dp, piece, wide), bf16),
            pltpu.VMEM((2 * tokens, cols), bf16),
            pltpu.VMEM((cols, 2 * tokens), bf16),
            pltpu.VMEM((2, cols, wide), bf16),
            DMA((6,)),
            DMA((4, 2)),
            pltpu.VMEM((n_dp, piece, wide), bf16),
            pltpu.VMEM((8, 128), jnp.int32),
            pltpu.VMEM((8, 128), jnp.int32),
            pltpu.VMEM((cols, wide), bf16),
            pltpu.VMEM((8, cols), f32),
            pltpu.VMEM((2, 8, cols), f32),
            pltpu.VMEM((rows_w, wide), bf16),
            pltpu.VMEM((tokens, 8), jnp.int32),
        ]
        + [DMA((n_dp,))] * 8
        + [DMA((2,))] * 6
        + [DMA((3,))] * 2
        + [DMA((3, 2, n_dp))] * 2
        + [DMA((3,) + levels(n_dp)[::-1])] * 2
        + [DMA],
        compiler_params=pltpu.CompilerParams(
            collective_id=1, has_side_effects=True, vmem_limit_bytes=VMEM_LIMIT
        ),
        name="deal",
    )(*args)


def seq_bounds(seq_ref, n_seq):
    ends, total = [], 0
    for j in range(n_seq):
        total = total + seq_ref[0, j]
        ends.append(total)
    starts = [ends[j] - seq_ref[0, j] for j in range(n_seq)]
    lives = [starts[j] + jnp.maximum(seq_ref[0, j] - seq_ref[1, j], 1) for j in range(n_seq)]
    return starts, ends, lives


def block_range(first, last, starts, ends, block):
    lo, hi = 0, ends[-1]
    for j in range(len(ends)):
        lo = jnp.where((first >= starts[j]) & (first < ends[j]), starts[j], lo)
        hi = jnp.where((last >= starts[j]) & (last < ends[j]), ends[j], hi)
    return lax.div(lo, block), lax.div(hi + block - 1, block)


def key_columns(starts, ends, lives, length, extra):
    pos = lax.broadcasted_iota(jnp.int32, (16, length), 1)
    row = lax.broadcasted_iota(jnp.int32, (16, length), 0)
    n_seq = len(ends)
    rows = jnp.where(row < n_seq, FAR, 0.0)
    rows = jnp.where((row >= n_seq) & (row < n_seq + extra), -1.0, rows)
    for j in range(n_seq):
        rows = jnp.where((row == j) & (pos >= starts[j]) & (pos < lives[j]), 0.0, rows)
    return jnp.concatenate([rows.T.astype(bf16), jnp.zeros((length, HEAD - 16), bf16)], axis=1)


def query_rows(starts, ends, length):
    pos = lax.broadcasted_iota(jnp.int32, (16, length), 1)
    row = lax.broadcasted_iota(jnp.int32, (16, length), 0)
    out = jnp.zeros((16, length), f32)
    for j in range(len(ends)):
        out = jnp.where((row == j) & (pos >= starts[j]) & (pos < ends[j]), 1.0, out)
    return out


def split_three(v):
    hi = v.astype(bf16).astype(f32)
    mid = (v - hi).astype(bf16).astype(f32)
    low = (v - hi - mid).astype(bf16).astype(f32)
    return hi, mid, low


def put_rows(base, values, first):
    row = lax.broadcasted_iota(jnp.int32, base.shape, 0)
    for i, v in enumerate(values):
        base = jnp.where(row == first + i, v, base)
    return base


def attend_kernel(n_seq, block, seq_ref, qkv_ref, qkvt_ref, ot_ref, lse_ref, kaug, qaug, vaug, acc, mx, sbuf):
    length = qkv_ref.shape[0]
    heads = qkv_ref.shape[1] // (3 * HEAD)
    width = heads * HEAD
    span = 2 * block
    starts, ends, lives = seq_bounds(seq_ref, n_seq)
    kcols = key_columns(starts, ends, lives, length, 0)
    qrows = query_rows(starts, ends, length)
    ones = (lax.broadcasted_iota(jnp.int32, (16, length), 0) == 0).astype(f32).astype(bf16)
    for h in range(heads):
        kaug[h, :, :HEAD] = qkv_ref[:, width + h * HEAD : width + (h + 1) * HEAD]
        kaug[h, :, HEAD:] = kcols
        qaug[h, :HEAD, :] = qkvt_ref[h * HEAD : (h + 1) * HEAD, :] * 0.125
        qaug[h, HEAD : HEAD + 16, :] = qrows.astype(bf16)
        qaug[h, HEAD + 16 :, :] = jnp.zeros((HEAD - 16, length), bf16)
        vaug[h, :HEAD, :] = qkvt_ref[2 * width + h * HEAD : 2 * width + (h + 1) * HEAD, :]
        vaug[h, HEAD:, :] = ones
    lse_ref[...] = jnp.zeros_like(lse_ref)

    def q_step(qb, carry):
        qs = pl.ds(pl.multiple_of(qb * block, block), block)
        lo, hi = block_range(qb * block, qb * block + block - 1, starts, ends, block)
        for h in range(heads):
            acc[h] = jnp.zeros((HEAD + 16, block), f32)
            mx[h] = jnp.full((8, block), 2 * FAR, f32)

        def max_step(size, i, inner):
            ks = pl.ds(pl.multiple_of((lo + 2 * i) * block, block), size)
            at = pl.ds(pl.multiple_of(i * span, span), size)
            ss = [nn(kaug[h, ks, :], qaug[h, :, qs]) for h in range(heads)]
            for h in range(heads):
                sbuf[h, at, :] = ss[h]
                mx[h] = jnp.maximum(mx[h], jnp.max(ss[h].reshape(size // 8, 8, block), axis=0))
            return inner

        pairs, odd = lax.div(hi - lo, 2), lax.rem(hi - lo, 2)
        lax.fori_loop(0, pairs, functools.partial(max_step, span), 0)
        lax.fori_loop(pairs, pairs + odd, functools.partial(max_step, block), 0)
        tops = []
        for h in range(heads):
            top = jnp.max(mx[h], axis=0, keepdims=True)
            tops.append(top)

        def sum_step(size, i, inner):
            ks = pl.ds(pl.multiple_of((lo + 2 * i) * block, block), size)
            at = pl.ds(pl.multiple_of(i * span, span), size)
            ps = [jnp.exp(sbuf[h, at, :] - tops[h]).astype(bf16) for h in range(heads)]
            for h in range(heads):
                acc[h] = acc[h] + nn(vaug[h, :, ks], ps[h])
            return inner

        lax.fori_loop(0, pairs, functools.partial(sum_step, span), 0)
        lax.fori_loop(pairs, pairs + odd, functools.partial(sum_step, block), 0)
        for h in range(heads):
            total = acc[h, HEAD : HEAD + 1, :]
            ot_ref[h * HEAD : (h + 1) * HEAD, qs] = (acc[h, :HEAD, :] / total).astype(bf16)
            lse_ref[h : h + 1, qs] = tops[h] + jnp.log(total)
        return carry

    lax.fori_loop(0, length // block, q_step, 0)


def attend_call(n_seq, seq, qkv, qkvt):
    length, cols = qkv.shape
    heads = cols // (3 * HEAD)
    block = 256
    return pl.pallas_call(
        functools.partial(attend_kernel, n_seq, block),
        out_shape=(sds((heads * HEAD, length), bf16), sds((8, length), f32)),
        in_specs=[SM, VM, VM],
        out_specs=(VM, VM),
        scratch_shapes=[
            pltpu.VMEM((heads, length, 2 * HEAD), bf16),
            pltpu.VMEM((heads, 2 * HEAD, length), bf16),
            pltpu.VMEM((heads, HEAD + 16, length), bf16),
            pltpu.VMEM((heads, HEAD + 16, block), f32),
            pltpu.VMEM((heads, 8, block), f32),
            pltpu.VMEM((heads, length, block), f32),
        ],
        compiler_params=pltpu.CompilerParams(vmem_limit_bytes=VMEM_LIMIT),
        cost_estimate=pl.CostEstimate(flops=4 * 10**9, bytes_accessed=6 * 10**6, transcendentals=10**7),
        name="attend",
    )(seq, qkv, qkvt)


def attend_back_kernel(
    n_seq, block, seq_ref, qkv_ref, qkvt_ref, dot_ref, ot_ref, lse_ref, dqkv_ref,
    kaug, qaug, vaug, doaug, qn, don, dqt, dk, dv,
):
    length = qkv_ref.shape[0]
    heads = qkv_ref.shape[1] // (3 * HEAD)
    width = heads * HEAD
    starts, ends, lives = seq_bounds(seq_ref, n_seq)
    kcols = key_columns(starts, ends, lives, length, 3)
    lane = lax.broadcasted_iota(jnp.int32, (length, HEAD), 1)
    vcols = jnp.where(lane < 3, -1.0, 0.0).astype(bf16)
    qrows = query_rows(starts, ends, length)
    zero = jnp.zeros((HEAD - 16, length), bf16)
    span = 2 * block
    for h in range(heads):
        hs = slice(h * HEAD, (h + 1) * HEAD)
        kaug[h, :, :HEAD] = qkv_ref[:, width + h * HEAD : width + (h + 1) * HEAD]
        kaug[h, :, HEAD:] = kcols
        vaug[h, :, :HEAD] = qkv_ref[:, 2 * width + h * HEAD : 2 * width + (h + 1) * HEAD]
        vaug[h, :, HEAD:] = vcols
        qaug[h, :HEAD, :] = qkvt_ref[hs, :] * 0.125
        qaug[h, HEAD : HEAD + 16, :] = put_rows(qrows, split_three(lse_ref[h : h + 1, :]), n_seq).astype(bf16)
        qaug[h, HEAD + 16 :, :] = zero
        do = dot_ref[hs, :]
        delta = jnp.sum(do.astype(f32) * ot_ref[hs, :].astype(f32), axis=0, keepdims=True)
        doaug[h, :HEAD, :] = do
        doaug[h, HEAD : HEAD + 16, :] = put_rows(
            jnp.zeros((16, length), f32), split_three(delta), 0
        ).astype(bf16)
        doaug[h, HEAD + 16 :, :] = zero
        qn[h] = qkv_ref[:, hs] * 0.125
        don[h] = do.T
        dqt[h] = jnp.zeros((HEAD, length), f32)

    def k_step(kb, carry):
        ks = pl.ds(pl.multiple_of(kb * block, block), block)
        lo, hi = block_range(kb * block, kb * block + block - 1, starts, ends, block)
        dk[...] = jnp.zeros_like(dk)
        dv[...] = jnp.zeros_like(dv)

        def q_step(size, i, inner):
            qs = pl.ds(pl.multiple_of((lo + 2 * i) * block, block), size)
            for h in range(heads):
                p = jnp.exp(nn(kaug[h, ks, :], qaug[h, :, qs]))
                ds = (p * nn(vaug[h, ks, :], doaug[h, :, qs])).astype(bf16)
                dv[h] = dv[h] + nn(p.astype(bf16), don[h, qs, :])
                dk[h] = dk[h] + nn(ds, qn[h, qs, :])
                kt = qkvt_ref[width + h * HEAD : width + (h + 1) * HEAD, ks]
                dqt[h, :, qs] = dqt[h, :, qs] + nn(kt, ds)
            return inner

        pairs, odd = lax.div(hi - lo, 2), lax.rem(hi - lo, 2)
        lax.fori_loop(0, pairs, functools.partial(q_step, span), 0)
        lax.fori_loop(pairs, pairs + odd, functools.partial(q_step, block), 0)
        for h in range(heads):
            vk = dk[h].astype(bf16)
            vv = dv[h].astype(bf16)
            a, b = width + h * HEAD, 2 * width + h * HEAD
            dqkv_ref[ks, a : a + HEAD] = vk
            dqkv_ref[ks, b : b + HEAD] = vv
        return carry

    lax.fori_loop(0, length // block, k_step, 0)
    for h in range(heads):
        v = (dqt[h] * 0.125).astype(bf16)
        dqkv_ref[:, h * HEAD : (h + 1) * HEAD] = v.T


def attend_back_call(n_seq, seq, qkv, qkvt, dot, ot, lse):
    length, cols = qkv.shape
    heads = cols // (3 * HEAD)
    block = 256
    nat = pltpu.VMEM((heads, length, 2 * HEAD), bf16)
    tra = pltpu.VMEM((heads, 2 * HEAD, length), bf16)
    return pl.pallas_call(
        functools.partial(attend_back_kernel, n_seq, block),
        out_shape=sds((length, cols), bf16),
        in_specs=[SM] + [VM] * 5,
        out_specs=VM,
        scratch_shapes=[
            nat, tra, nat, tra,
            pltpu.VMEM((heads, length, HEAD), bf16),
            pltpu.VMEM((heads, length, HEAD), bf16),
            pltpu.VMEM((heads, HEAD, length), f32),
            pltpu.VMEM((heads, block, HEAD), f32),
            pltpu.VMEM((heads, block, HEAD), f32),
        ],
        compiler_params=pltpu.CompilerParams(vmem_limit_bytes=VMEM_LIMIT),
        cost_estimate=pl.CostEstimate(flops=10**10, bytes_accessed=12 * 10**6, transcendentals=10**7),
        name="attend_back",
    )(seq, qkv, qkvt, dot, ot, lse)


def shard_of(r, c):
    return lax.rem(r + 2 * c, 4)


def middle_kernel(
    n_dp, oin_ref, xf_any, dys_ref, w_ref, back_ref, dh1_ref, dout_ref, *rest
):
    n_in, n_out = levels(n_dp)
    n = n_in + n_out
    parts, rest = (rest[:n_in], rest[n_in:n], rest[n : n + 4]), rest[n + 4 :]
    middle_body(n_dp, oin_ref, xf_any, dys_ref, w_ref, back_ref, dh1_ref, dout_ref, *parts, *rest)


def middle_body(
    n_dp, oin_ref, xf_any, dys_ref, w_ref, back_ref, dh1_ref, dout_ref, a_refs, b_refs, z_refs,
    xv, xsem, fin, s_a, r_a, dyin, dyb, ot_ref, dot_ref, wup, wdn, wo, vec, ub, hid, slope, dub, sums, gbuf, gin, facc, yacc,
    so, ro, sg, rg, lsem, wss, wrs, sgb, rgb, sgt, rgt, gsem, sd, rd, sm, rm, zsem,
):
    d, r, c = me()
    half = lax.rem(r, 2)
    wide = xf_any.shape[3]
    width = 2 * wide
    tok = dyb.shape[0]
    mine = pl.ds(pl.multiple_of(c * tok, tok), tok)
    x_cp = pltpu.make_async_copy(xf_any.at[half, :, mine, :], xv, xsem)
    x_cp.start()
    hrows = oin_ref.shape[0]
    core = (d, r, 1 - c)
    peers = [(d, flip(r), c), (d, flip(r), 1 - c), core]
    ring = [(lax.rem(d + k, n_dp), r, c) for k in range(1, n_dp)]
    greet(peers + ring + [(dev[0], r, 1 - c) for dev in ring])
    base = r - half
    shard = shard_of(r, c)
    o_cp = []
    for i, dev in enumerate(peers):
        q = (dev[1] - base) * 2 + dev[2]
        src = oin_ref.at[:, pl.ds(pl.multiple_of(q * tok, tok), tok)]
        cp = remote(src, ot_ref.at[shard], so.at[i], ro.at[i], dev)
        cp.start()
        o_cp.append(cp)
    myq = pl.ds(pl.multiple_of((half * 2 + c) * tok, tok), tok)
    ot_ref[shard] = oin_ref[:, myq]

    piece = dys_ref.shape[1]
    here = pl.ds(pl.multiple_of(d * piece, piece), piece)
    d_cp = []
    for k, dev in enumerate(ring):
        cp = remote(dys_ref.at[dev[0]], dyin.at[here, :], sd.at[k], rd.at[k], dev)
        cp.start()
        d_cp.append(cp)
    dyin[here, :] = dys_ref[d]

    loads = [[], [], []]
    mycols = pl.ds(pl.multiple_of(c * wide, 128), wide)
    for j in range(4):
        js = slice(j * hrows, (j + 1) * hrows)
        loads[0].append((w_ref.at[j, OUT:VEC], wo.at[js, mycols]))
        loads[0].append((w_ref.at[j, VEC : VEC + 16], ub.at[j, c]))
        for h in range(2):
            hs = slice(h * wide, (h + 1) * wide)
            loads[1].append((w_ref.at[j, hs], wup.at[j, mycols, hs]))
        loads[2].append((w_ref.at[j, DOWN:OUT], wdn.at[j, :, mycols]))
    w_cps = []
    for i, group in enumerate(loads):
        cps = []
        for k, (src, dst) in enumerate(group):
            a = pltpu.make_async_copy(src, dst, lsem.at[i, k])
            a.start()
            b = remote(src, dst, wss.at[i, k], wrs.at[i, k], core)
            b.start()
            cps += [a, b]
        w_cps.append(cps)

    def settle(i):
        for cp in w_cps[i]:
            cp.wait()

    for cp in o_cp:
        cp.wait_recv()
    x_cp.wait()
    x = jnp.concatenate([xv[0], xv[1]], axis=1).astype(f32)
    settle(0)
    vec[...] = jnp.concatenate([ub[0, 0], ub[0, 1]], axis=1)
    ob, g1, s1, db, g2, s2 = [vec[i : i + 1, :].astype(f32) for i in range(6)]
    o = ot_ref[...].reshape(width, tok).T
    h1 = x + (nn(o, wo[...]) + ob)
    mu = jnp.mean(h1, axis=1, keepdims=True)
    r1 = lax.rsqrt(jnp.mean(h1 * h1, axis=1, keepdims=True) - mu * mu + EPS)
    n1 = (h1 - mu) * r1
    y1 = (n1 * g1 + s1).astype(bf16)
    for cp in d_cp:
        cp.wait_recv()
    theirs = pl.ds(pl.multiple_of((1 - c) * tok, tok), tok)
    dy_cp = remote(dyin.at[theirs, :], dyb, sm, rm, core)
    dy_cp.start()
    settle(1)
    settle(2)
    facc[...] = jnp.zeros_like(facc)

    def ahead(j, carry):
        bias = jnp.concatenate([ub[j, 0, 6:7, :], ub[j, 0, 7:8, :]], axis=1).astype(f32)
        u = nn(y1, wup[j]) + bias
        cdf = 0.5 * (1.0 + lax.erf(u * INV_ROOT_TWO))
        hj = (u * cdf).astype(bf16)
        hid[j] = hj
        slope[j] = cdf + u * jnp.exp(-0.5 * u * u) * INV_ROOT_TAU
        facc[...] += nn(hj, wdn[j])
        return carry

    lax.fori_loop(0, 4, ahead, 0)
    h2 = y1.astype(f32) + (facc[...] + db)
    mu2 = jnp.mean(h2, axis=1, keepdims=True)
    r2 = lax.rsqrt(jnp.mean(h2 * h2, axis=1, keepdims=True) - mu2 * mu2 + EPS)
    n2 = (h2 - mu2) * r2
    res = (n2 * g2 + s2).astype(bf16)
    fin[0] = res[:, :wide]
    fin[1] = res[:, wide:]
    send_back(n_dp, fin, back_ref, s_a, r_a)
    dy_cp.wait_recv()
    own, other = dyin[mine, :], dyb[...]
    left = jnp.where(c == 0, own, other)
    right = jnp.where(c == 0, other, own)
    dy = jnp.concatenate([left, right], axis=1).astype(f32)
    e2 = dy * g2
    dh2 = r2 * (e2 - jnp.mean(e2, axis=1, keepdims=True) - n2 * jnp.mean(e2 * n2, axis=1, keepdims=True))
    g2g = jnp.sum(dy * n2, axis=0, keepdims=True)
    s2g = jnp.sum(dy, axis=0, keepdims=True)
    df = dh2.astype(bf16)
    dbg = jnp.sum(df.astype(f32), axis=0, keepdims=True)
    yacc[...] = dh2
    def big_cp(j):
        return remote(gbuf.at[j, 1 - c, 0:OUT], gin.at[j, 0:OUT], sgb.at[j], rgb.at[j], core)

    def back(j, carry):
        du = (nt(df, wdn[j]) * slope[j]).astype(bf16)
        dub[j] = du
        sums[j] = jnp.broadcast_to(jnp.sum(du.astype(f32), axis=0, keepdims=True), (8, width))
        yacc[...] += nt(du, wup[j])
        return carry

    lax.fori_loop(0, 4, back, 0)
    dy1 = yacc[...]
    e1 = dy1 * g1
    dh1 = r1 * (e1 - jnp.mean(e1, axis=1, keepdims=True) - n1 * jnp.mean(e1 * n1, axis=1, keepdims=True))
    dh1_ref[...] = dh1
    g1g = jnp.sum(dy1 * n1, axis=0, keepdims=True)
    s1g = jnp.sum(dy1, axis=0, keepdims=True)
    da = dh1.astype(bf16)
    obg = jnp.sum(da.astype(f32), axis=0, keepdims=True)
    dot_ref[...] = nt(da, wo[...]).T.astype(bf16).reshape(dot_ref.shape)
    g_cp = []
    for i, dev in enumerate(peers):
        cp = remote(dot_ref.at[shard_of(dev[1], dev[2])], dout_ref.at[:, myq], sg.at[i], rg.at[i], dev)
        cp.start()
        g_cp.append(cp)
    dout_ref[:, myq] = dot_ref[shard]
    y1t = y1.T

    def grads(j, carry):
        gd = tn(hid[j], df).astype(bf16)
        gu = nn(y1t, dub[j]).astype(bf16)
        for cc in range(2):
            cs = slice(cc * wide, (cc + 1) * wide)
            for h in range(2):
                gbuf[j, cc, h * wide : (h + 1) * wide, :] = gu[cs, h * wide : (h + 1) * wide]
            gbuf[j, cc, DOWN:OUT, :] = gd[:, cs]
        big_cp(j).start()
        return carry

    lax.fori_loop(0, 4, grads, 0)
    go = nn(ot_ref[...].reshape(width, tok), da).astype(bf16)
    pad = gbuf.shape[2] - VEC
    row = lax.broadcasted_iota(jnp.int32, (pad, wide), 0)
    t_cp = []
    for j in range(4):
        for cc in range(2):
            cs = slice(cc * wide, (cc + 1) * wide)
            gbuf[j, cc, OUT:VEC, :] = go[j * hrows : (j + 1) * hrows, cs]
            tail = jnp.zeros((pad, wide), f32)
            for i, v in enumerate((obg, g1g, s1g, dbg, g2g, s2g)):
                tail = jnp.where(row == i, v[:, cs], tail)
            tail = jnp.where(row == 6, sums[j, 0:1, :wide], tail)
            tail = jnp.where(row == 7, sums[j, 0:1, wide:], tail)
            gbuf[j, cc, VEC:, :] = tail.astype(bf16)
        cp = remote(gbuf.at[j, 1 - c, OUT:], gin.at[j, OUT:], sgt.at[j], rgt.at[j], core)
        cp.start()
        t_cp.append(cp)
    rows_q = a_refs[0].shape[2]
    rows_d = rows_q * n_dp
    n_in, n_out = levels(n_dp)
    outs = []
    for j in range(4):
        big_cp(j).wait()
        t_cp[j].wait()
        gin[j] = (gin[j].astype(f32) + gbuf[j, c].astype(f32)).astype(bf16)
        n_first, n_second, refs = (n_in, n_out, a_refs) if j < 2 else (n_out, n_in, b_refs)
        for k in range(n_first):
            for m in range(n_second):
                if j < 2:
                    s = m * n_in + lax.rem(lax.rem(d, n_in) + k, n_in)
                else:
                    s = lax.rem(lax.div(d, n_in) + k, n_out) * n_in + m
                span = pl.ds(pl.multiple_of(s * rows_q, rows_q), rows_q)
                cp = pltpu.make_async_copy(gin.at[j, span], refs[k].at[m, j % 2], gsem.at[j, k * n_second + m])
                cp.start()
                outs.append(cp)
    for k in range(4):
        cp = pltpu.make_async_copy(gin.at[lax.rem(r + k, 4), rows_d:], z_refs[k], zsem.at[k])
        cp.start()
        outs.append(cp)
    got_back(n_dp, fin, back_ref, s_a, r_a)
    sent_back(n_dp, fin, back_ref, s_a, r_a)
    for cp in o_cp + d_cp + [dy_cp]:
        cp.wait_send()
    for cp in g_cp + outs:
        cp.wait()


def middle_call(n_dp, oin, xf, dys, w, g_rows):
    tok, wide = xf.shape[2] // 2, xf.shape[3]
    width = 2 * wide
    hrows = oin.shape[0]
    n_in, n_out = levels(n_dp)
    rows_q = g_rows * 3 // 4 // n_dp
    return pl.pallas_call(
        functools.partial(middle_kernel, n_dp),
        out_shape=(
            sds((2 * tok, wide), bf16),
            sds((tok, width), f32),
            sds((hrows, 4 * tok), bf16),
        )
        + (sds((n_out, 2, rows_q, wide), bf16),) * n_in
        + (sds((n_in, 2, rows_q, wide), bf16),) * n_out
        + (sds((g_rows - rows_q * n_dp, wide), bf16),) * 4,
        in_specs=[VM, ANY, VM, ANY],
        out_specs=(VM, VM, VM) + (ANY,) * (n_in + n_out + 4),
        scratch_shapes=[
            pltpu.VMEM((2, tok, wide), bf16),
            DMA,
            pltpu.VMEM((2, tok, wide), bf16),
            DMA((n_dp // 2, 2)), DMA((n_dp,)),
            pltpu.VMEM((2 * tok, wide), bf16),
            pltpu.VMEM((tok, wide), bf16),
            pltpu.VMEM((4, hrows, tok), bf16),
            pltpu.VMEM((4, hrows, tok), bf16),
            pltpu.VMEM((4, width, width), bf16),
            pltpu.VMEM((4, width, width), bf16),
            pltpu.VMEM((width, width), bf16),
            pltpu.VMEM((16, width), bf16),
            pltpu.VMEM((4, 2, 16, wide), bf16),
            pltpu.VMEM((4, tok, width), bf16),
            pltpu.VMEM((4, tok, width), f32),
            pltpu.VMEM((4, tok, width), bf16),
            pltpu.VMEM((4, 8, width), f32),
            pltpu.VMEM((4, 2, g_rows, wide), bf16),
            pltpu.VMEM((4, g_rows, wide), bf16),
            pltpu.VMEM((tok, width), f32),
            pltpu.VMEM((tok, width), f32),
            DMA((3,)), DMA((3,)), DMA((3,)), DMA((3,)),
            DMA((3, 8)), DMA((3, 8)), DMA((3, 8)),
            DMA((4,)), DMA((4,)), DMA((4,)), DMA((4,)),
            DMA((4, n_dp)), DMA((n_dp,)), DMA((n_dp,)), DMA, DMA, DMA((4,)),
        ],
        compiler_params=pltpu.CompilerParams(
            collective_id=2, has_side_effects=True, vmem_limit_bytes=VMEM_LIMIT
        ),
        cost_estimate=pl.CostEstimate(flops=16 * 10**9, bytes_accessed=30 * 10**6, transcendentals=4 * 10**6),
        name="middle",
    )(oin, xf, dys, w)


def return_kernel(n_dp, dqkv_any, wq_any, xf_any, dh1_any, *rest):
    n_in, n_out = levels(n_dp)
    n = n_in + n_out
    parts, rest = (rest[:n_in], rest[n_in:n], rest[n : n + 4]), rest[n + 4 :]
    return_body(n_dp, dqkv_any, wq_any, xf_any, dh1_any, *parts, *rest)


def return_body(
    n_dp, dqkv_any, wq_any, xf_any, dh1_any, a_parts, b_parts, z_parts,
    back_ref, gout_ref, gall_ref,
    dqkv_ref, wq, xf, dh1, apart, bpart, zpart, zsum, zrx, s_v, r_v, lsem, psem,
    asum, bsum, ain, bin_, rsum, zin, fin, tocore, fromcore, toz, fromz, gq_ref, gqin, gsum, xq, gfin,
    s_1, r_1, s_2, r_2, s_r, r_r, s_t, r_t, s_p, r_p, s_b, r_b, s_c, r_c, s_z, r_z, s_q, r_q, s_x, r_x, s_g, r_g, zload,
):
    d, r, c = me()
    n_in, n_out = levels(n_dp)
    o, i = lax.div(d, n_in), lax.rem(d, n_in)
    half = lax.rem(r, 2)
    tok, width = dh1_any.shape
    wide = width // 2
    core = (d, r, 1 - c)
    zdev = (d, flip(r), c)
    far_row = lax.rem(r + 2, 4)
    rows_dev = [(d, lax.rem(r + k, 4), c) for k in (1, 2, 3)]
    n_ch = 3
    chunk = rsum.shape[1] // n_ch
    z_loads = [pltpu.make_async_copy(z_parts[k], zpart.at[k], zload.at[k]) for k in range(4)]
    part_loads = []
    for t in range(n_ch):
        ts = slice(t * chunk, (t + 1) * chunk)
        group = [
            pltpu.make_async_copy(a_parts[k].at[:, :, ts], apart.at[k, :, :, ts], psem.at[t, k]) for k in range(n_in)
        ]
        group += [
            pltpu.make_async_copy(b_parts[k].at[:, :, ts], bpart.at[k, :, :, ts], psem.at[t, n_in + k])
            for k in range(n_out)
        ]
        part_loads.append(group)
    loads = [
        pltpu.make_async_copy(src, dst, lsem.at[k])
        for k, (src, dst) in enumerate(((wq_any, wq), (dqkv_any, dqkv_ref), (dh1_any, dh1), (xf_any, xf)))
    ]
    for cp in loads[:2] + part_loads[0] + part_loads[1] + part_loads[2] + z_loads + loads[2:]:
        cp.start()
    peers = [(lax.rem(d + k, n_dp), r, cc) for k in range(1, n_dp) for cc in (0, 1)]
    greet(peers + rows_dev + [core, (d, far_row, 1 - c)])

    def part(h, cc):
        q = h * 2 + cc
        rows = dqkv_ref[pl.ds(pl.multiple_of(q * tok, tok), tok), :]
        return jnp.concatenate([nn(rows, wq[0]), nn(rows, wq[1])], axis=1)

    a_cp, b_cp = [], []

    def second(t):
        ts = slice(t * chunk, (t + 1) * chunk)
        for cp in part_loads[t]:
            cp.wait()
        total = apart[0, :, :, ts].astype(f32)
        for k in range(1, n_in):
            total = total + apart[k, :, :, ts].astype(f32)
        asum[:, :, ts] = total.astype(bf16)
        total = bpart[0, :, :, ts].astype(f32)
        for k in range(1, n_out):
            total = total + bpart[k, :, :, ts].astype(f32)
        bsum[:, :, ts] = total.astype(bf16)
        for k in range(1, n_out):
            dest = lax.rem(o + k, n_out)
            cp = remote(
                asum.at[dest, :, ts], ain.at[k, :, ts], s_1.at[k, t], r_1.at[k, t], (dest * n_in + i, r, c)
            )
            cp.start()
            a_cp.append(cp)
        for k in range(1, n_in):
            dest = lax.rem(i + k, n_in)
            cp = remote(
                bsum.at[dest, :, ts], bin_.at[k, :, ts], s_2.at[k, t], r_2.at[k, t], (o * n_in + dest, r, c)
            )
            cp.start()
            b_cp.append(cp)

    for cp in loads[:2]:
        cp.wait()
    tocore[0] = part(1 - half, 1 - c).astype(bf16)
    cp_far = remote(tocore.at[0], fromcore.at[0], s_c.at[0], r_c.at[0], core)
    cp_far.start()
    second(0)
    far = part(1 - half, c)
    cp_far.wait_recv()
    toz[...] = (far + fromcore[0].astype(f32)).astype(bf16)
    cp_z = remote(toz, fromz, s_z, r_z, zdev)
    cp_z.start()
    second(1)
    second(2)
    for cp in z_loads:
        cp.wait()
    total = zpart[0].astype(f32)
    for k in range(1, 4):
        total = total + zpart[k].astype(f32)
    zsum[...] = total.astype(bf16)
    rows_z = zsum.shape[0] // n_dp

    def zrows(s):
        return pl.ds(pl.multiple_of(s * rows_z, rows_z), rows_z)

    v_cp = []
    for k in range(1, n_dp):
        dest = lax.rem(d + k, n_dp)
        cp = remote(zsum.at[zrows(dest), :], zrx.at[k], s_v.at[k], r_v.at[k], (dest, r, c))
        cp.start()
        v_cp.append(cp)

    row_cp = []

    def to_rows(t):
        ts = slice(t * chunk, (t + 1) * chunk)
        total = asum[o, :, ts].astype(f32)
        for k in range(1, n_out):
            a_cp[t * (n_out - 1) + k - 1].wait_recv()
            total = total + ain[k, :, ts].astype(f32)
        rsum[0:2, ts] = total.astype(bf16)
        total = bsum[i, :, ts].astype(f32)
        for k in range(1, n_in):
            b_cp[t * (n_in - 1) + k - 1].wait_recv()
            total = total + bin_[k, :, ts].astype(f32)
        rsum[2:4, ts] = total.astype(bf16)
        for k, dev in enumerate(rows_dev):
            cp = remote(rsum.at[dev[1], ts], zin.at[k, ts], s_r.at[k, t], r_r.at[k, t], dev)
            cp.start()
            row_cp.append(cp)

    to_rows(0)

    length, n_cols = dqkv_ref.shape
    loads[3].wait()
    for f in range(2):
        g = tn(dqkv_ref[: length // 2, :], xf[0, f]) + tn(dqkv_ref[length // 2 :, :], xf[1, f])
        gq_ref[f, :n_cols, :] = g.astype(bf16)
        to_rows(1 + f)
    third = n_cols // 3
    sums = jnp.sum(dqkv_ref[...].astype(f32), axis=0, keepdims=True)
    bias = jnp.concatenate([sums[:, :third], sums[:, 2 * third :]], axis=1)
    pad = gq_ref.shape[1] - n_cols
    row = lax.broadcasted_iota(jnp.int32, (pad, wide), 0)
    tail = jnp.where(row == 0, bias, 0.0).astype(bf16)
    for f in range(2):
        gq_ref[f, n_cols:, :] = tail
    rq = gq_ref.shape[1] // n_dp

    def quarter(s):
        return pl.ds(pl.multiple_of(s * rq, rq), rq)

    q_cp = []
    for k in range(1, n_dp):
        dest = lax.rem(d + k, n_dp)
        cp = remote(gq_ref.at[:, quarter(dest), :], gqin.at[k], s_q.at[k], r_q.at[k], (dest, r, c))
        cp.start()
        q_cp.append(cp)

    tocore[1] = part(half, 1 - c).astype(bf16)
    cp_near = remote(tocore.at[1], fromcore.at[1], s_c.at[1], r_c.at[1], core)
    cp_near.start()

    total = zsum[zrows(d), :].astype(f32)
    for k in range(1, n_dp):
        v_cp[k - 1].wait_recv()
        total = total + zrx[k].astype(f32)
    rows_d = n_dp * rsum.shape[1]
    gall_ref[pl.ds(pl.multiple_of(rows_d + d * rows_z, rows_z), rows_z), :] = total.astype(bf16)
    vfan = Fan(
        n_dp,
        lambda s: gall_ref.at[pl.ds(pl.multiple_of(rows_d + s * rows_z, rows_z), rows_z), :],
        [(s_t.at[3, 0], r_t.at[3, 0]), (s_t.at[3, 1], r_t.at[3, 1]), (s_p.at[3], r_p.at[3])],
        True,
    )
    vfan.send()

    loads[2].wait()
    total = part(half, c) + dh1[...]
    cp_near.wait_recv()
    total = total + fromcore[1].astype(f32)

    acc = gq_ref[:, quarter(d), :].astype(f32)
    for k in range(1, n_dp):
        q_cp[k - 1].wait_recv()
        acc = acc + gqin[k].astype(f32)
    gsum[...] = acc.astype(bf16)
    to_one = remote(gsum.at[1], xq.at[1], s_x.at[1], r_x.at[1], (d, r, 1))
    far_0 = remote(gsum.at[0], xq.at[0], s_x.at[0], r_x.at[0], (d, far_row, 0))
    far_1 = remote(gsum.at[1], xq.at[0], s_x.at[1], r_x.at[0], (d, far_row, 1))

    @pl.when(c == 0)
    def _():
        to_one.start()

    @pl.when(c == 1)
    def _():
        far_0.start()
        far_1.start()

    cp_z.wait_recv()
    total = (total + fromz[...].astype(f32)).astype(bf16)
    fin[0] = total[:, :wide]
    fin[1] = total[:, wide:]
    send_back(n_dp, fin, back_ref, s_b, r_b)

    vfan.pass_on()
    n_keep = rsum.shape[1]
    t_cp, fans = [], []
    for t in range(n_ch):
        ts = slice(t * chunk, (t + 1) * chunk)
        held = rsum[r, ts].astype(f32)
        for k in range(3):
            row_cp[t * 3 + k].wait_recv()
            held = held + zin[k, ts].astype(f32)
        keep = pl.ds(pl.multiple_of(d * n_keep + t * chunk, chunk), chunk)
        gall_ref[keep, :] = held.astype(bf16)
        fan = Fan(
            n_dp,
            lambda s, t=t: gall_ref.at[pl.ds(pl.multiple_of(s * n_keep + t * chunk, chunk), chunk), :],
            [(s_t.at[t, 0], r_t.at[t, 0]), (s_t.at[t, 1], r_t.at[t, 1]), (s_p.at[t], r_p.at[t])],
            t % 2 == 0,
        )
        fan.send()
        fans.append(fan)
        if t:
            fans[t - 1].pass_on()
    fans[-1].pass_on()

    far_0.wait_recv()

    @pl.when(c == 0)
    def _():
        gfin[...] = (gsum[0].astype(f32) + xq[0].astype(f32)).astype(bf16)

    @pl.when(c == 1)
    def _():
        to_one.wait_recv()
        gfin[...] = (xq[0].astype(f32) + xq[1].astype(f32)).astype(bf16)

    for k in range(1, n_dp):
        dest = lax.rem(d + k, n_dp)
        cp = remote(gfin, gout_ref.at[quarter(d), :], s_g.at[k], r_g.at[k], (dest, r, c))
        cp.start()
        t_cp.append(cp)
    gout_ref[quarter(d), :] = gfin[...]
    got_back(n_dp, fin, back_ref, s_b, r_b)
    sent_back(n_dp, fin, back_ref, s_b, r_b)
    for cp in [cp_far, cp_near, cp_z] + q_cp + a_cp + b_cp + row_cp:
        cp.wait_send()
    for cp in t_cp:
        cp.wait()
    for fan in fans + [vfan]:
        fan.finish()
    for cp in v_cp:
        cp.wait_send()

    @pl.when(c == 0)
    def _():
        to_one.wait_send()

    @pl.when(c == 1)
    def _():
        far_0.wait_send()
        far_1.wait_send()


def return_call(n_dp, dqkv, wq, xf, dh1, a_parts, b_parts, z_parts, gq_rows):
    n_in, n_out = levels(n_dp)
    tok, width = dh1.shape
    wide = width // 2
    share = a_parts[0].shape[2]
    rows_z = z_parts[0].shape[0]
    tokens = 2 * tok

    def vm(*shape):
        return pltpu.VMEM(shape, bf16)

    return pl.pallas_call(
        functools.partial(return_kernel, n_dp),
        out_shape=(sds((tokens, wide), bf16), sds((gq_rows, wide), bf16), sds((n_dp * share + rows_z, wide), bf16)),
        in_specs=[ANY] * (8 + n_in + n_out),
        out_specs=(VM,) * 3,
        scratch_shapes=[
            vm(*dqkv.shape), vm(*wq.shape), vm(*xf.shape), pltpu.VMEM(dh1.shape, f32),
            vm(n_in, n_out, 2, share, wide), vm(n_out, n_in, 2, share, wide),
            vm(4, rows_z, wide), vm(rows_z, wide), vm(n_dp, rows_z // n_dp, wide), DMA((n_dp,)), DMA((n_dp,)),
            DMA((4,)), DMA((4, n_in + n_out)),
            vm(n_out, 2, share, wide), vm(n_in, 2, share, wide), vm(n_out, 2, share, wide), vm(n_in, 2, share, wide),
            vm(4, share, wide), vm(3, share, wide),
            vm(2, tok, wide), vm(2, tok, width), vm(2, tok, width), vm(tok, width), vm(tok, width),
            vm(2, gq_rows, wide), vm(n_dp, 2, gq_rows // n_dp, wide), vm(2, gq_rows // n_dp, wide),
            vm(2, gq_rows // n_dp, wide), vm(gq_rows // n_dp, wide),
            DMA((n_out, 4)), DMA((n_out, 4)), DMA((n_in, 4)), DMA((n_in, 4)),
            DMA((3, 4)), DMA((3, 4)), DMA((4, 2, n_dp)), DMA((4, 2, n_dp)), DMA((4, n_out, n_in)), DMA((4, n_out, n_in)),
            DMA((n_dp // 2, 2)), DMA((n_dp,)),
            DMA((2,)), DMA((2,)), DMA, DMA,
            DMA((n_dp,)), DMA((n_dp,)), DMA((2,)), DMA((2,)), DMA((n_dp,)), DMA((n_dp,)), DMA((4,)),
        ],
        compiler_params=pltpu.CompilerParams(
            collective_id=4, has_side_effects=True, vmem_limit_bytes=VMEM_LIMIT
        ),
        name="return",
    )(dqkv, wq, xf, dh1, *a_parts, *b_parts, *z_parts)


def finish_kernel(a_any, b_any, deal_ref, g_any, q_any, *refs):
    outs, bufs = refs[:8], refs[8:16]
    qb_ref, vb_ref, ob_ref, g1_ref, s1_ref, ub_ref, db_ref, g2_ref, s2_ref = refs[16:25]
    a_ref, b_ref, g_ref, q_ref, isem, osem = refs[25:]
    loads = [
        pltpu.make_async_copy(src, dst, isem.at[i])
        for i, (src, dst) in enumerate(((a_any, a_ref), (g_any, g_ref), (b_any, b_ref), (q_any, q_ref)))
    ]
    for cp in loads:
        cp.start()
    stores = []

    def store(i):
        cp = pltpu.make_async_copy(bufs[i], outs[i], osem.at[i])
        cp.start()
        stores.append(cp)

    out, ig, up, dn, ow, qw, kw, vw = bufs
    tokens, wide = a_ref.shape
    third = qw.shape[0]
    place = (lax.broadcasted_iota(jnp.int32, (tokens, tokens), 0) == deal_ref[...]).astype(bf16)
    loads[0].wait()
    out[...] = nn(place, a_ref[...]).astype(bf16)
    store(0)
    loads[1].wait()
    up[:, :wide] = g_ref[:wide, :].astype(f32)
    up[:, wide:] = g_ref[wide : 2 * wide, :].astype(f32)
    store(2)
    dn[...] = g_ref[DOWN:OUT, :].astype(f32)
    store(3)
    ow[...] = g_ref[OUT:VEC, :].astype(f32)
    store(4)
    loads[2].wait()
    ig[...] = nn(place, b_ref[...]).astype(bf16)
    store(1)
    loads[3].wait()
    for i, ref in enumerate((qw, kw, vw)):
        ref[...] = q_ref[i * third : (i + 1) * third, :].astype(f32)
        store(5 + i)
    bias = q_ref[3 * third : 3 * third + 16, :].astype(f32)[0:1]
    qb_ref[...] = bias[0, :third]
    vb_ref[...] = bias[0, third:]
    vec = g_ref[VEC : VEC + 16, :].astype(f32)
    for i, ref in enumerate((ob_ref, g1_ref, s1_ref, db_ref, g2_ref, s2_ref)):
        ref[...] = vec[i]
    ub_ref[0:wide] = vec[6]
    ub_ref[wide : 2 * wide] = vec[7]
    for cp in stores:
        cp.wait()


def finish_call(back_a, back_b, deal, gall, gq, third):
    tokens, wide = back_a.shape
    one = sds((wide,), f32)
    row = sds((third,), f32)
    head = sds((third, wide), f32)
    tok = sds((tokens, wide), bf16)
    big = (tok, tok, sds((wide, 2 * wide), f32), sds((2 * wide, wide), f32), head, head, head, head)
    small = (row, row, one, one, one, sds((2 * wide,), f32), one, one, one)

    def kernel(*refs):
        ins, outs, scratch = refs[:5], refs[5:22], refs[22:]
        finish_kernel(*ins, *outs[:8], *scratch[:8], *outs[8:], *scratch[8:])

    outs = pl.pallas_call(
        kernel,
        out_shape=big + small,
        in_specs=[ANY, ANY, VM, ANY, ANY],
        out_specs=(ANY,) * 8 + (VM,) * 9,
        scratch_shapes=[pltpu.VMEM(x.shape, x.dtype) for x in big]
        + [pltpu.VMEM(x.shape, bf16) for x in (back_a, back_b, gall, gq)]
        + [DMA((4,)), DMA((8,))],
        compiler_params=pltpu.CompilerParams(vmem_limit_bytes=VMEM_LIMIT),
        name="finish",
    )(back_a, back_b, deal, gall, gq)
    out, ig, up, dn, ow, qw, kw, vw, qb, vb, ob, g1, s1, ub, db, g2, s2 = outs
    return [out, ig, qw, qb, kw, vw, vb, ow, ob, g1, s1, up, ub, dn, db, g2, s2]


def round_up(v, m):
    return (v + m - 1) // m * m


def on_device(
    n_dp, inputs, out_grad, deal, seq_lengths, key_trim, query_weight, query_bias, key_weight,
    value_weight, value_bias, out_weight, out_bias, first_gain, first_shift, up_weight, up_bias,
    down_weight, down_bias, second_gain, second_shift,
):
    wide = inputs.shape[1]
    n_seq = seq_lengths.shape[1]
    step = 16 * n_dp
    third = query_weight.shape[1]
    rows_w = round_up(VEC + 16, step)
    xf, dys, qkv, qkvt, wq, seq, wg = deal_call(
        n_dp, rows_w,
        (
            inputs, out_grad, deal, query_weight.T, key_weight.T, value_weight.T, query_bias, value_bias, up_weight,
            down_weight, out_weight, out_bias, first_gain, first_shift, down_bias, second_gain, second_shift, up_bias,
            seq_lengths, key_trim,
        ),
    )
    ot, lse = attend_call(n_seq, seq, qkv, qkvt)
    back_a, dh1, dot, *grads = middle_call(n_dp, ot, xf, dys, wg, rows_w)
    n_in, n_out = levels(n_dp)
    a_parts, b_parts, z_parts = grads[:n_in], grads[n_in : n_in + n_out], grads[n_in + n_out :]
    for k in range(1, n_in):
        a_parts[k] = lax.ppermute(
            a_parts[k], "dp", [(o * n_in + i, o * n_in + (i + k) % n_in) for o in range(n_out) for i in range(n_in)]
        )
    for k in range(1, n_out):
        b_parts[k] = lax.ppermute(
            b_parts[k], "dp", [(o * n_in + i, (o + k) % n_out * n_in + i) for o in range(n_out) for i in range(n_in)]
        )
    for k in range(1, 4):
        z_parts[k] = lax.ppermute(z_parts[k], "row", [(i, (i + k) % 4) for i in range(4)])
    dqkv = attend_back_call(n_seq, seq, qkv, qkvt, dot, ot, lse)
    gq_rows = round_up(3 * third + 16, step)
    back_b, gq, gall = return_call(n_dp, dqkv, wq, xf, dh1, a_parts, b_parts, z_parts, gq_rows)
    outs = list(finish_call(back_a, back_b, deal, gall, gq, third))
    for i in (2, 4, 5):
        outs[i] = outs[i].T
    return tuple(outs)


def solution(mesh):
    n_dp = mesh.shape["dp"]
    tok = P(("dp", "row"), "col")
    one = P("col")
    row = P("row")
    a = P("col", "row")
    b = P("row", "col")
    seqs = P(("dp", "col"), None)
    in_specs = (
        tok, tok, P(("dp", "row"), None), seqs, seqs, a, row, a, a, row, b, one, one, one, a, row, b, one, one, one,
    )
    out_specs = (tok, tok, a, row, a, a, row, b, one, one, one, a, row, b, one, one, one)
    return jax.shard_map(
        functools.partial(on_device, n_dp), mesh=mesh, in_specs=in_specs, out_specs=out_specs, check_vma=False
    )
```

```python
import functools

import jax
import jax.numpy as jnp
from jax import lax
from jax.experimental import pallas as pl
from jax.experimental.pallas import tpu as pltpu
from jax.sharding import PartitionSpec as P

MESH = pl.DeviceIdType.MESH
f32 = jnp.float32
bf16 = jnp.bfloat16

HEAD = 64
EPS = 1e-05
FAR = -1e30
INV_ROOT_TWO = 0.7071067811865476
INV_ROOT_TAU = 0.3989422804014327
VMEM_LIMIT = 62 * 1024 * 1024
DOWN, OUT, VEC = 768, 1536, 1728

VM = pl.BlockSpec(memory_space=pltpu.VMEM)
SM = pl.BlockSpec(memory_space=pltpu.SMEM)
ANY = pl.BlockSpec(memory_space=pl.ANY)
DMA = pltpu.SemaphoreType.DMA


def nn(a, b):
    return lax.dot_general(a, b, (((1,), (0,)), ((), ())), preferred_element_type=f32)


def nt(a, b):
    return lax.dot_general(a, b, (((1,), (1,)), ((), ())), preferred_element_type=f32)


def tn(a, b):
    return lax.dot_general(a, b, (((0,), (0,)), ((), ())), preferred_element_type=f32)


def sds(shape, dtype):
    return jax.ShapeDtypeStruct(shape, dtype)


def me():
    return lax.axis_index("dp"), lax.axis_index("row"), lax.axis_index("col")


def flip(v):
    return v + 1 - 2 * lax.rem(v, 2)


def remote(src, dst, ssem, rsem, dev):
    return pltpu.make_async_remote_copy(
        src_ref=src, dst_ref=dst, send_sem=ssem, recv_sem=rsem, device_id=dev, device_id_type=MESH
    )


def greet(devs):
    barrier = pltpu.get_barrier_semaphore()
    for dev in devs:
        pl.semaphore_signal(barrier, inc=1, device_id=dev, device_id_type=MESH)
    pl.semaphore_wait(barrier, len(devs))


def send_back(n_dp, src, back, ss, rs):
    d, r, c = me()
    n_half = n_dp // 2
    piece = back.shape[0] // n_dp
    here = pl.ds(pl.multiple_of(d * piece, piece), piece)
    for i in range(n_half):
        s = c * n_half + i
        for cc in range(2):
            ref = src.at[cc, i * piece : (i + 1) * piece, :]
            cp = remote(ref, back.at[here, :], ss.at[i, cc], rs.at[d], (s, r, cc))
            local = (s == d) & (c == cc)

            @pl.when(jnp.logical_not(local))
            def _():
                cp.start()

            @pl.when(local)
            def _():
                back[here, :] = src[cc, i * piece : (i + 1) * piece, :]


def sent_back(n_dp, src, back, ss, rs):
    d, r, c = me()
    n_half = n_dp // 2
    piece = back.shape[0] // n_dp
    for i in range(n_half):
        s = c * n_half + i
        for cc in range(2):
            ref = src.at[cc, i * piece : (i + 1) * piece, :]

            @pl.when(jnp.logical_not((s == d) & (c == cc)))
            def _():
                remote(ref, back.at[0:piece, :], ss.at[i, cc], rs.at[0], (s, r, cc)).wait_send()


def got_back(n_dp, src, back, ss, rs):
    d, r, c = me()
    holder = lax.div(d, n_dp // 2)
    piece = back.shape[0] // n_dp
    for g in range(n_dp):

        @pl.when(jnp.logical_not((d == g) & (holder == c)))
        def _():
            remote(
                src.at[0, 0:piece, :], back.at[g * piece : (g + 1) * piece, :], ss.at[0, 0], rs.at[g], (d, r, 1 - c)
            ).wait_recv()


def levels(n_dp):
    n_in = 2 if n_dp < 16 else 4
    return n_in, n_dp // n_in


class Fan:
    def __init__(self, n_dp, piece, sems, outer_first):
        self.n_in, self.n_out = levels(n_dp)
        d, self.r, self.c = me()
        self.o, self.i = lax.div(d, self.n_in), lax.rem(d, self.n_in)
        self.piece, self.outer_first = piece, outer_first
        self.sems = sems

    def out(self, m):
        return lax.rem(self.o + m + self.n_out, self.n_out)

    def inn(self, m):
        return lax.rem(self.i + m + self.n_in, self.n_in)

    def at(self, o, i):
        return self.piece(o * self.n_in + i)

    def own(self, which, m):
        ref = self.at(self.o, self.i)
        ss, rs = self.sems[which]
        dev = (self.out(m), self.i) if which == 0 else (self.o, self.inn(m))
        return remote(ref, ref, ss.at[m], rs.at[m], (dev[0] * self.n_in + dev[1], self.r, self.c))

    def passed(self, mo, mi, outer_first):
        ss, rs = self.sems[2]
        if outer_first:
            ref, dev = self.at(self.out(-mo), self.i), (self.o, self.inn(mi))
        else:
            ref, dev = self.at(self.o, self.inn(-mi)), (self.out(mo), self.i)
        return remote(ref, ref, ss.at[mo, mi], rs.at[mo, mi], (dev[0] * self.n_in + dev[1], self.r, self.c))

    def counts(self):
        return range(1, self.n_out), range(1, self.n_in)

    def send(self):
        outs, ins = self.counts()
        for m in outs:
            self.own(0, m).start()
        for m in ins:
            self.own(1, m).start()

    def pass_on(self):
        outs, ins = self.counts()

        def way(outer_first):
            for m in outs if outer_first else ins:
                self.own(0 if outer_first else 1, m).wait_recv()
                for n in ins if outer_first else outs:
                    self.passed(m if outer_first else n, n if outer_first else m, outer_first).start()
            for m in ins if outer_first else outs:
                self.own(1 if outer_first else 0, m).wait_recv()

        if isinstance(self.outer_first, bool):
            way(self.outer_first)
        else:

            @pl.when(self.outer_first)
            def _():
                way(True)

            @pl.when(jnp.logical_not(self.outer_first))
            def _():
                way(False)

    def finish(self):
        outs, ins = self.counts()
        for m in outs:
            self.own(0, m).wait_send()
        for m in ins:
            self.own(1, m).wait_send()
        for mo in outs:
            for mi in ins:
                self.passed(mo, mi, True).wait()


def deal_kernel(
    n_dp, rows_w, x_ref, dy_ref, deal_ref, qw_ref, kw_ref, vw_ref, qb_ref, vb_ref, up_ref, dn_ref, ow_ref,
    ob_ref, g1_ref, s1_ref, db_ref, g2_ref, s2_ref, ub_ref, len_ref, trim_ref,
    xf_out, dys_out, qkv_out, qkvt_out, wq_out, seqo_ref, wg_ref,
    xf_ref, dys_ref, qkv_ref, qkvt_ref, wq_ref, so, sq,
    xs, seq, seqrx, w, bias, biases, blob, col,
    sx, rx, sc, rc, sz, rz, sc2, rc2, sw, rw, sb, rb, sm, rm, ss, rs, sf, rf, sp, rp, sl,
):
    d, r, c = me()
    half = lax.rem(r, 2)
    tokens, wide = x_ref.shape
    piece = tokens // n_dp
    third = qw_ref.shape[0]
    core = (d, r, 1 - c)
    zdev = (d, flip(r), c)
    far_row = lax.rem(r + 2, 4)
    ring = [(lax.rem(d + k, n_dp), r, c) for k in range(1, n_dp)]
    rows_dev = [(d, lax.rem(r + k, 4), c) for k in (1, 2, 3)]
    greet(ring + rows_dev + [core, (d, far_row, 1 - c)])

    blob[0:wide, :] = up_ref[:, :wide]
    blob[wide : 2 * wide, :] = up_ref[:, wide:]
    blob[DOWN:OUT, :] = dn_ref[...]
    blob[OUT:VEC, :] = ow_ref[...]
    vecs = [v[...].reshape(1, wide) for v in (ob_ref, g1_ref, s1_ref, db_ref, g2_ref, s2_ref)]
    vecs += [ub_ref[0:wide].reshape(1, wide), ub_ref[wide : 2 * wide].reshape(1, wide)]
    row = lax.broadcasted_iota(jnp.int32, (16, wide), 0)
    tail = jnp.zeros((16, wide), f32)
    for i, v in enumerate(vecs):
        tail = jnp.where(row == i, v.astype(f32), tail)
    blob[VEC : VEC + 16, :] = tail.astype(bf16)
    blob[VEC + 16 :, :] = jnp.zeros((rows_w - VEC - 16, wide), bf16)
    share = rows_w // n_dp
    my_share = pl.ds(pl.multiple_of(d * share, share), share)
    share_cp = [
        remote(blob.at[my_share, :], wg_ref.at[r, my_share, :], ss.at[k], rs.at[k], dev)
        for k, dev in enumerate(rows_dev)
    ]
    for cp in share_cp:
        cp.start()
    local_w = pltpu.make_async_copy(blob, wg_ref.at[r], sl)
    local_w.start()

    def rows(s):
        return pl.ds(pl.multiple_of(s * piece, piece), piece)

    col[...] = jnp.broadcast_to(deal_ref[...], (8, tokens)).T
    lane = lax.broadcasted_iota(jnp.int32, (piece, tokens), 1)
    sends = []
    for k in list(range(1, n_dp)) + [0]:
        dest = lax.rem(d + k, n_dp)
        pick = (col[rows(dest), 0:1] == lane).astype(bf16)
        px = nn(pick, x_ref[...]).astype(bf16)
        if k:
            xs[k] = px
            cp = remote(xs.at[k], xf_ref.at[half, c, rows(d), :], sx.at[k], rx.at[k], (dest, r, c))
            cp.start()
            sends.append(cp)
        else:
            xf_ref[half, c, rows(d), :] = px

    w[:third, :] = qw_ref[...]
    w[third : 2 * third, :] = kw_ref[...]
    w[2 * third :, :] = vw_ref[...]
    w_far = remote(w, wq_ref.at[c], sw.at[0], rw.at[c], (d, far_row, 1))
    w_far.start()
    w_near = remote(w, wq_ref.at[1], sw.at[1], rw.at[1], (d, r, 0))
    flat = jnp.concatenate(
        [qb_ref[...].reshape(1, third), jnp.zeros((1, third), bf16), vb_ref[...].reshape(1, third)], axis=1
    )
    bias[...] = jnp.broadcast_to(flat.astype(f32), (8, 3 * third))
    b_far = remote(bias, biases.at[1], sb.at[0], rb.at[0], (d, far_row, 1))

    @pl.when(c == 0)
    def _():
        wq_ref[0] = w[...]
        b_far.start()

    @pl.when(c == 1)
    def _():
        w_near.start()

    biases[0] = bias[...]
    seq[...] = jnp.zeros_like(seq)
    seq[0:1, 0 : len_ref.shape[1]] = len_ref[...]
    seq[1:2, 0 : len_ref.shape[1]] = trim_ref[...]
    seq_cp = remote(seq, seqrx, sm.at[0], rm.at[0], core)
    seq_cp.start()

    core_cp, z_cp, core2_cp = [], [], []
    for k in range(n_dp):
        s = lax.rem(d - k + n_dp, n_dp)
        ref = xf_ref.at[half, c, rows(s), :]
        if k:
            sends[k - 1].wait_recv()
        a = remote(ref, ref, sz.at[k], rz.at[k], zdev)
        a.start()
        b = remote(ref, ref, sc.at[k], rc.at[k], core)
        b.start()
        z_cp.append(a)
        core_cp.append(b)

    fans = []
    for k in range(3):
        share_cp[k].wait_recv()
        j = lax.rem(r - k + 3, 4)
        fan = Fan(
            n_dp,
            lambda s, j=j: wg_ref.at[j, pl.ds(pl.multiple_of(s * share, share), share), :],
            [(sf.at[k, 0], rf.at[k, 0]), (sf.at[k, 1], rf.at[k, 1]), (sp.at[k], rp.at[k])],
            j < 2,
        )
        fan.send()
        fans.append(fan)
        if k == 0:

            def pick_dy(dest, carry):
                pick = (col[rows(dest), 0:1] == lane).astype(bf16)
                dys_ref[dest] = nn(pick, dy_ref[...]).astype(bf16)
                return carry

            lax.fori_loop(0, n_dp, pick_dy, 0)
        else:
            fans[k - 1].pass_on()

    @pl.when(c == 0)
    def _():
        w_near.wait_recv()
        b_far.wait_send()

    @pl.when(c == 1)
    def _():
        w_near.wait_send()
        b_far.wait_recv()
        remote(w, wq_ref.at[0], sw.at[0], rw.at[0], (d, far_row, 1)).wait_recv()
        remote(w, wq_ref.at[1], sw.at[0], rw.at[1], (d, far_row, 1)).wait_recv()

    for k in range(n_dp):
        core_cp[k].wait_recv()
    stores = [
        pltpu.make_async_copy(xf_ref.at[half], xf_out.at[half], so.at[0]),
        pltpu.make_async_copy(wq_ref, wq_out, so.at[1]),
        pltpu.make_async_copy(dys_ref, dys_out, so.at[2]),
    ]
    for cp in stores:
        cp.start()
    brow = jnp.where(c == 0, biases[0], biases[1])[0:1, :]

    def saves(h, i):
        out = pl.ds(pl.multiple_of(h * tokens + i * 512, 512), 512)
        return (
            pltpu.make_async_copy(qkv_ref.at[out, :], qkv_out.at[out, :], sq.at[h, i]),
            pltpu.make_async_copy(qkvt_ref.at[:, out], qkvt_out.at[:, out], sq.at[h, 2 + i]),
        )

    def project(h):
        def one(i, carry):
            base = pl.ds(pl.multiple_of(i * 512, 512), 512)
            y = nt(xf_ref[h, 0, base, :], wq_ref[0]) + nt(xf_ref[h, 1, base, :], wq_ref[1]) + brow
            y = y.astype(bf16)
            out = pl.ds(pl.multiple_of(h * tokens + i * 512, 512), 512)
            qkv_ref[out, :] = y
            qkvt_ref[:, out] = y.T
            for cp in saves(h, i):
                cp.start()
            return carry

        lax.fori_loop(0, tokens // 512, one, 0)

    project(half)
    fans[2].pass_on()

    for k in range(n_dp):
        s = lax.rem(d - k + n_dp, n_dp)
        z_cp[k].wait_recv()
        ref = xf_ref.at[1 - half, c, rows(s), :]
        b = remote(ref, ref, sc2.at[k], rc2.at[k], core)
        b.start()
        core2_cp.append(b)

    w_far.wait_send()
    for k in range(n_dp):
        core2_cp[k].wait_recv()
    stores.append(pltpu.make_async_copy(xf_ref.at[1 - half], xf_out.at[1 - half], so.at[5]))
    stores[-1].start()
    project(1 - half)
    seq_cp.wait()
    is_mine = lax.div(r, 2) == c
    seqo_ref[...] = jnp.where(is_mine, seq[...], seqrx[...])
    for fan in fans:
        fan.finish()
    for cp in sends + core_cp + z_cp + core2_cp + share_cp:
        cp.wait_send()
    for cp in stores:
        cp.wait()
    for h in range(2):
        for i in range(tokens // 512):
            for cp in saves(h, i):
                cp.wait()
    local_w.wait()


def deal_call(n_dp, rows_w, args):
    x, qw = args[0], args[3]
    tokens, wide = x.shape
    piece = tokens // n_dp
    cols = 3 * qw.shape[0]
    return pl.pallas_call(
        functools.partial(deal_kernel, n_dp, rows_w),
        out_shape=(
            sds((2, 2, tokens, wide), bf16),
            sds((n_dp, piece, wide), bf16),
            sds((2 * tokens, cols), bf16),
            sds((cols, 2 * tokens), bf16),
            sds((2, cols, wide), bf16),
            sds((8, 128), jnp.int32),
            sds((4, rows_w, wide), bf16),
        ),
        in_specs=[VM] * len(args),
        out_specs=(ANY,) * 5 + (VM, ANY),
        scratch_shapes=[
            pltpu.VMEM((2, 2, tokens, wide), bf16),
            pltpu.VMEM((n_dp, piece, wide), bf16),
            pltpu.VMEM((2 * tokens, cols), bf16),
            pltpu.VMEM((cols, 2 * tokens), bf16),
            pltpu.VMEM((2, cols, wide), bf16),
            DMA((6,)),
            DMA((2, 4)),
            pltpu.VMEM((n_dp, piece, wide), bf16),
            pltpu.VMEM((8, 128), jnp.int32),
            pltpu.VMEM((8, 128), jnp.int32),
            pltpu.VMEM((cols, wide), bf16),
            pltpu.VMEM((8, cols), f32),
            pltpu.VMEM((2, 8, cols), f32),
            pltpu.VMEM((rows_w, wide), bf16),
            pltpu.VMEM((tokens, 8), jnp.int32),
        ]
        + [DMA((n_dp,))] * 8
        + [DMA((2,))] * 6
        + [DMA((3,))] * 2
        + [DMA((3, 2, n_dp))] * 2
        + [DMA((3,) + levels(n_dp)[::-1])] * 2
        + [DMA],
        compiler_params=pltpu.CompilerParams(
            collective_id=1, has_side_effects=True, vmem_limit_bytes=VMEM_LIMIT
        ),
        name="deal",
    )(*args)


def seq_bounds(seq_ref, n_seq):
    ends, total = [], 0
    for j in range(n_seq):
        total = total + seq_ref[0, j]
        ends.append(total)
    starts = [ends[j] - seq_ref[0, j] for j in range(n_seq)]
    lives = [starts[j] + jnp.maximum(seq_ref[0, j] - seq_ref[1, j], 1) for j in range(n_seq)]
    return starts, ends, lives


def block_range(first, last, starts, ends, block):
    lo, hi = 0, ends[-1]
    for j in range(len(ends)):
        lo = jnp.where((first >= starts[j]) & (first < ends[j]), starts[j], lo)
        hi = jnp.where((last >= starts[j]) & (last < ends[j]), ends[j], hi)
    return lax.div(lo, block), lax.div(hi + block - 1, block)


def key_columns(starts, ends, lives, length, extra):
    pos = lax.broadcasted_iota(jnp.int32, (16, length), 1)
    row = lax.broadcasted_iota(jnp.int32, (16, length), 0)
    n_seq = len(ends)
    rows = jnp.where(row < n_seq, FAR, 0.0)
    rows = jnp.where((row >= n_seq) & (row < n_seq + extra), -1.0, rows)
    for j in range(n_seq):
        rows = jnp.where((row == j) & (pos >= starts[j]) & (pos < lives[j]), 0.0, rows)
    return jnp.concatenate([rows.T.astype(bf16), jnp.zeros((length, HEAD - 16), bf16)], axis=1)


def query_rows(starts, ends, length):
    pos = lax.broadcasted_iota(jnp.int32, (16, length), 1)
    row = lax.broadcasted_iota(jnp.int32, (16, length), 0)
    out = jnp.zeros((16, length), f32)
    for j in range(len(ends)):
        out = jnp.where((row == j) & (pos >= starts[j]) & (pos < ends[j]), 1.0, out)
    return out


def split_three(v):
    hi = v.astype(bf16).astype(f32)
    mid = (v - hi).astype(bf16).astype(f32)
    low = (v - hi - mid).astype(bf16).astype(f32)
    return hi, mid, low


def put_rows(base, values, first):
    row = lax.broadcasted_iota(jnp.int32, base.shape, 0)
    for i, v in enumerate(values):
        base = jnp.where(row == first + i, v, base)
    return base


def attend_kernel(n_seq, block, seq_ref, qkv_ref, qkvt_ref, ot_ref, lse_ref, kaug, qaug, vaug, acc, mx, sbuf):
    length = qkv_ref.shape[0]
    heads = qkv_ref.shape[1] // (3 * HEAD)
    width = heads * HEAD
    span = 2 * block
    starts, ends, lives = seq_bounds(seq_ref, n_seq)
    kcols = key_columns(starts, ends, lives, length, 0)
    qrows = query_rows(starts, ends, length)
    ones = (lax.broadcasted_iota(jnp.int32, (16, length), 0) == 0).astype(f32).astype(bf16)
    for h in range(heads):
        kaug[h, :, :HEAD] = qkv_ref[:, width + h * HEAD : width + (h + 1) * HEAD]
        kaug[h, :, HEAD:] = kcols
        qaug[h, :HEAD, :] = qkvt_ref[h * HEAD : (h + 1) * HEAD, :] * 0.125
        qaug[h, HEAD : HEAD + 16, :] = qrows.astype(bf16)
        qaug[h, HEAD + 16 :, :] = jnp.zeros((HEAD - 16, length), bf16)
        vaug[h, :HEAD, :] = qkvt_ref[2 * width + h * HEAD : 2 * width + (h + 1) * HEAD, :]
        vaug[h, HEAD:, :] = ones
    lse_ref[...] = jnp.zeros_like(lse_ref)

    def q_step(qb, carry):
        qs = pl.ds(pl.multiple_of(qb * block, block), block)
        lo, hi = block_range(qb * block, qb * block + block - 1, starts, ends, block)
        for h in range(heads):
            acc[h] = jnp.zeros((HEAD + 16, block), f32)
            mx[h] = jnp.full((8, block), 2 * FAR, f32)

        def max_step(size, i, inner):
            ks = pl.ds(pl.multiple_of((lo + 2 * i) * block, block), size)
            at = pl.ds(pl.multiple_of(i * span, span), size)
            ss = [nn(kaug[h, ks, :], qaug[h, :, qs]) for h in range(heads)]
            for h in range(heads):
                sbuf[h, at, :] = ss[h]
                mx[h] = jnp.maximum(mx[h], jnp.max(ss[h].reshape(size // 8, 8, block), axis=0))
            return inner

        pairs, odd = lax.div(hi - lo, 2), lax.rem(hi - lo, 2)
        lax.fori_loop(0, pairs, functools.partial(max_step, span), 0)
        lax.fori_loop(pairs, pairs + odd, functools.partial(max_step, block), 0)
        tops = []
        for h in range(heads):
            top = jnp.max(mx[h], axis=0, keepdims=True)
            tops.append(top)

        def sum_step(size, i, inner):
            ks = pl.ds(pl.multiple_of((lo + 2 * i) * block, block), size)
            at = pl.ds(pl.multiple_of(i * span, span), size)
            ps = [jnp.exp(sbuf[h, at, :] - tops[h]).astype(bf16) for h in range(heads)]
            for h in range(heads):
                acc[h] = acc[h] + nn(vaug[h, :, ks], ps[h])
            return inner

        lax.fori_loop(0, pairs, functools.partial(sum_step, span), 0)
        lax.fori_loop(pairs, pairs + odd, functools.partial(sum_step, block), 0)
        for h in range(heads):
            total = acc[h, HEAD : HEAD + 1, :]
            ot_ref[h * HEAD : (h + 1) * HEAD, qs] = (acc[h, :HEAD, :] / total).astype(bf16)
            lse_ref[h : h + 1, qs] = tops[h] + jnp.log(total)
        return carry

    lax.fori_loop(0, length // block, q_step, 0)


def attend_call(n_seq, seq, qkv, qkvt):
    length, cols = qkv.shape
    heads = cols // (3 * HEAD)
    block = 256
    return pl.pallas_call(
        functools.partial(attend_kernel, n_seq, block),
        out_shape=(sds((heads * HEAD, length), bf16), sds((8, length), f32)),
        in_specs=[SM, VM, VM],
        out_specs=(VM, VM),
        scratch_shapes=[
            pltpu.VMEM((heads, length, 2 * HEAD), bf16),
            pltpu.VMEM((heads, 2 * HEAD, length), bf16),
            pltpu.VMEM((heads, HEAD + 16, length), bf16),
            pltpu.VMEM((heads, HEAD + 16, block), f32),
            pltpu.VMEM((heads, 8, block), f32),
            pltpu.VMEM((heads, length, block), f32),
        ],
        compiler_params=pltpu.CompilerParams(vmem_limit_bytes=VMEM_LIMIT),
        cost_estimate=pl.CostEstimate(flops=4 * 10**9, bytes_accessed=6 * 10**6, transcendentals=10**7),
        name="attend",
    )(seq, qkv, qkvt)


def attend_back_kernel(
    n_seq, block, seq_ref, qkv_ref, qkvt_ref, dot_ref, ot_ref, lse_ref, dqkv_ref,
    kaug, qaug, vaug, doaug, qn, don, dqt, dk, dv,
):
    length = qkv_ref.shape[0]
    heads = qkv_ref.shape[1] // (3 * HEAD)
    width = heads * HEAD
    starts, ends, lives = seq_bounds(seq_ref, n_seq)
    kcols = key_columns(starts, ends, lives, length, 3)
    lane = lax.broadcasted_iota(jnp.int32, (length, HEAD), 1)
    vcols = jnp.where(lane < 3, -1.0, 0.0).astype(bf16)
    qrows = query_rows(starts, ends, length)
    zero = jnp.zeros((HEAD - 16, length), bf16)
    span = 2 * block
    for h in range(heads):
        hs = slice(h * HEAD, (h + 1) * HEAD)
        kaug[h, :, :HEAD] = qkv_ref[:, width + h * HEAD : width + (h + 1) * HEAD]
        kaug[h, :, HEAD:] = kcols
        vaug[h, :, :HEAD] = qkv_ref[:, 2 * width + h * HEAD : 2 * width + (h + 1) * HEAD]
        vaug[h, :, HEAD:] = vcols
        qaug[h, :HEAD, :] = qkvt_ref[hs, :] * 0.125
        qaug[h, HEAD : HEAD + 16, :] = put_rows(qrows, split_three(lse_ref[h : h + 1, :]), n_seq).astype(bf16)
        qaug[h, HEAD + 16 :, :] = zero
        do = dot_ref[hs, :]
        delta = jnp.sum(do.astype(f32) * ot_ref[hs, :].astype(f32), axis=0, keepdims=True)
        doaug[h, :HEAD, :] = do
        doaug[h, HEAD : HEAD + 16, :] = put_rows(
            jnp.zeros((16, length), f32), split_three(delta), 0
        ).astype(bf16)
        doaug[h, HEAD + 16 :, :] = zero
        qn[h] = qkv_ref[:, hs] * 0.125
        don[h] = do.T
        dqt[h] = jnp.zeros((HEAD, length), f32)

    def k_step(kb, carry):
        ks = pl.ds(pl.multiple_of(kb * block, block), block)
        lo, hi = block_range(kb * block, kb * block + block - 1, starts, ends, block)
        dk[...] = jnp.zeros_like(dk)
        dv[...] = jnp.zeros_like(dv)

        def q_step(size, i, inner):
            qs = pl.ds(pl.multiple_of((lo + 2 * i) * block, block), size)
            for h in range(heads):
                p = jnp.exp(nn(kaug[h, ks, :], qaug[h, :, qs]))
                ds = (p * nn(vaug[h, ks, :], doaug[h, :, qs])).astype(bf16)
                dv[h] = dv[h] + nn(p.astype(bf16), don[h, qs, :])
                dk[h] = dk[h] + nn(ds, qn[h, qs, :])
                kt = qkvt_ref[width + h * HEAD : width + (h + 1) * HEAD, ks]
                dqt[h, :, qs] = dqt[h, :, qs] + nn(kt, ds)
            return inner

        pairs, odd = lax.div(hi - lo, 2), lax.rem(hi - lo, 2)
        lax.fori_loop(0, pairs, functools.partial(q_step, span), 0)
        lax.fori_loop(pairs, pairs + odd, functools.partial(q_step, block), 0)
        for h in range(heads):
            vk = dk[h].astype(bf16)
            vv = dv[h].astype(bf16)
            a, b = width + h * HEAD, 2 * width + h * HEAD
            dqkv_ref[ks, a : a + HEAD] = vk
            dqkv_ref[ks, b : b + HEAD] = vv
        return carry

    lax.fori_loop(0, length // block, k_step, 0)
    for h in range(heads):
        v = (dqt[h] * 0.125).astype(bf16)
        dqkv_ref[:, h * HEAD : (h + 1) * HEAD] = v.T


def attend_back_call(n_seq, seq, qkv, qkvt, dot, ot, lse):
    length, cols = qkv.shape
    heads = cols // (3 * HEAD)
    block = 256
    nat = pltpu.VMEM((heads, length, 2 * HEAD), bf16)
    tra = pltpu.VMEM((heads, 2 * HEAD, length), bf16)
    return pl.pallas_call(
        functools.partial(attend_back_kernel, n_seq, block),
        out_shape=sds((length, cols), bf16),
        in_specs=[SM] + [VM] * 5,
        out_specs=VM,
        scratch_shapes=[
            nat, tra, nat, tra,
            pltpu.VMEM((heads, length, HEAD), bf16),
            pltpu.VMEM((heads, length, HEAD), bf16),
            pltpu.VMEM((heads, HEAD, length), f32),
            pltpu.VMEM((heads, block, HEAD), f32),
            pltpu.VMEM((heads, block, HEAD), f32),
        ],
        compiler_params=pltpu.CompilerParams(vmem_limit_bytes=VMEM_LIMIT),
        cost_estimate=pl.CostEstimate(flops=10**10, bytes_accessed=12 * 10**6, transcendentals=10**7),
        name="attend_back",
    )(seq, qkv, qkvt, dot, ot, lse)


def shard_of(r, c):
    return lax.rem(r + 2 * c, 4)


def middle_kernel(
    n_dp, oin_ref, xf_any, dys_ref, w_ref, back_ref, dh1_ref, dout_ref, *rest
):
    n_in, n_out = levels(n_dp)
    n = n_in + n_out
    parts, rest = (rest[:n_in], rest[n_in:n], rest[n : n + 4]), rest[n + 4 :]
    middle_body(n_dp, oin_ref, xf_any, dys_ref, w_ref, back_ref, dh1_ref, dout_ref, *parts, *rest)


def middle_body(
    n_dp, oin_ref, xf_any, dys_ref, w_ref, back_ref, dh1_ref, dout_ref, a_refs, b_refs, z_refs,
    xv, xsem, fin, s_a, r_a, dyin, dyb, ot_ref, dot_ref, wup, wdn, wo, vec, ub, hid, slope, dub, sums, gbuf, gin, facc, yacc,
    so, ro, sg, rg, lsem, wss, wrs, sgb, rgb, sgt, rgt, gsem, sd, rd, sm, rm, zsem,
):
    d, r, c = me()
    half = lax.rem(r, 2)
    wide = xf_any.shape[3]
    width = 2 * wide
    tok = dyb.shape[0]
    mine = pl.ds(pl.multiple_of(c * tok, tok), tok)
    x_cp = pltpu.make_async_copy(xf_any.at[half, :, mine, :], xv, xsem)
    x_cp.start()
    hrows = oin_ref.shape[0]
    core = (d, r, 1 - c)
    peers = [(d, flip(r), c), (d, flip(r), 1 - c), core]
    ring = [(lax.rem(d + k, n_dp), r, c) for k in range(1, n_dp)]
    greet(peers + ring + [(dev[0], r, 1 - c) for dev in ring])
    base = r - half
    shard = shard_of(r, c)
    o_cp = []
    for i, dev in enumerate(peers):
        q = (dev[1] - base) * 2 + dev[2]
        src = oin_ref.at[:, pl.ds(pl.multiple_of(q * tok, tok), tok)]
        cp = remote(src, ot_ref.at[shard], so.at[i], ro.at[i], dev)
        cp.start()
        o_cp.append(cp)
    myq = pl.ds(pl.multiple_of((half * 2 + c) * tok, tok), tok)
    ot_ref[shard] = oin_ref[:, myq]

    piece = dys_ref.shape[1]
    here = pl.ds(pl.multiple_of(d * piece, piece), piece)
    d_cp = []
    for k, dev in enumerate(ring):
        cp = remote(dys_ref.at[dev[0]], dyin.at[here, :], sd.at[k], rd.at[k], dev)
        cp.start()
        d_cp.append(cp)
    dyin[here, :] = dys_ref[d]

    loads = [[], [], []]
    mycols = pl.ds(pl.multiple_of(c * wide, 128), wide)
    for j in range(4):
        js = slice(j * hrows, (j + 1) * hrows)
        loads[0].append((w_ref.at[j, OUT:VEC], wo.at[js, mycols]))
        loads[0].append((w_ref.at[j, VEC : VEC + 16], ub.at[j, c]))
        for h in range(2):
            hs = slice(h * wide, (h + 1) * wide)
            loads[1].append((w_ref.at[j, hs], wup.at[j, mycols, hs]))
        loads[2].append((w_ref.at[j, DOWN:OUT], wdn.at[j, :, mycols]))
    w_cps = []
    for i, group in enumerate(loads):
        cps = []
        for k, (src, dst) in enumerate(group):
            a = pltpu.make_async_copy(src, dst, lsem.at[i, k])
            a.start()
            b = remote(src, dst, wss.at[i, k], wrs.at[i, k], core)
            b.start()
            cps += [a, b]
        w_cps.append(cps)

    def settle(i):
        for cp in w_cps[i]:
            cp.wait()

    for cp in o_cp:
        cp.wait_recv()
    x_cp.wait()
    x = jnp.concatenate([xv[0], xv[1]], axis=1).astype(f32)
    settle(0)
    vec[...] = jnp.concatenate([ub[0, 0], ub[0, 1]], axis=1)
    ob, g1, s1, db, g2, s2 = [vec[i : i + 1, :].astype(f32) for i in range(6)]
    o = ot_ref[...].reshape(width, tok).T
    h1 = x + (nn(o, wo[...]) + ob)
    mu = jnp.mean(h1, axis=1, keepdims=True)
    r1 = lax.rsqrt(jnp.mean(h1 * h1, axis=1, keepdims=True) - mu * mu + EPS)
    n1 = (h1 - mu) * r1
    y1 = (n1 * g1 + s1).astype(bf16)
    for cp in d_cp:
        cp.wait_recv()
    theirs = pl.ds(pl.multiple_of((1 - c) * tok, tok), tok)
    dy_cp = remote(dyin.at[theirs, :], dyb, sm, rm, core)
    dy_cp.start()
    settle(1)
    settle(2)
    facc[...] = jnp.zeros_like(facc)

    def ahead(j, carry):
        bias = jnp.concatenate([ub[j, 0, 6:7, :], ub[j, 0, 7:8, :]], axis=1).astype(f32)
        u = nn(y1, wup[j]) + bias
        cdf = 0.5 * (1.0 + lax.erf(u * INV_ROOT_TWO))
        hj = (u * cdf).astype(bf16)
        hid[j] = hj
        slope[j] = cdf + u * jnp.exp(-0.5 * u * u) * INV_ROOT_TAU
        facc[...] += nn(hj, wdn[j])
        return carry

    lax.fori_loop(0, 4, ahead, 0)
    h2 = y1.astype(f32) + (facc[...] + db)
    mu2 = jnp.mean(h2, axis=1, keepdims=True)
    r2 = lax.rsqrt(jnp.mean(h2 * h2, axis=1, keepdims=True) - mu2 * mu2 + EPS)
    n2 = (h2 - mu2) * r2
    res = (n2 * g2 + s2).astype(bf16)
    fin[0] = res[:, :wide]
    fin[1] = res[:, wide:]
    send_back(n_dp, fin, back_ref, s_a, r_a)
    dy_cp.wait_recv()
    own, other = dyin[mine, :], dyb[...]
    left = jnp.where(c == 0, own, other)
    right = jnp.where(c == 0, other, own)
    dy = jnp.concatenate([left, right], axis=1).astype(f32)
    e2 = dy * g2
    dh2 = r2 * (e2 - jnp.mean(e2, axis=1, keepdims=True) - n2 * jnp.mean(e2 * n2, axis=1, keepdims=True))
    g2g = jnp.sum(dy * n2, axis=0, keepdims=True)
    s2g = jnp.sum(dy, axis=0, keepdims=True)
    df = dh2.astype(bf16)
    dbg = jnp.sum(df.astype(f32), axis=0, keepdims=True)
    yacc[...] = dh2
    def big_cp(j):
        return remote(gbuf.at[j, 1 - c, 0:OUT], gin.at[j, 0:OUT], sgb.at[j], rgb.at[j], core)

    def back(j, carry):
        du = (nt(df, wdn[j]) * slope[j]).astype(bf16)
        dub[j] = du
        sums[j] = jnp.broadcast_to(jnp.sum(du.astype(f32), axis=0, keepdims=True), (8, width))
        yacc[...] += nt(du, wup[j])
        return carry

    lax.fori_loop(0, 4, back, 0)
    dy1 = yacc[...]
    e1 = dy1 * g1
    dh1 = r1 * (e1 - jnp.mean(e1, axis=1, keepdims=True) - n1 * jnp.mean(e1 * n1, axis=1, keepdims=True))
    dh1_ref[...] = dh1
    g1g = jnp.sum(dy1 * n1, axis=0, keepdims=True)
    s1g = jnp.sum(dy1, axis=0, keepdims=True)
    da = dh1.astype(bf16)
    obg = jnp.sum(da.astype(f32), axis=0, keepdims=True)
    dot_ref[...] = nt(da, wo[...]).T.astype(bf16).reshape(dot_ref.shape)
    g_cp = []
    for i, dev in enumerate(peers):
        cp = remote(dot_ref.at[shard_of(dev[1], dev[2])], dout_ref.at[:, myq], sg.at[i], rg.at[i], dev)
        cp.start()
        g_cp.append(cp)
    dout_ref[:, myq] = dot_ref[shard]
    y1t = y1.T

    def grads(j, carry):
        gd = tn(hid[j], df).astype(bf16)
        gu = nn(y1t, dub[j]).astype(bf16)
        for cc in range(2):
            cs = slice(cc * wide, (cc + 1) * wide)
            for h in range(2):
                gbuf[j, cc, h * wide : (h + 1) * wide, :] = gu[cs, h * wide : (h + 1) * wide]
            gbuf[j, cc, DOWN:OUT, :] = gd[:, cs]
        big_cp(j).start()
        return carry

    lax.fori_loop(0, 4, grads, 0)
    go = nn(ot_ref[...].reshape(width, tok), da).astype(bf16)
    pad = gbuf.shape[2] - VEC
    row = lax.broadcasted_iota(jnp.int32, (pad, wide), 0)
    t_cp = []
    for j in range(4):
        for cc in range(2):
            cs = slice(cc * wide, (cc + 1) * wide)
            gbuf[j, cc, OUT:VEC, :] = go[j * hrows : (j + 1) * hrows, cs]
            tail = jnp.zeros((pad, wide), f32)
            for i, v in enumerate((obg, g1g, s1g, dbg, g2g, s2g)):
                tail = jnp.where(row == i, v[:, cs], tail)
            tail = jnp.where(row == 6, sums[j, 0:1, :wide], tail)
            tail = jnp.where(row == 7, sums[j, 0:1, wide:], tail)
            gbuf[j, cc, VEC:, :] = tail.astype(bf16)
        cp = remote(gbuf.at[j, 1 - c, OUT:], gin.at[j, OUT:], sgt.at[j], rgt.at[j], core)
        cp.start()
        t_cp.append(cp)
    rows_q = a_refs[0].shape[2]
    rows_d = rows_q * n_dp
    n_in, n_out = levels(n_dp)
    outs = []
    for j in range(4):
        big_cp(j).wait()
        t_cp[j].wait()
        gin[j] = (gin[j].astype(f32) + gbuf[j, c].astype(f32)).astype(bf16)
        n_first, n_second, refs = (n_in, n_out, a_refs) if j < 2 else (n_out, n_in, b_refs)
        for k in range(n_first):
            for m in range(n_second):
                if j < 2:
                    s = m * n_in + lax.rem(lax.rem(d, n_in) + k, n_in)
                else:
                    s = lax.rem(lax.div(d, n_in) + k, n_out) * n_in + m
                span = pl.ds(pl.multiple_of(s * rows_q, rows_q), rows_q)
                cp = pltpu.make_async_copy(gin.at[j, span], refs[k].at[m, j % 2], gsem.at[j, k * n_second + m])
                cp.start()
                outs.append(cp)
    for k in range(4):
        cp = pltpu.make_async_copy(gin.at[lax.rem(r + k, 4), rows_d:], z_refs[k], zsem.at[k])
        cp.start()
        outs.append(cp)
    got_back(n_dp, fin, back_ref, s_a, r_a)
    sent_back(n_dp, fin, back_ref, s_a, r_a)
    for cp in o_cp + d_cp + [dy_cp]:
        cp.wait_send()
    for cp in g_cp + outs:
        cp.wait()


def middle_call(n_dp, oin, xf, dys, w, g_rows):
    tok, wide = xf.shape[2] // 2, xf.shape[3]
    width = 2 * wide
    hrows = oin.shape[0]
    n_in, n_out = levels(n_dp)
    rows_q = g_rows * 3 // 4 // n_dp
    return pl.pallas_call(
        functools.partial(middle_kernel, n_dp),
        out_shape=(
            sds((2 * tok, wide), bf16),
            sds((tok, width), f32),
            sds((hrows, 4 * tok), bf16),
        )
        + (sds((n_out, 2, rows_q, wide), bf16),) * n_in
        + (sds((n_in, 2, rows_q, wide), bf16),) * n_out
        + (sds((g_rows - rows_q * n_dp, wide), bf16),) * 4,
        in_specs=[VM, ANY, VM, ANY],
        out_specs=(VM, VM, VM) + (ANY,) * (n_in + n_out + 4),
        scratch_shapes=[
            pltpu.VMEM((2, tok, wide), bf16),
            DMA,
            pltpu.VMEM((2, tok, wide), bf16),
            DMA((n_dp // 2, 2)), DMA((n_dp,)),
            pltpu.VMEM((2 * tok, wide), bf16),
            pltpu.VMEM((tok, wide), bf16),
            pltpu.VMEM((4, hrows, tok), bf16),
            pltpu.VMEM((4, hrows, tok), bf16),
            pltpu.VMEM((4, width, width), bf16),
            pltpu.VMEM((4, width, width), bf16),
            pltpu.VMEM((width, width), bf16),
            pltpu.VMEM((16, width), bf16),
            pltpu.VMEM((4, 2, 16, wide), bf16),
            pltpu.VMEM((4, tok, width), bf16),
            pltpu.VMEM((4, tok, width), f32),
            pltpu.VMEM((4, tok, width), bf16),
            pltpu.VMEM((4, 8, width), f32),
            pltpu.VMEM((4, 2, g_rows, wide), bf16),
            pltpu.VMEM((4, g_rows, wide), bf16),
            pltpu.VMEM((tok, width), f32),
            pltpu.VMEM((tok, width), f32),
            DMA((3,)), DMA((3,)), DMA((3,)), DMA((3,)),
            DMA((3, 8)), DMA((3, 8)), DMA((3, 8)),
            DMA((4,)), DMA((4,)), DMA((4,)), DMA((4,)),
            DMA((4, n_dp)), DMA((n_dp,)), DMA((n_dp,)), DMA, DMA, DMA((4,)),
        ],
        compiler_params=pltpu.CompilerParams(
            collective_id=2, has_side_effects=True, vmem_limit_bytes=VMEM_LIMIT
        ),
        cost_estimate=pl.CostEstimate(flops=16 * 10**9, bytes_accessed=30 * 10**6, transcendentals=4 * 10**6),
        name="middle",
    )(oin, xf, dys, w)


def return_kernel(n_dp, dqkv_any, wq_any, xf_any, dh1_any, *rest):
    n_in, n_out = levels(n_dp)
    n = n_in + n_out
    parts, rest = (rest[:n_in], rest[n_in:n], rest[n : n + 4]), rest[n + 4 :]
    return_body(n_dp, dqkv_any, wq_any, xf_any, dh1_any, *parts, *rest)


def return_body(
    n_dp, dqkv_any, wq_any, xf_any, dh1_any, a_parts, b_parts, z_parts,
    back_ref, gout_ref, gall_ref,
    dqkv_ref, wq, xf, dh1, apart, bpart, zpart, zsum, zrx, s_v, r_v, lsem, psem,
    asum, bsum, ain, bin_, rsum, zin, fin, tocore, fromcore, toz, fromz, gq_ref, gqin, gsum, xq, gfin,
    s_1, r_1, s_2, r_2, s_r, r_r, s_t, r_t, s_p, r_p, s_b, r_b, s_c, r_c, s_z, r_z, s_q, r_q, s_x, r_x, s_g, r_g, zload,
):
    d, r, c = me()
    n_in, n_out = levels(n_dp)
    o, i = lax.div(d, n_in), lax.rem(d, n_in)
    half = lax.rem(r, 2)
    tok, width = dh1_any.shape
    wide = width // 2
    core = (d, r, 1 - c)
    zdev = (d, flip(r), c)
    far_row = lax.rem(r + 2, 4)
    rows_dev = [(d, lax.rem(r + k, 4), c) for k in (1, 2, 3)]
    n_ch = 3
    chunk = rsum.shape[1] // n_ch
    z_loads = [pltpu.make_async_copy(z_parts[k], zpart.at[k], zload.at[k]) for k in range(4)]
    part_loads = []
    for t in range(n_ch):
        ts = slice(t * chunk, (t + 1) * chunk)
        group = [
            pltpu.make_async_copy(a_parts[k].at[:, :, ts], apart.at[k, :, :, ts], psem.at[t, k]) for k in range(n_in)
        ]
        group += [
            pltpu.make_async_copy(b_parts[k].at[:, :, ts], bpart.at[k, :, :, ts], psem.at[t, n_in + k])
            for k in range(n_out)
        ]
        part_loads.append(group)
    loads = [
        pltpu.make_async_copy(src, dst, lsem.at[k])
        for k, (src, dst) in enumerate(((wq_any, wq), (dqkv_any, dqkv_ref), (dh1_any, dh1), (xf_any, xf)))
    ]
    for cp in loads[:2] + part_loads[0] + part_loads[1] + part_loads[2] + z_loads + loads[2:]:
        cp.start()
    peers = [(lax.rem(d + k, n_dp), r, cc) for k in range(1, n_dp) for cc in (0, 1)]
    greet(peers + rows_dev + [core, (d, far_row, 1 - c)])

    def part(h, cc):
        q = h * 2 + cc
        rows = dqkv_ref[pl.ds(pl.multiple_of(q * tok, tok), tok), :]
        return jnp.concatenate([nn(rows, wq[0]), nn(rows, wq[1])], axis=1)

    a_cp, b_cp = [], []

    def second(t):
        ts = slice(t * chunk, (t + 1) * chunk)
        for cp in part_loads[t]:
            cp.wait()
        total = apart[0, :, :, ts].astype(f32)
        for k in range(1, n_in):
            total = total + apart[k, :, :, ts].astype(f32)
        asum[:, :, ts] = total.astype(bf16)
        total = bpart[0, :, :, ts].astype(f32)
        for k in range(1, n_out):
            total = total + bpart[k, :, :, ts].astype(f32)
        bsum[:, :, ts] = total.astype(bf16)
        for k in range(1, n_out):
            dest = lax.rem(o + k, n_out)
            cp = remote(
                asum.at[dest, :, ts], ain.at[k, :, ts], s_1.at[k, t], r_1.at[k, t], (dest * n_in + i, r, c)
            )
            cp.start()
            a_cp.append(cp)
        for k in range(1, n_in):
            dest = lax.rem(i + k, n_in)
            cp = remote(
                bsum.at[dest, :, ts], bin_.at[k, :, ts], s_2.at[k, t], r_2.at[k, t], (o * n_in + dest, r, c)
            )
            cp.start()
            b_cp.append(cp)

    for cp in loads[:2]:
        cp.wait()
    tocore[0] = part(1 - half, 1 - c).astype(bf16)
    cp_far = remote(tocore.at[0], fromcore.at[0], s_c.at[0], r_c.at[0], core)
    cp_far.start()
    second(0)
    far = part(1 - half, c)
    cp_far.wait_recv()
    toz[...] = (far + fromcore[0].astype(f32)).astype(bf16)
    cp_z = remote(toz, fromz, s_z, r_z, zdev)
    cp_z.start()
    second(1)
    second(2)
    for cp in z_loads:
        cp.wait()
    total = zpart[0].astype(f32)
    for k in range(1, 4):
        total = total + zpart[k].astype(f32)
    zsum[...] = total.astype(bf16)
    rows_z = zsum.shape[0] // n_dp

    def zrows(s):
        return pl.ds(pl.multiple_of(s * rows_z, rows_z), rows_z)

    v_cp = []
    for k in range(1, n_dp):
        dest = lax.rem(d + k, n_dp)
        cp = remote(zsum.at[zrows(dest), :], zrx.at[k], s_v.at[k], r_v.at[k], (dest, r, c))
        cp.start()
        v_cp.append(cp)

    row_cp = []

    def to_rows(t):
        ts = slice(t * chunk, (t + 1) * chunk)
        total = asum[o, :, ts].astype(f32)
        for k in range(1, n_out):
            a_cp[t * (n_out - 1) + k - 1].wait_recv()
            total = total + ain[k, :, ts].astype(f32)
        rsum[0:2, ts] = total.astype(bf16)
        total = bsum[i, :, ts].astype(f32)
        for k in range(1, n_in):
            b_cp[t * (n_in - 1) + k - 1].wait_recv()
            total = total + bin_[k, :, ts].astype(f32)
        rsum[2:4, ts] = total.astype(bf16)
        for k, dev in enumerate(rows_dev):
            cp = remote(rsum.at[dev[1], ts], zin.at[k, ts], s_r.at[k, t], r_r.at[k, t], dev)
            cp.start()
            row_cp.append(cp)

    to_rows(0)

    length, n_cols = dqkv_ref.shape
    loads[3].wait()
    for f in range(2):
        g = tn(dqkv_ref[: length // 2, :], xf[0, f]) + tn(dqkv_ref[length // 2 :, :], xf[1, f])
        gq_ref[f, :n_cols, :] = g.astype(bf16)
        to_rows(1 + f)
    third = n_cols // 3
    sums = jnp.sum(dqkv_ref[...].astype(f32), axis=0, keepdims=True)
    bias = jnp.concatenate([sums[:, :third], sums[:, 2 * third :]], axis=1)
    pad = gq_ref.shape[1] - n_cols
    row = lax.broadcasted_iota(jnp.int32, (pad, wide), 0)
    tail = jnp.where(row == 0, bias, 0.0).astype(bf16)
    for f in range(2):
        gq_ref[f, n_cols:, :] = tail
    rq = gq_ref.shape[1] // n_dp

    def quarter(s):
        return pl.ds(pl.multiple_of(s * rq, rq), rq)

    q_cp = []
    for k in range(1, n_dp):
        dest = lax.rem(d + k, n_dp)
        cp = remote(gq_ref.at[:, quarter(dest), :], gqin.at[k], s_q.at[k], r_q.at[k], (dest, r, c))
        cp.start()
        q_cp.append(cp)

    tocore[1] = part(half, 1 - c).astype(bf16)
    cp_near = remote(tocore.at[1], fromcore.at[1], s_c.at[1], r_c.at[1], core)
    cp_near.start()

    total = zsum[zrows(d), :].astype(f32)
    for k in range(1, n_dp):
        v_cp[k - 1].wait_recv()
        total = total + zrx[k].astype(f32)
    rows_d = n_dp * rsum.shape[1]
    gall_ref[pl.ds(pl.multiple_of(rows_d + d * rows_z, rows_z), rows_z), :] = total.astype(bf16)
    vfan = Fan(
        n_dp,
        lambda s: gall_ref.at[pl.ds(pl.multiple_of(rows_d + s * rows_z, rows_z), rows_z), :],
        [(s_t.at[3, 0], r_t.at[3, 0]), (s_t.at[3, 1], r_t.at[3, 1]), (s_p.at[3], r_p.at[3])],
        True,
    )
    vfan.send()

    loads[2].wait()
    total = part(half, c) + dh1[...]
    cp_near.wait_recv()
    total = total + fromcore[1].astype(f32)

    acc = gq_ref[:, quarter(d), :].astype(f32)
    for k in range(1, n_dp):
        q_cp[k - 1].wait_recv()
        acc = acc + gqin[k].astype(f32)
    gsum[...] = acc.astype(bf16)
    to_one = remote(gsum.at[1], xq.at[1], s_x.at[1], r_x.at[1], (d, r, 1))
    far_0 = remote(gsum.at[0], xq.at[0], s_x.at[0], r_x.at[0], (d, far_row, 0))
    far_1 = remote(gsum.at[1], xq.at[0], s_x.at[1], r_x.at[0], (d, far_row, 1))

    @pl.when(c == 0)
    def _():
        to_one.start()

    @pl.when(c == 1)
    def _():
        far_0.start()
        far_1.start()

    cp_z.wait_recv()
    total = (total + fromz[...].astype(f32)).astype(bf16)
    fin[0] = total[:, :wide]
    fin[1] = total[:, wide:]
    send_back(n_dp, fin, back_ref, s_b, r_b)

    vfan.pass_on()
    n_keep = rsum.shape[1]
    t_cp, fans = [], []
    for t in range(n_ch):
        ts = slice(t * chunk, (t + 1) * chunk)
        held = rsum[r, ts].astype(f32)
        for k in range(3):
            row_cp[t * 3 + k].wait_recv()
            held = held + zin[k, ts].astype(f32)
        keep = pl.ds(pl.multiple_of(d * n_keep + t * chunk, chunk), chunk)
        gall_ref[keep, :] = held.astype(bf16)
        fan = Fan(
            n_dp,
            lambda s, t=t: gall_ref.at[pl.ds(pl.multiple_of(s * n_keep + t * chunk, chunk), chunk), :],
            [(s_t.at[t, 0], r_t.at[t, 0]), (s_t.at[t, 1], r_t.at[t, 1]), (s_p.at[t], r_p.at[t])],
            t % 2 == 0,
        )
        fan.send()
        fans.append(fan)
        if t:
            fans[t - 1].pass_on()
    fans[-1].pass_on()

    far_0.wait_recv()

    @pl.when(c == 0)
    def _():
        gfin[...] = (gsum[0].astype(f32) + xq[0].astype(f32)).astype(bf16)

    @pl.when(c == 1)
    def _():
        to_one.wait_recv()
        gfin[...] = (xq[0].astype(f32) + xq[1].astype(f32)).astype(bf16)

    for k in range(1, n_dp):
        dest = lax.rem(d + k, n_dp)
        cp = remote(gfin, gout_ref.at[quarter(d), :], s_g.at[k], r_g.at[k], (dest, r, c))
        cp.start()
        t_cp.append(cp)
    gout_ref[quarter(d), :] = gfin[...]
    got_back(n_dp, fin, back_ref, s_b, r_b)
    sent_back(n_dp, fin, back_ref, s_b, r_b)
    for cp in [cp_far, cp_near, cp_z] + q_cp + a_cp + b_cp + row_cp:
        cp.wait_send()
    for cp in t_cp:
        cp.wait()
    for fan in fans + [vfan]:
        fan.finish()
    for cp in v_cp:
        cp.wait_send()

    @pl.when(c == 0)
    def _():
        to_one.wait_send()

    @pl.when(c == 1)
    def _():
        far_0.wait_send()
        far_1.wait_send()


def return_call(n_dp, dqkv, wq, xf, dh1, a_parts, b_parts, z_parts, gq_rows):
    n_in, n_out = levels(n_dp)
    tok, width = dh1.shape
    wide = width // 2
    share = a_parts[0].shape[2]
    rows_z = z_parts[0].shape[0]
    tokens = 2 * tok

    def vm(*shape):
        return pltpu.VMEM(shape, bf16)

    return pl.pallas_call(
        functools.partial(return_kernel, n_dp),
        out_shape=(sds((tokens, wide), bf16), sds((gq_rows, wide), bf16), sds((n_dp * share + rows_z, wide), bf16)),
        in_specs=[ANY] * (8 + n_in + n_out),
        out_specs=(VM,) * 3,
        scratch_shapes=[
            vm(*dqkv.shape), vm(*wq.shape), vm(*xf.shape), pltpu.VMEM(dh1.shape, f32),
            vm(n_in, n_out, 2, share, wide), vm(n_out, n_in, 2, share, wide),
            vm(4, rows_z, wide), vm(rows_z, wide), vm(n_dp, rows_z // n_dp, wide), DMA((n_dp,)), DMA((n_dp,)),
            DMA((4,)), DMA((4, n_in + n_out)),
            vm(n_out, 2, share, wide), vm(n_in, 2, share, wide), vm(n_out, 2, share, wide), vm(n_in, 2, share, wide),
            vm(4, share, wide), vm(3, share, wide),
            vm(2, tok, wide), vm(2, tok, width), vm(2, tok, width), vm(tok, width), vm(tok, width),
            vm(2, gq_rows, wide), vm(n_dp, 2, gq_rows // n_dp, wide), vm(2, gq_rows // n_dp, wide),
            vm(2, gq_rows // n_dp, wide), vm(gq_rows // n_dp, wide),
            DMA((n_out, 4)), DMA((n_out, 4)), DMA((n_in, 4)), DMA((n_in, 4)),
            DMA((3, 4)), DMA((3, 4)), DMA((4, 2, n_dp)), DMA((4, 2, n_dp)), DMA((4, n_out, n_in)), DMA((4, n_out, n_in)),
            DMA((n_dp // 2, 2)), DMA((n_dp,)),
            DMA((2,)), DMA((2,)), DMA, DMA,
            DMA((n_dp,)), DMA((n_dp,)), DMA((2,)), DMA((2,)), DMA((n_dp,)), DMA((n_dp,)), DMA((4,)),
        ],
        compiler_params=pltpu.CompilerParams(
            collective_id=4, has_side_effects=True, vmem_limit_bytes=VMEM_LIMIT
        ),
        name="return",
    )(dqkv, wq, xf, dh1, *a_parts, *b_parts, *z_parts)


def finish_kernel(a_any, b_any, deal_ref, g_any, q_any, *refs):
    outs, bufs = refs[:8], refs[8:16]
    qb_ref, vb_ref, ob_ref, g1_ref, s1_ref, ub_ref, db_ref, g2_ref, s2_ref = refs[16:25]
    a_ref, b_ref, g_ref, q_ref, isem, osem = refs[25:]
    loads = [
        pltpu.make_async_copy(src, dst, isem.at[i])
        for i, (src, dst) in enumerate(((a_any, a_ref), (g_any, g_ref), (b_any, b_ref), (q_any, q_ref)))
    ]
    for cp in loads:
        cp.start()
    stores = []

    def store(i):
        cp = pltpu.make_async_copy(bufs[i], outs[i], osem.at[i])
        cp.start()
        stores.append(cp)

    out, ig, up, dn, ow, qw, kw, vw = bufs
    tokens, wide = a_ref.shape
    third = qw.shape[0]
    place = (lax.broadcasted_iota(jnp.int32, (tokens, tokens), 0) == deal_ref[...]).astype(bf16)
    loads[0].wait()
    out[...] = nn(place, a_ref[...]).astype(bf16)
    store(0)
    loads[1].wait()
    up[:, :wide] = g_ref[:wide, :].astype(f32)
    up[:, wide:] = g_ref[wide : 2 * wide, :].astype(f32)
    store(2)
    dn[...] = g_ref[DOWN:OUT, :].astype(f32)
    store(3)
    ow[...] = g_ref[OUT:VEC, :].astype(f32)
    store(4)
    loads[2].wait()
    ig[...] = nn(place, b_ref[...]).astype(bf16)
    store(1)
    loads[3].wait()
    for i, ref in enumerate((qw, kw, vw)):
        ref[...] = q_ref[i * third : (i + 1) * third, :].astype(f32)
        store(5 + i)
    bias = q_ref[3 * third : 3 * third + 16, :].astype(f32)[0:1]
    qb_ref[...] = bias[0, :third]
    vb_ref[...] = bias[0, third:]
    vec = g_ref[VEC : VEC + 16, :].astype(f32)
    for i, ref in enumerate((ob_ref, g1_ref, s1_ref, db_ref, g2_ref, s2_ref)):
        ref[...] = vec[i]
    ub_ref[0:wide] = vec[6]
    ub_ref[wide : 2 * wide] = vec[7]
    for cp in stores:
        cp.wait()


def finish_call(back_a, back_b, deal, gall, gq, third):
    tokens, wide = back_a.shape
    one = sds((wide,), f32)
    row = sds((third,), f32)
    head = sds((third, wide), f32)
    tok = sds((tokens, wide), bf16)
    big = (tok, tok, sds((wide, 2 * wide), f32), sds((2 * wide, wide), f32), head, head, head, head)
    small = (row, row, one, one, one, sds((2 * wide,), f32), one, one, one)

    def kernel(*refs):
        ins, outs, scratch = refs[:5], refs[5:22], refs[22:]
        finish_kernel(*ins, *outs[:8], *scratch[:8], *outs[8:], *scratch[8:])

    outs = pl.pallas_call(
        kernel,
        out_shape=big + small,
        in_specs=[ANY, ANY, VM, ANY, ANY],
        out_specs=(ANY,) * 8 + (VM,) * 9,
        scratch_shapes=[pltpu.VMEM(x.shape, x.dtype) for x in big]
        + [pltpu.VMEM(x.shape, bf16) for x in (back_a, back_b, gall, gq)]
        + [DMA((4,)), DMA((8,))],
        compiler_params=pltpu.CompilerParams(vmem_limit_bytes=VMEM_LIMIT),
        name="finish",
    )(back_a, back_b, deal, gall, gq)
    out, ig, up, dn, ow, qw, kw, vw, qb, vb, ob, g1, s1, ub, db, g2, s2 = outs
    return [out, ig, qw, qb, kw, vw, vb, ow, ob, g1, s1, up, ub, dn, db, g2, s2]


def round_up(v, m):
    return (v + m - 1) // m * m


def on_device(
    n_dp, inputs, out_grad, deal, seq_lengths, key_trim, query_weight, query_bias, key_weight,
    value_weight, value_bias, out_weight, out_bias, first_gain, first_shift, up_weight, up_bias,
    down_weight, down_bias, second_gain, second_shift,
):
    wide = inputs.shape[1]
    n_seq = seq_lengths.shape[1]
    step = 16 * n_dp
    third = query_weight.shape[1]
    rows_w = round_up(VEC + 16, step)
    xf, dys, qkv, qkvt, wq, seq, wg = deal_call(
        n_dp, rows_w,
        (
            inputs, out_grad, deal, query_weight.T, key_weight.T, value_weight.T, query_bias, value_bias, up_weight,
            down_weight, out_weight, out_bias, first_gain, first_shift, down_bias, second_gain, second_shift, up_bias,
            seq_lengths, key_trim,
        ),
    )
    ot, lse = attend_call(n_seq, seq, qkv, qkvt)
    back_a, dh1, dot, *grads = middle_call(n_dp, ot, xf, dys, wg, rows_w)
    n_in, n_out = levels(n_dp)
    a_parts, b_parts, z_parts = grads[:n_in], grads[n_in : n_in + n_out], grads[n_in + n_out :]
    for k in range(1, n_in):
        a_parts[k] = lax.ppermute(
            a_parts[k], "dp", [(o * n_in + i, o * n_in + (i + k) % n_in) for o in range(n_out) for i in range(n_in)]
        )
    for k in range(1, n_out):
        b_parts[k] = lax.ppermute(
            b_parts[k], "dp", [(o * n_in + i, (o + k) % n_out * n_in + i) for o in range(n_out) for i in range(n_in)]
        )
    for k in range(1, 4):
        z_parts[k] = lax.ppermute(z_parts[k], "row", [(i, (i + k) % 4) for i in range(4)])
    dqkv = attend_back_call(n_seq, seq, qkv, qkvt, dot, ot, lse)
    gq_rows = round_up(3 * third + 16, step)
    back_b, gq, gall = return_call(n_dp, dqkv, wq, xf, dh1, a_parts, b_parts, z_parts, gq_rows)
    outs = list(finish_call(back_a, back_b, deal, gall, gq, third))
    for i in (2, 4, 5):
        outs[i] = outs[i].T
    return tuple(outs)


def solution(mesh):
    n_dp = mesh.shape["dp"]
    tok = P(("dp", "row"), "col")
    one = P("col")
    row = P("row")
    a = P("col", "row")
    b = P("row", "col")
    seqs = P(("dp", "col"), None)
    in_specs = (
        tok, tok, P(("dp", "row"), None), seqs, seqs, a, row, a, a, row, b, one, one, one, a, row, b, one, one, one,
    )
    out_specs = (tok, tok, a, row, a, a, row, b, one, one, one, a, row, b, one, one, one)
    return jax.shard_map(
        functools.partial(on_device, n_dp), mesh=mesh, in_specs=in_specs, out_specs=out_specs, check_vma=False
    )
```
